256 devices in a mesh: seq: 8 (over y, core), item: 32 (over z, x).
Axes of the slice: x: 4, y: 4, z: 8, core: 2. Of those that a mesh axis runs over, the one named last changes fastest.
Arguments:
- events: float32 [32, 1024, 512], P('item', 'seq'), may hold values from -6 to 6
- w_uvqk: float32 [512, 2048], replicated, may hold values from -0.25 to 0.25
- out_gain: float32 [512], replicated, may hold values from 0.5 to 1.5
- w_out: float32 [512, 512], replicated, may hold values from -0.25 to 0.25
- item_table: float32 [32768, 512], P('item'), may hold values from -0.25 to 0.25
- user_lengths: int32 [32, 4], P('item'), may hold values from 1 to 512, 1024 in all within a row
- neg_ids: int32 [4, 512], replicated, may hold values from 0 to 1023
- panel_owner: int32 [4], replicated, may hold values from 0 to 31
- block_mask: int32 [32, 8], P('item', 'seq'), may hold values from 1 to 65535
- targets: int32 [32, 1024], P('item', 'seq'), may hold values from 0 to 2047
Outputs:
- mean_loss: float32 [], replicated
- event_grad: float32 [32, 1024, 512], P('item', 'seq')
- table_grad: float32 [32768, 512], P('item')
The draws below stay inside these ranges and needn't reach their ends.
Inputs may be any that keep to these rules, and one draw needn't show every extreme that they name: `user_lengths`: the 4 lengths of a group sum to 1024, the longest is exactly 512. `neg_ids`: rows may repeat within and across panels. `panel_owner`: several panels may have one owner. `block_mask`: bit k of an entry admits negative columns 128 k to 128 k + 127 for the 128 events of that block.
All inputs are finite; a program needn't handle non-finite values.
Results may differ from the reference program's by a relative error of at most 0.0003.
Values sent between devices are 32-bit elements; how exact they have to be, the bound alone decides.
A program may use at most 64 MiB of HBM per device.

```python
import math
import jax
import jax.numpy as jnp
import numpy as np
from jax import lax

D = 512
H = 16
USERS = 4
PANELS = 4
PANEL = 512
CAND_DEV = 1024
GROUP = 1024
USER_MOST = 512
GROUPS = 32
TOKENS = 32768
NEG = 2048
ITEMS = 32768
N_ITEM = 32


def with_ends(result, rng, low, high):
    extent = result.shape
    spot = [jax.random.randint(jax.random.fold_in(rng, axis), (), 0, extent[axis]) for axis in range(len(extent))]
    result = result.at[tuple(spot)].set(low)
    longest = extent.index(max(extent))
    spot[longest] = (spot[longest] + 1) % extent[longest]
    return result.at[tuple(spot)].set(high)


def block_scale(stream_key, dims, shards, smallest, high):
    level, own = 1.0, jax.random.fold_in(stream_key, 6)
    for dim, parts in shards:
        heights = jnp.exp(jax.random.uniform(jax.random.fold_in(own, dim), (parts,), jnp.float32, smallest / len(shards), high / len(shards)))
        level = level * jnp.repeat(heights, dims[dim] // parts).reshape([-1 if axis == dim else 1 for axis in range(len(dims))])
    return level


def split_up(number_of, total, bound, lean):
    weights = [(1 << 20) // math.isqrt(standing ** lean) + 1 for standing in range(2, number_of + 1)]
    surplus, given = total - bound - (number_of - 1), [1] * (number_of - 1)
    while surplus > 0:
        movable = [i for i in range(number_of - 1) if given[i] < bound]
        mass, left = sum([weights[i] for i in movable]), surplus
        for i in movable:
            extra = min(bound - given[i], max(1, left * weights[i] // mass), surplus)
            given[i] = given[i] + extra
            surplus = surplus - extra
    return np.array([bound] + given)


def ragged_sizes(stream_key, count, total, limit, skew):
    if count == 2:
        one = jax.random.randint(stream_key, (), max(1, total - limit), min(limit, total - 1) + 1)
        return jnp.stack([one, total - one])
    sizes = jnp.asarray(split_up(count, total, limit, skew), jnp.int32)
    pairs = (count - 1) // 2
    giver, receiver = sizes[1:1 + 2 * pairs:2], sizes[2:2 + 2 * pairs:2]
    slack = jnp.minimum(giver - 1, limit - receiver)
    moved = jax.random.randint(jax.random.fold_in(stream_key, 1), (pairs,), 0, 1 << 20) % (slack + 1)
    sizes = sizes.at[1:1 + 2 * pairs:2].set(giver - moved).at[2:2 + 2 * pairs:2].set(receiver + moved)
    return sizes[jax.random.permutation(jax.random.fold_in(stream_key, 2), count)]


def centred(key, shape, deviation, bound, cuts=(), kind=jnp.bfloat16):
    entries = deviation * jax.random.normal(key, shape, jnp.float32)
    if cuts:
        entries = entries * block_scale(key, shape, cuts, -0.22, 0.18)
    return jnp.clip(entries, -bound, bound).astype(kind)


def setup_inputs(seed: int = 0) -> dict:
    keys = jax.random.split(jax.random.key(seed), 11)
    events = centred(keys[0], (GROUPS, GROUP, D), 1.0, 6.0, ((0, 32), (1, 8)), jnp.float32)
    w_uvqk = centred(keys[1], (D, 4 * D), D ** -0.5, 0.25, (), jnp.float32)
    out_gain = jnp.clip(1.0 + 0.1 * jax.random.normal(keys[2], (D,), jnp.float32), 0.5, 1.5)
    w_out = centred(keys[3], (D, D), D ** -0.5, 0.25, (), jnp.float32)
    item_table = centred(keys[4], (ITEMS, D), D ** -0.5, 0.25, ((0, 32),), jnp.float32)
    user_lengths = jax.vmap(lambda own: ragged_sizes(own, USERS, GROUP, USER_MOST, 2))(jax.random.split(keys[5], GROUPS)).reshape((GROUPS, USERS)).astype(jnp.int32)
    neg_ids = with_ends(jax.random.randint(keys[6], (PANELS, PANEL), 0, CAND_DEV), jax.random.fold_in(keys[6], 1), 0, CAND_DEV - 1).astype(jnp.int32)
    panel_owner = with_ends(jax.random.randint(keys[7], (PANELS,), 0, N_ITEM), jax.random.fold_in(keys[7], 1), 0, N_ITEM - 1).astype(jnp.int32)
    block_mask = with_ends(jax.random.randint(keys[8], (GROUPS, GROUP // 128), 1, 2 ** (NEG // 128)), jax.random.fold_in(keys[8], 1), 1, (2 ** (NEG // 128)) - 1).astype(jnp.int32)
    targets = with_ends(jax.random.randint(keys[9], (GROUPS, GROUP), 0, NEG), jax.random.fold_in(keys[9], 1), 0, NEG - 1).astype(jnp.int32)
    return dict(events=events, w_uvqk=w_uvqk, out_gain=out_gain, w_out=w_out, item_table=item_table, user_lengths=user_lengths, neg_ids=neg_ids, panel_owner=panel_owner, block_mask=block_mask, targets=targets)


highest = lax.Precision.HIGHEST
beta_weight = 0.75
epsilon = 1e-05

def user_index(lengths, positions):
    user_ends = jnp.cumsum(lengths).astype(jnp.int32)
    return lax.optimization_barrier(jnp.sum((positions[:, None] >= user_ends[None, :]).astype(jnp.int32), axis=1))

def loss_terms(outputs, negatives, mask_words, target_cols):
    logits = jnp.einsum('td,nd->tn', outputs, negatives, precision=highest)
    columns = jnp.arange(negatives.shape[0], dtype=jnp.int32)
    mask_bits = jnp.repeat(mask_words, 128)
    live_cols = jnp.bitwise_and(jnp.right_shift(mask_bits[:, None], columns[None, :] // 128), 1).astype(logits.dtype)
    is_target = (columns[None, :] == target_cols[:, None]).astype(logits.dtype)
    neg_weight = live_cols * (1.0 - is_target)
    loss_part = jnp.sum(beta_weight * is_target * jax.nn.softplus(-logits) + neg_weight * jax.nn.softplus(logits))
    grad_logits = neg_weight * jax.nn.sigmoid(logits) - beta_weight * is_target * jax.nn.sigmoid(-logits)
    grad_rows = jnp.dot(grad_logits, negatives, precision=highest)
    panel_part = jnp.einsum('tn,td->nd', grad_logits, outputs, precision=highest)
    return (loss_part, grad_rows, panel_part)

def hstu_group(rows_in, lengths, w_uvqk, out_gain, w_out):
    group_len, width = rows_in.shape
    projected = jax.nn.silu(jnp.dot(rows_in, w_uvqk, precision=highest))
    gates_u = projected[:, :width]
    packed = projected[:, width:].reshape(group_len, 3, H, width // H)
    positions = jnp.arange(group_len, dtype=jnp.int32)
    user_ids = user_index(lengths, positions)
    allowed = ((user_ids[:, None] == user_ids[None, :]) & (positions[:, None] >= positions[None, :])).astype(rows_in.dtype)

    def one_head(stacked):
        scores = jnp.dot(stacked[:, 1], stacked[:, 2].T, precision=highest)
        return jnp.dot(jax.nn.silu(scores) * allowed, stacked[:, 0], precision=highest)
    attended = lax.map(one_head, jnp.transpose(packed, (2, 0, 1, 3)))
    attended = jnp.transpose(attended, (1, 0, 2)).reshape(group_len, width)
    row_mean = lax.optimization_barrier(jnp.mean(attended, axis=1, keepdims=True))
    centered = attended - row_mean
    variance = lax.optimization_barrier(jnp.mean(centered * centered, axis=1, keepdims=True))
    normed = centered * lax.rsqrt(variance + epsilon) * out_gain
    return rows_in + jnp.dot(normed * gates_u, w_out, precision=highest)

def reference(events, w_uvqk, out_gain, w_out, item_table, user_lengths, neg_ids, panel_owner, block_mask, targets):
    table_rows = (panel_owner[:, None] * CAND_DEV + neg_ids).reshape(-1).astype(jnp.int32)
    negatives = item_table[table_rows]

    def group_step(running, group_args):
        loss_sum, panel_sum = running
        rows_in, lengths, mask_words, target_cols = group_args
        outputs = hstu_group(rows_in, lengths, w_uvqk, out_gain, w_out)
        loss_part, grad_rows, panel_part = loss_terms(outputs, negatives, mask_words, target_cols)
        return ((loss_sum + loss_part, panel_sum + panel_part), grad_rows)
    start_carry = (jnp.zeros((), jnp.float32), jnp.zeros(negatives.shape, jnp.float32))
    (loss_total, panel_total), event_grad = lax.scan(group_step, start_carry, (events, user_lengths, block_mask, targets))
    table_grad = jnp.zeros_like(item_table).at[table_rows].add(panel_total)
    return (loss_total / TOKENS, event_grad, table_grad)
```

```python
import functools

import jax
import jax.numpy as jnp
from jax import lax
from jax.experimental import pallas as pl
from jax.experimental.pallas import tpu as pltpu
from jax.sharding import PartitionSpec as P

H = 16
X_RING = 4
beta_weight = 0.75
epsilon = 1e-05
f32, bf16 = jnp.float32, jnp.bfloat16
MESH = pl.DeviceIdType.MESH
VMEM_LIMIT = 60 * 1024 * 1024

VM = pl.BlockSpec(memory_space=pltpu.VMEM)
SM = pl.BlockSpec(memory_space=pltpu.SMEM)
ANY = pl.BlockSpec(memory_space=pl.ANY)
NN = (((1,), (0,)), ((), ()))
NT = (((1,), (1,)), ((), ()))
TN = (((0,), (0,)), ((), ()))


def split(x):
    hi = x.astype(bf16)
    return hi, (x - hi.astype(f32)).astype(bf16)


def mm(a, b, dims=NN):
    return lax.dot_general(a, b, dims, preferred_element_type=f32)


def mm3(a, b, dims=NN):
    (ah, al), (bh, bl) = a, b
    return mm(ah, bh, dims) + (mm(al, bh, dims) + mm(ah, bl, dims))


def sigmoid(x):
    return 0.5 + 0.5 * jnp.tanh(0.5 * x)


class Place:
    def __init__(self, n_seq, n_item):
        self.S, self.I = n_seq, n_item
        self.X = X_RING
        self.Z = n_item // self.X
        self.Y = n_seq // 2
        self.s = lax.axis_index("seq")
        self.i = lax.axis_index("item")
        self.y, self.c = self.s // 2, self.s % 2
        self.z, self.x = self.i // self.X, self.i % self.X

    def at_x(self, x):
        return (self.s, self.z * self.X + x)

    def at_z(self, z):
        return (self.s, z * self.X + self.x)

    def at_y(self, y):
        return (2 * y + self.c, self.i)

    def at_s(self, s):
        return (s, self.i)

    def partner(self):
        return (2 * self.y + 1 - self.c, self.i)


def rdma(src, dst, send, recv, dev):
    return pltpu.make_async_remote_copy(
        src_ref=src, dst_ref=dst, send_sem=send, recv_sem=recv, device_id=dev, device_id_type=MESH
    )


class Ring4:
    def __init__(self, me, dev, part, src, send, recv):
        self.me, self.dev, self.part, self.src = me, dev, part, src
        self.send, self.recv = send, recv
        self.right, self.left = (me + 1) % 4, (me + 3) % 4
        self.opp = (me + 2) % 4

    def _c(self, slot, src, k, h, to):
        return rdma(src, self.part(k, h), self.send.at[slot], self.recv.at[slot], self.dev(to))

    def start(self):
        me = self.me
        self.r = [self._c(h, self.src(h), me, h, self.right) for h in (0, 1)]
        self.l = [self._c(2 + h, self.src(h), me, h, self.left) for h in (0, 1)]
        self.r[0].start()
        self.l[1].start()
        self.r[1].start()
        self.l[0].start()

    def forward_right(self):
        self.r[0].wait_recv()
        self.fr = self._c(4, self.part(self.left, 0), self.left, 0, self.right)
        self.fr.start()

    def forward_left(self):
        self.l[1].wait_recv()
        self.fl = self._c(5, self.part(self.right, 1), self.right, 1, self.left)
        self.fl.start()

    def wait_left(self):
        self.r[1].wait_recv()

    def wait_right(self):
        self.l[0].wait_recv()

    def wait_opp(self):
        self.fr.wait_recv()
        self.fl.wait_recv()

    def wait_sends(self):
        for c in (*self.r, *self.l, self.fr, self.fl):
            c.wait_send()


class CoreSends:
    def __init__(self, dev, send, recv):
        self.dev, self.send, self.recv, self.copies = dev, send, recv, []

    def push(self, src, dst):
        n = len(self.copies)
        c = rdma(src, dst, self.send.at[n], self.recv.at[n], self.dev)
        c.start()
        self.copies.append(c)

    def finish(self):
        for c in self.copies:
            c.wait()


def entry_barrier(devs):
    barrier = pltpu.get_barrier_semaphore()
    for d in devs:
        pl.semaphore_signal(barrier, inc=1, device_id=d, device_id_type=MESH)
    pl.semaphore_wait(barrier, len(devs))


def seq_peers(pc):
    return [pc.at_s((pc.s + d) % pc.S) for d in range(1, pc.S)]


def plane_peers(pc):
    xs = [pc.at_x((pc.x + d) % pc.X) for d in range(1, pc.X)]
    zs = [pc.at_z((pc.z + d) % pc.Z) for d in range(1, pc.Z)]
    return xs + zs


class SeqGather:
    def __init__(self, pc, src, full, send, recv, csend, crecv, lsem):
        half = src.shape[0] // 2
        self.pc, self.full, self.src = pc, full, src
        part = lambda y, h: full.at[2 * y + pc.c, pl.ds(h * half, half)]
        own = lambda h: src.at[pl.ds(h * half, half)]
        self.ring = Ring4(pc.y, pc.at_y, part, own, send, recv)
        self.core = CoreSends(pc.partner(), csend, crecv)
        self.local = pltpu.make_async_copy(src, full.at[pc.s], lsem)

    def blk(self, y):
        return self.full.at[2 * y + self.pc.c]

    def start(self):
        self.ring.start()
        self.core.push(self.src, self.blk(self.pc.y))
        self.local.start()

    def middle(self):
        r = self.ring
        r.forward_right()
        r.forward_left()
        r.wait_left()
        self.core.push(self.blk(r.left), self.blk(r.left))
        r.wait_right()
        self.core.push(self.blk(r.right), self.blk(r.right))

    def finish(self):
        r = self.ring
        r.wait_opp()
        self.core.push(self.blk(r.opp), self.blk(r.opp))
        r.wait_sends()
        self.core.finish()
        self.local.wait()


SEQ_SEMS = [pltpu.SemaphoreType.DMA((6,))] * 2 + [pltpu.SemaphoreType.DMA((4,))] * 2 + [
    pltpu.SemaphoreType.DMA
]


class Reduce:
    def __init__(self, pc, part, full, rx, sx, rz, own, sems):
        self.pc, self.part, self.full = pc, part, full
        self.rx, self.sx, self.rz, self.own = rx, sx, rz, own
        self.xs, self.xr, self.zs, self.zr, self.gs, self.gr = sems[:6]
        self.a1, self.a2, self.b1, self.b2 = sems[6:10], sems[10:12], sems[12:14], sems[14:16]
        self.sems = sems

    def start_x(self):
        pc = self.pc
        self.cx = []
        for d in (2, 1, 3):
            to = (pc.x + d) % pc.X
            c = rdma(
                self.part.at[to], self.rx.at[d - 1], self.xs.at[d - 1], self.xr.at[d - 1], pc.at_x(to)
            )
            c.start()
            self.cx.append(c)

    def start_z(self):
        pc = self.pc
        for c in self.cx:
            c.wait_recv()
        self.sx[...] = (self.part[pc.x] + self.rx[0]) + (self.rx[1] + self.rx[2])
        self.cz = []
        for d in range(1, pc.Z):
            to = (pc.z + d) % pc.Z
            c = rdma(self.sx.at[to], self.rz.at[d - 1], self.zs.at[d - 1], self.zr.at[d - 1], pc.at_z(to))
            c.start()
            self.cz.append(c)

    def start_gather(self):
        pc = self.pc
        total = self.sx[pc.z]
        for d, c in enumerate(self.cz):
            c.wait_recv()
        for d in range(pc.Z - 1):
            total = total + self.rz[d]
        half = total.shape[1] // 2
        rows = total.shape[0]
        self.own[0] = total[:, :half]
        self.own[1] = total[:, half:]
        mine = self.full.at[:, pc.y, pc.c, pc.x, pl.ds(pl.multiple_of(pc.z * rows, rows), rows), :]
        self.local = pltpu.make_async_copy(self.own, mine, self.sems[16])
        self.local.start()
        self.cg = []
        for d in range(1, pc.Z):
            to = (pc.z + d) % pc.Z
            c = rdma(self.own, mine, self.gs.at[d - 1], self.gr.at[d - 1], pc.at_z(to))
            c.start()
            self.cg.append(c)

    def rings(self):
        pc, full, sems = self.pc, self.full, self.sems
        zr = full.shape[4]
        hz = zr // 2
        for c in self.cg:
            c.wait_recv()
        self.local.wait()

        ax_part = lambda k, h: full.at[0, pc.y, pc.c, k, pl.ds(h * hz, hz), :]
        ax = Ring4(pc.x, pc.at_x, ax_part, lambda h: ax_part(pc.x, h), sems[6], sems[7])
        by_part = lambda k, h: full.at[1, k, pc.c, pc.x, pl.ds(h * hz, hz), :]
        by = Ring4(pc.y, pc.at_y, by_part, lambda h: by_part(pc.y, h), sems[8], sems[9])
        ay_part = lambda k, h: full.at[0, k, pc.c, pl.ds(2 * h, 2), :, :]
        ay = Ring4(pc.y, pc.at_y, ay_part, lambda h: ay_part(pc.y, h), sems[10], sems[11])
        bx_part = lambda k, h: full.at[1, pl.ds(2 * h, 2), pc.c, k, :, :]
        bx = Ring4(pc.x, pc.at_x, bx_part, lambda h: bx_part(pc.x, h), sems[12], sems[13])
        core = CoreSends(pc.partner(), sems[14], sems[15])
        a_blk = lambda k: full.at[0, k, pc.c]
        b_blk = lambda k: full.at[1, :, pc.c, k]
        push_a = lambda k: core.push(a_blk(k), a_blk(k))
        push_b = lambda k: core.push(b_blk(k), b_blk(k))

        ax.start()
        by.start()
        ax.forward_right()
        by.forward_right()
        ax.forward_left()
        by.forward_left()
        ax.wait_left()
        ax.wait_right()
        ax.wait_opp()
        ay.start()
        push_a(pc.y)
        by.wait_left()
        by.wait_right()
        by.wait_opp()
        bx.start()
        push_b(pc.x)
        ay.forward_right()
        bx.forward_right()
        ay.forward_left()
        bx.forward_left()
        ay.wait_left()
        push_a(ay.left)
        bx.wait_left()
        push_b(bx.left)
        ay.wait_right()
        push_a(ay.right)
        bx.wait_right()
        push_b(bx.right)
        ay.wait_opp()
        push_a(ay.opp)
        bx.wait_opp()
        push_b(bx.opp)
        for r in (ax, by, ay, bx):
            r.wait_sends()
        for c in (*self.cx, *self.cz, *self.cg):
            c.wait_send()
        core.finish()


def reduce_scratch(X, Z, R, D):
    D6 = pltpu.SemaphoreType.DMA((6,))
    D8 = pltpu.SemaphoreType.DMA((8,))
    DX = pltpu.SemaphoreType.DMA((X - 1,))
    DZ = pltpu.SemaphoreType.DMA((max(Z - 1, 1),))
    return [
        pltpu.VMEM((X - 1, Z, R, D), f32),
        pltpu.VMEM((Z, R, D), f32),
        pltpu.VMEM((max(Z - 1, 1), R, D), f32),
        pltpu.VMEM((2, R, D // 2), f32),
        DX, DX, DZ, DZ, DZ, DZ,
        D6, D6, D6, D6, D6, D6, D6, D6,
        D8, D8,
        pltpu.SemaphoreType.DMA,
    ]


N_REDUCE = 21


def gather_rows_kernel(n_seq, n_item, neg_ref, owner_ref, table_ref, part_ref):
    pc = Place(n_seq, n_item)
    rows, share = table_ref.shape[0], part_ref.shape[0]
    per_panel = neg_ref.shape[1] // share
    panel = pc.s // per_panel
    first = pl.multiple_of((pc.s % per_panel) * share, share)
    ids = neg_ref[pl.ds(panel, 1), pl.ds(first, share)]
    own = owner_ref[panel] == pc.i

    @pl.when(own)
    def _():
        spot = lax.broadcasted_iota(jnp.int32, (rows, share), 0)
        pick = jnp.where(spot == ids, 1.0, 0.0).astype(bf16)
        hi, lo = split(table_ref[...])
        part_ref[...] = mm(pick, hi, TN) + mm(pick, lo, TN)

    @pl.when(jnp.logical_not(own))
    def _():
        part_ref[...] = jnp.zeros_like(part_ref)


def first_kernel(n_seq, n_item, ev_ref, part_ref, ev_all, neg_all, *scratch):
    pc = Place(n_seq, n_item)
    seq = SeqGather(pc, ev_ref.at[0], ev_all, *scratch[:5])
    red = Reduce(pc, part_ref, neg_all, *scratch[5:9], scratch[9:])
    entry_barrier(plane_peers(pc) + seq_peers(pc))
    red.start_x()
    seq.start()
    red.start_z()
    seq.middle()
    red.start_gather()
    seq.finish()
    red.rings()


def attention_kernel(
    n_seq, n_item, ev_all, lens_ref, w_ref, gain_ref, wo_ref, tgt_ref, msk_ref, out_ref,
    xw, xh, xl, kvh, kvl, qs, gates, att, allow, sem,
):
    pc = Place(n_seq, n_item)
    tok, D = xw.shape[1], xw.shape[2]
    win = xw.shape[0] * tok
    w0 = jnp.maximum(pc.s - (xw.shape[0] - 1), 0)
    copy = pltpu.make_async_copy(ev_all.at[pl.ds(w0, xw.shape[0])], xw, sem)
    copy.start()
    copy.wait()
    q_blk = pc.s - w0
    hi, lo = split(xw[...].reshape(win, D))
    xh[...] = hi
    xl[...] = lo
    half = D // 2

    def project(first, xs):
        return mm3(xs, split(w_ref[:, pl.ds(pl.multiple_of(first, half), half)]))

    def kv_step(n, _):
        r = project(jnp.where(n < 2, D + n * half, 2 * D + n * half), (xh[...], xl[...]))
        kvh[n], kvl[n] = split(r * sigmoid(r))
        return 0

    lax.fori_loop(0, 4, kv_step, 0)
    x_own = xw[q_blk]
    xo = split(x_own)
    for n in range(2):
        r = project(2 * D + n * half, xo)
        qs[n] = r * sigmoid(r)
        r = project(n * half, xo)
        gates[n] = r * sigmoid(r)

    row = pc.s * tok + lax.broadcasted_iota(jnp.int32, (tok, win), 0)
    col = w0 * tok + lax.broadcasted_iota(jnp.int32, (tok, win), 1)
    begin = jnp.zeros((tok, win), jnp.int32)
    end = lens_ref[0, 0]
    for u in range(1, lens_ref.shape[1] + 1):
        begin = jnp.where(row >= end, end, begin)
        if u < lens_ref.shape[1]:
            end = end + lens_ref[0, u]
    allow[...] = jnp.where((col >= begin) & (col <= row), 1.0, 0.0)

    hd = D // H
    hpg = 128 // hd
    lane_head = lax.broadcasted_iota(jnp.int32, (tok, 128), 1) // hd

    def heads(m, _):
        for g in range(half // 128):
            lanes = slice(g * 128, (g + 1) * 128)
            kh, kl = kvh[2 + m][:, lanes], kvl[2 + m][:, lanes]
            vh, vl = kvh[m][:, lanes], kvl[m][:, lanes]
            q = qs[m][:, lanes]
            qst = jnp.concatenate([jnp.where(lane_head == h, q, 0.0) for h in range(hpg)], axis=0)
            qh, ql = split(qst)
            sc = mm(jnp.concatenate([qh, ql], axis=1), jnp.concatenate([kh, kh], axis=1), NT)
            sc = sc + mm(qh, kl, NT)
            p = (sc * sigmoid(sc)).reshape(hpg, tok, win) * allow[...][None]
            ph, plo = split(p.reshape(hpg * tok, win))
            o = mm(ph, jnp.concatenate([vh, vl], axis=1))
            o = (o[:, :128] + o[:, 128:]) + mm(plo, vh)
            got = jnp.zeros((tok, 128), f32)
            for h in range(hpg):
                got = got + jnp.where(lane_head == h, o[h * tok:(h + 1) * tok], 0.0)
            att[m, :, lanes] = got
        return 0

    lax.fori_loop(0, 2, heads, 0)
    a = jnp.concatenate([att[0], att[1]], axis=1)
    centered = a - jnp.mean(a, axis=1, keepdims=True)
    var = jnp.mean(centered * centered, axis=1, keepdims=True)
    normed = centered * lax.rsqrt(var + epsilon) * gain_ref[...]
    gated = normed * jnp.concatenate([gates[0], gates[1]], axis=1)
    out_ref[:tok, :] = x_own + mm3(split(gated), split(wo_ref[...]))
    out_ref[tok:, :] = jnp.zeros((out_ref.shape[0] - tok, D), f32)
    out_ref[tok:tok + 1, :tok] = tgt_ref[...].astype(f32)
    out_ref[tok:tok + 1, tok:2 * tok] = jnp.broadcast_to(msk_ref[...], (1, tok)).astype(f32)


def outputs_kernel(n_seq, n_item, out_ref, out_all, *scratch):
    pc = Place(n_seq, n_item)
    seq = SeqGather(pc, out_ref, out_all, *scratch)
    entry_barrier(seq_peers(pc))
    seq.start()
    seq.middle()
    seq.finish()


def loss_core(logits, target, live):
    m = jnp.where(target, -logits, logits)
    w = jnp.where(target, -beta_weight, live)
    e = jnp.exp(-jnp.abs(m))
    sig = jnp.where(m >= 0.0, 1.0, e) / (1.0 + e)
    return w * sig, jnp.abs(w), jnp.maximum(m, 0.0) + jnp.log1p(e)


def loss_kernel(
    n_seq, n_item, out_all, neg_ref, grad_ref, panel_ref, loss_ref, acc, loss_acc,
):
    pc = Place(n_seq, n_item)
    tok, D = grad_ref.shape[1], grad_ref.shape[2]
    half = D // 2
    share = panel_ref.shape[0]
    mine = out_all[pc.s]
    oh = [split(mine[:tok, k * half:(k + 1) * half]) for k in (0, 1)]
    tcol = jnp.transpose(jnp.broadcast_to(mine[tok:tok + 1, :tok], (tok, tok)))
    tcol = jnp.concatenate([tcol, tcol], axis=1).astype(jnp.int32)
    mcol = jnp.broadcast_to(mine[tok:tok + 1, tok:tok + 1], (tok, 2 * tok)).astype(jnp.int32)
    lane = lax.broadcasted_iota(jnp.int32, (tok, 2 * tok), 1)
    acc[...] = jnp.zeros_like(acc)
    loss_acc[...] = jnp.zeros_like(loss_acc)
    step = 2 * tok

    def own_tokens(j, _):
        at = pl.ds(pl.multiple_of(j * step, step), step)
        n0, n1 = split(neg_ref[0, at, :]), split(neg_ref[1, at, :])
        logits = mm3(oh[0], n0, NT) + mm3(oh[1], n1, NT)
        live = (jnp.right_shift(mcol, 2 * j + lane // 128) & 1).astype(f32)
        g, w, sp = loss_core(logits, lane + j * step == tcol, live)
        loss_acc[...] += w * sp
        gs = split(g)
        acc[0] += mm3(gs, n0)
        acc[1] += mm3(gs, n1)
        return 0

    lax.fori_loop(0, neg_ref.shape[1] // step, own_tokens, 0)
    grad_ref[0, :, :half] = acc[0]
    grad_ref[0, :, half:] = acc[1]
    loss_ref[...] = jnp.broadcast_to(jnp.sum(loss_acc[...]), loss_ref.shape)

    at = pl.ds(pl.multiple_of(pc.s * share, share), share)
    m0, m1 = split(neg_ref[0, at, :]), split(neg_ref[1, at, :])
    sub = lax.broadcasted_iota(jnp.int32, (share, 2 * tok), 0)
    panel_ref[...] = jnp.zeros_like(panel_ref)

    def own_columns(b, _):
        pair = [out_all[2 * b], out_all[2 * b + 1]]
        ob = jnp.concatenate([p[:tok] for p in pair], axis=0)
        tg = jnp.concatenate([p[tok:tok + 1, :tok] for p in pair], axis=1).astype(jnp.int32)
        mk = jnp.concatenate([p[tok:tok + 1, tok:2 * tok] for p in pair], axis=1).astype(jnp.int32)
        obh, obl = split(ob)
        k0 = (obh[:, :half], obl[:, :half])
        k1 = (obh[:, half:], obl[:, half:])
        logits = mm3(m0, k0, NT) + mm3(m1, k1, NT)
        column = pc.s * share + sub
        live = (jnp.right_shift(jnp.broadcast_to(mk, column.shape), column // 128) & 1).astype(f32)
        g, _, _ = loss_core(logits, column == jnp.broadcast_to(tg, column.shape), live)
        panel_ref[...] += mm3(split(g), (obh, obl))
        return 0

    lax.fori_loop(0, out_all.shape[0] // 2, own_columns, 0)


def last_kernel(n_seq, n_item, part_ref, loss_ref, panel_all, total_ref, *scratch):
    pc = Place(n_seq, n_item)
    red = Reduce(pc, part_ref, panel_all, *scratch[:4], scratch[4:N_REDUCE])
    (lx, tx, lz, tz, ls, xs, xr, zs, zr, ss, sr) = scratch[N_REDUCE:]
    entry_barrier(plane_peers(pc) + seq_peers(pc))
    red.start_x()
    copies = []
    for d in range(1, pc.X):
        c = rdma(loss_ref, lx.at[d - 1], xs.at[d - 1], xr.at[d - 1], pc.at_x((pc.x + d) % pc.X))
        c.start()
        copies.append(c)
    red.start_z()
    for c in copies:
        c.wait_recv()
    tx[...] = loss_ref[...] + lx[0] + lx[1] + lx[2]
    more = []
    for d in range(1, pc.Z):
        c = rdma(tx, lz.at[d - 1], zs.at[d - 1], zr.at[d - 1], pc.at_z((pc.z + d) % pc.Z))
        c.start()
        more.append(c)
    red.start_gather()
    total = tx[...]
    for c in more:
        c.wait_recv()
    for d in range(pc.Z - 1):
        total = total + lz[d]
    tz[...] = total
    last = []
    for d in range(1, pc.S):
        c = rdma(tz, ls.at[d - 1], ss.at[d - 1], sr.at[d - 1], pc.at_s((pc.s + d) % pc.S))
        c.start()
        last.append(c)
    red.rings()
    for c in last:
        c.wait_recv()
    for d in range(pc.S - 1):
        total = total + ls[d]
    total_ref[...] = total
    for c in (*copies, *more, *last):
        c.wait_send()


def scatter_kernel(n_item, scale, panel_all, neg_ref, owner_ref, total_ref, table_ref, loss_ref, buf, sem):
    item = lax.axis_index("item")
    rows = table_ref.shape[0]
    panel = neg_ref.shape[1]
    half = buf.shape[2]
    table_ref[...] = jnp.zeros_like(table_ref)
    loss_ref[...] = total_ref[...] * scale
    for p in range(neg_ref.shape[0]):

        @pl.when(owner_ref[p] == item)
        def _():
            copy = pltpu.make_async_copy(panel_all.at[:, pl.ds(p * panel, panel), :], buf, sem)
            copy.start()
            spot = lax.broadcasted_iota(jnp.int32, (rows, panel), 0)
            pick = jnp.where(spot == neg_ref[pl.ds(p, 1), :], 1.0, 0.0).astype(bf16)
            copy.wait()
            for k in (0, 1):
                hi, lo = split(buf[k])
                table_ref[:, k * half:(k + 1) * half] += mm(pick, hi) + mm(pick, lo)


def params(cid=None):
    if cid is None:
        return pltpu.CompilerParams(vmem_limit_bytes=VMEM_LIMIT)
    return pltpu.CompilerParams(
        vmem_limit_bytes=VMEM_LIMIT, collective_id=cid, has_side_effects=True
    )


def per_device(
    n_seq, n_item, events, w_uvqk, out_gain, w_out, item_table,
    user_lengths, neg_ids, panel_owner, block_mask, targets,
):
    _, tok, D = events.shape
    X, Z, Y = X_RING, n_item // X_RING, n_seq // 2
    n_neg = neg_ids.shape[0] * neg_ids.shape[1]
    share = n_neg // n_seq
    R = share // n_item
    half = D // 2
    shape = jax.ShapeDtypeStruct

    part = pl.pallas_call(
        functools.partial(gather_rows_kernel, n_seq, n_item),
        out_shape=shape((share, D), f32),
        in_specs=[VM, SM, VM], out_specs=VM, compiler_params=params(), name="gather_rows",
    )(neg_ids, panel_owner, item_table)

    full = shape((2, Y, 2, X, Z * R, half), f32)
    ev_all, neg_all = pl.pallas_call(
        functools.partial(first_kernel, n_seq, n_item),
        out_shape=(shape((n_seq, tok, D), f32), full),
        in_specs=[VM, VM], out_specs=(ANY, ANY),
        scratch_shapes=SEQ_SEMS + reduce_scratch(X, Z, R, D),
        compiler_params=params(1), name="first_exchange",
    )(events, part.reshape(X, Z, R, D))

    blocks = 5
    win = blocks * tok
    aug = tok + 16
    outputs = pl.pallas_call(
        functools.partial(attention_kernel, n_seq, n_item),
        out_shape=shape((aug, D), f32),
        in_specs=[ANY, SM, VM, VM, VM, VM, VM], out_specs=VM,
        scratch_shapes=[
            pltpu.VMEM((blocks, tok, D), f32),
            pltpu.VMEM((win, D), bf16), pltpu.VMEM((win, D), bf16),
            pltpu.VMEM((4, win, half), bf16), pltpu.VMEM((4, win, half), bf16),
            pltpu.VMEM((2, tok, half), f32), pltpu.VMEM((2, tok, half), f32),
            pltpu.VMEM((2, tok, half), f32), pltpu.VMEM((tok, win), f32),
            pltpu.SemaphoreType.DMA,
        ],
        compiler_params=params(), name="attention",
    )(ev_all, user_lengths, w_uvqk, out_gain.reshape(1, D), w_out, targets, block_mask)

    out_all = pl.pallas_call(
        functools.partial(outputs_kernel, n_seq, n_item),
        out_shape=shape((n_seq, aug, D), f32),
        in_specs=[VM], out_specs=ANY, scratch_shapes=SEQ_SEMS,
        compiler_params=params(2), name="gather_outputs",
    )(outputs)

    event_grad, panel, loss = pl.pallas_call(
        functools.partial(loss_kernel, n_seq, n_item),
        out_shape=(shape((1, tok, D), f32), shape((share, D), f32), shape((8, 128), f32)),
        in_specs=[VM, VM], out_specs=(VM, VM, VM),
        scratch_shapes=[pltpu.VMEM((2, tok, half), f32), pltpu.VMEM((tok, 2 * tok), f32)],
        compiler_params=params(), name="loss",
    )(out_all, neg_all.reshape(2, n_neg, half))

    tile = pltpu.VMEM((8, 128), f32)
    dma = pltpu.SemaphoreType.DMA
    nz = max(Z - 1, 1)
    panel_all, total = pl.pallas_call(
        functools.partial(last_kernel, n_seq, n_item),
        out_shape=(full, shape((8, 128), f32)),
        in_specs=[VM, VM], out_specs=(ANY, VM),
        scratch_shapes=reduce_scratch(X, Z, R, D) + [
            pltpu.VMEM((X - 1, 8, 128), f32), tile, pltpu.VMEM((nz, 8, 128), f32), tile,
            pltpu.VMEM((n_seq - 1, 8, 128), f32),
            dma((X - 1,)), dma((X - 1,)), dma((nz,)), dma((nz,)), dma((n_seq - 1,)), dma((n_seq - 1,)),
        ],
        compiler_params=params(3), name="last_exchange",
    )(panel.reshape(X, Z, R, D), loss)

    scale = 1.0 / (tok * n_seq * n_item)
    table_grad, mean_loss = pl.pallas_call(
        functools.partial(scatter_kernel, n_item, scale),
        out_shape=(shape(item_table.shape, f32), shape((8, 128), f32)),
        in_specs=[ANY, VM, SM, VM], out_specs=(VM, VM),
        scratch_shapes=[pltpu.VMEM((2, neg_ids.shape[1], half), f32), pltpu.SemaphoreType.DMA],
        compiler_params=params(), name="scatter",
    )(panel_all.reshape(2, n_neg, half), neg_ids, panel_owner, total)
    return (mean_loss[0, 0], event_grad, table_grad)


def solution(mesh):
    placed = (
        P("item", "seq", None), P(), P(), P(), P("item", None), P("item", None),
        P(), P(), P("item", "seq"), P("item", "seq"),
    )
    body = functools.partial(per_device, mesh.shape["seq"], mesh.shape["item"])
    return jax.shard_map(
        body, mesh=mesh, in_specs=placed,
        out_specs=(P(), P("item", "seq", None), P("item", None)), check_vma=False,
    )
```

```python
import functools

import jax
import jax.numpy as jnp
from jax import lax
from jax.experimental import pallas as pl
from jax.experimental.pallas import tpu as pltpu
from jax.sharding import PartitionSpec as P

H = 16
X_RING = 4
beta_weight = 0.75
epsilon = 1e-05
f32, bf16 = jnp.float32, jnp.bfloat16
MESH = pl.DeviceIdType.MESH
VMEM_LIMIT = 60 * 1024 * 1024

VM = pl.BlockSpec(memory_space=pltpu.VMEM)
SM = pl.BlockSpec(memory_space=pltpu.SMEM)
ANY = pl.BlockSpec(memory_space=pl.ANY)
NN = (((1,), (0,)), ((), ()))
NT = (((1,), (1,)), ((), ()))
TN = (((0,), (0,)), ((), ()))


def split(x):
    hi = x.astype(bf16)
    return hi, (x - hi.astype(f32)).astype(bf16)


def mm(a, b, dims=NN):
    return lax.dot_general(a, b, dims, preferred_element_type=f32)


def mm3(a, b, dims=NN):
    (ah, al), (bh, bl) = a, b
    return mm(ah, bh, dims) + (mm(al, bh, dims) + mm(ah, bl, dims))


def sigmoid(x):
    return 0.5 + 0.5 * jnp.tanh(0.5 * x)


class Place:
    def __init__(self, n_seq, n_item):
        self.S, self.I = n_seq, n_item
        self.X = X_RING
        self.Z = n_item // self.X
        self.Y = n_seq // 2
        self.s = lax.axis_index("seq")
        self.i = lax.axis_index("item")
        self.y, self.c = self.s // 2, self.s % 2
        self.z, self.x = self.i // self.X, self.i % self.X

    def at_x(self, x):
        return (self.s, self.z * self.X + x)

    def at_z(self, z):
        return (self.s, z * self.X + self.x)

    def at_y(self, y):
        return (2 * y + self.c, self.i)

    def at_s(self, s):
        return (s, self.i)

    def partner(self):
        return (2 * self.y + 1 - self.c, self.i)


def rdma(src, dst, send, recv, dev):
    return pltpu.make_async_remote_copy(
        src_ref=src, dst_ref=dst, send_sem=send, recv_sem=recv, device_id=dev, device_id_type=MESH
    )


class Ring4:
    def __init__(self, me, dev, part, send, recv, causal=False):
        self.me, self.dev, self.part, self.causal = me, dev, part, causal
        self.send, self.recv = send, recv
        self.right, self.left = (me + 1) % 4, (me + 3) % 4
        self.opp = (me + 2) % 4

    def _c(self, slot, src, k, h, to):
        return rdma(src, self.part(k, h), self.send.at[slot], self.recv.at[slot], self.dev(to))

    def start(self):
        me = self.me
        self.r = [self._c(h, self.part(me, h), me, h, self.right) for h in (0, 1)]
        self.l1 = self._c(3, self.part(me, 1), me, 1, self.left)
        self.r[0].start()
        self.l1.start()
        self.r[1].start()
        self.l = [self.l1]
        if not self.causal:
            self.l.append(self._c(2, self.part(me, 0), me, 0, self.left))
            self.l[1].start()

    def forward_right(self):
        self.r[0].wait_recv()
        self.fr = self._c(4, self.part(self.left, 0), self.left, 0, self.right)
        self.fr.start()

    def forward_left(self):
        self.l1.wait_recv()
        self.fl = self._c(5, self.part(self.right, 1), self.right, 1, self.left)
        self.fl.start()

    def wait_left(self):
        self.r[1].wait_recv()

    def wait_right(self):
        self.l[1].wait_recv()

    def wait_opp(self):
        self.fr.wait_recv()
        self.fl.wait_recv()

    def wait_sends(self):
        for c in (*self.r, *self.l, self.fr, self.fl):
            c.wait_send()


class CoreSends:
    def __init__(self, dev, send, recv):
        self.dev, self.send, self.recv, self.copies = dev, send, recv, []

    def push(self, src, dst):
        n = len(self.copies)
        c = rdma(src, dst, self.send.at[n], self.recv.at[n], self.dev)
        c.start()
        self.copies.append(c)

    def wait_recv(self, n):
        self.copies[n].wait_recv()

    def wait_sends(self):
        for c in self.copies:
            c.wait_send()


def enter(devs):
    barrier = pltpu.get_barrier_semaphore()
    for d in devs:
        pl.semaphore_signal(barrier, inc=1, device_id=d, device_id_type=MESH)
    return lambda: pl.semaphore_wait(barrier, len(devs))


def seq_peers(pc):
    return [pc.at_s((pc.s + d) % pc.S) for d in range(1, pc.S)]


def plane_peers(pc):
    xs = [pc.at_x((pc.x + d) % pc.X) for d in range(1, pc.X)]
    zs = [pc.at_z((pc.z + d) % pc.Z) for d in range(1, pc.Z)]
    return xs + zs


class SeqGather:
    def __init__(self, pc, full, sems, causal=False):
        send, recv, csend, crecv = sems
        half = full.shape[1] // 2
        self.pc, self.full, self.causal = pc, full, causal
        part = lambda y, h: full.at[2 * y + pc.c, pl.ds(h * half, half)]
        self.ring = Ring4(pc.y, pc.at_y, part, send, recv, causal)
        self.core = CoreSends(pc.partner(), csend, crecv)

    def push(self, y):
        blk = self.full.at[2 * y + self.pc.c]
        self.core.push(blk, blk)

    def start(self):
        self.ring.start()
        self.push(self.pc.y)

    def forward(self):
        self.ring.forward_right()
        self.ring.forward_left()

    def near(self):
        r = self.ring
        r.wait_left()
        self.push(r.left)
        if not self.causal:
            r.wait_right()
            self.push(r.right)

    def far(self):
        self.ring.wait_opp()
        self.push(self.ring.opp)

    def pair(self, n):
        self.core.wait_recv(n)

    def wait_sends(self):
        self.ring.wait_sends()
        self.core.wait_sends()


def dma(n):
    return pltpu.SemaphoreType.DMA((n,))


SEQ_SEMS = [dma(6), dma(6), dma(4), dma(4)]


class Reduce:
    def __init__(self, pc, part, full, rx, sx, rz, own, sems):
        self.pc, self.part, self.full = pc, part, full
        self.rx, self.sx, self.rz, self.own = rx, sx, rz, own
        self.xs, self.xr, self.zs, self.zr, self.gs, self.gr = sems[:6]
        self.sems = sems

    def start_x(self):
        pc = self.pc
        self.cx = []
        for d in (2, 1, 3):
            to = (pc.x + d) % pc.X
            c = rdma(
                self.part.at[to], self.rx.at[d - 1], self.xs.at[d - 1], self.xr.at[d - 1], pc.at_x(to)
            )
            c.start()
            self.cx.append(c)

    def start_z(self):
        pc = self.pc
        for c in self.cx:
            c.wait_recv()
        self.sx[...] = (self.part[pc.x] + self.rx[0]) + (self.rx[1] + self.rx[2])
        self.cz = []
        for d in range(1, pc.Z):
            to = (pc.z + d) % pc.Z
            c = rdma(self.sx.at[to], self.rz.at[d - 1], self.zs.at[d - 1], self.zr.at[d - 1], pc.at_z(to))
            c.start()
            self.cz.append(c)

    def start_gather(self):
        pc = self.pc
        total = self.sx[pc.z]
        for d, c in enumerate(self.cz):
            c.wait_recv()
        for d in range(pc.Z - 1):
            total = total + self.rz[d]
        half = total.shape[1] // 2
        rows = total.shape[0]
        self.own[0] = total[:, :half]
        self.own[1] = total[:, half:]
        mine = self.full.at[:, pc.y, pc.c, pc.x, pl.ds(pl.multiple_of(pc.z * rows, rows), rows), :]
        self.local = pltpu.make_async_copy(self.own, mine, self.sems[16])
        self.local.start()
        self.cg = []
        for d in range(1, pc.Z):
            to = (pc.z + d) % pc.Z
            c = rdma(self.own, mine, self.gs.at[d - 1], self.gr.at[d - 1], pc.at_z(to))
            c.start()
            self.cg.append(c)

    def set_rings(self):
        pc, full, sems = self.pc, self.full, self.sems
        hz = full.shape[4] // 2
        hx, hy = pc.X // 2, pc.Y // 2
        ax = lambda k, h: full.at[0, pc.y, pc.c, k, pl.ds(h * hz, hz), :]
        by = lambda k, h: full.at[1, k, pc.c, pc.x, pl.ds(h * hz, hz), :]
        ay = lambda k, h: full.at[0, k, pc.c, pl.ds(hx * h, hx), :, :]
        bx = lambda k, h: full.at[1, pl.ds(hy * h, hy), pc.c, k, :, :]
        self.ax = Ring4(pc.x, pc.at_x, ax, sems[6], sems[7])
        self.by = Ring4(pc.y, pc.at_y, by, sems[8], sems[9])
        self.ay = Ring4(pc.y, pc.at_y, ay, sems[10], sems[11])
        self.bx = Ring4(pc.x, pc.at_x, bx, sems[12], sems[13])
        self.ca = CoreSends(pc.partner(), sems[14], sems[15])
        self.cb = CoreSends(pc.partner(), sems[17], sems[18])

    def push_a(self, k):
        blk = self.full.at[0, k, self.pc.c]
        self.ca.push(blk, blk)

    def push_b(self, k):
        blk = self.full.at[1, :, self.pc.c, k]
        self.cb.push(blk, blk)

    def rings_start(self):
        self.set_rings()
        for c in self.cg:
            c.wait_recv()
        self.local.wait()
        self.ax.start()
        self.by.start()

    def rings_forward(self):
        self.ax.forward_right()
        self.by.forward_right()
        self.ax.forward_left()
        self.by.forward_left()

    def b_start(self):
        self.by.wait_left()
        self.by.wait_right()
        self.by.wait_opp()
        self.bx.start()
        self.push_b(self.pc.x)

    def a_wait(self):
        self.ax.wait_left()
        self.ax.wait_right()
        self.ax.wait_opp()

    def a_start(self):
        self.ay.start()
        self.push_a(self.pc.y)

    def forward(self, r):
        r.forward_right()
        r.forward_left()

    def near(self, r, push):
        r.wait_left()
        push(r.left)
        r.wait_right()
        push(r.right)

    def far(self, r, push):
        r.wait_opp()
        push(r.opp)

    def wait_core(self):
        for c in (self.ca, self.cb):
            for n in range(4):
                c.wait_recv(n)

    def wait_sends(self):
        for r in (self.ax, self.by, self.ay, self.bx):
            r.wait_sends()
        for c in (*self.cx, *self.cz, *self.cg):
            c.wait_send()
        self.ca.wait_sends()
        self.cb.wait_sends()


def reduce_scratch(X, Z, R, D):
    nz = max(Z - 1, 1)
    return [
        pltpu.VMEM((X - 1, Z, R, D), f32),
        pltpu.VMEM((Z, R, D), f32),
        pltpu.VMEM((nz, R, D), f32),
        pltpu.VMEM((2, R, D // 2), f32),
        dma(X - 1), dma(X - 1), dma(nz), dma(nz), dma(nz), dma(nz),
        dma(6), dma(6), dma(6), dma(6), dma(6), dma(6), dma(6), dma(6),
        dma(4), dma(4), pltpu.SemaphoreType.DMA, dma(4), dma(4),
    ]


N_REDUCE = 23


class LossSum:
    def __init__(self, pc, refs):
        self.pc = pc
        (self.t0, self.lx, self.tx, self.lz, self.tz, self.ls,
         self.xs, self.xr, self.zs, self.zr, self.ss, self.sr) = refs
        self.all = []

    def _send(self, src, dst, send, recv, devs):
        out = []
        for d, dev in enumerate(devs):
            c = rdma(src, dst.at[d], send.at[d], recv.at[d], dev)
            c.start()
            out.append(c)
        self.all += out
        return out

    def start_x(self):
        pc = self.pc
        devs = [pc.at_x((pc.x + d) % pc.X) for d in range(1, pc.X)]
        self.c = self._send(self.t0, self.lx, self.xs, self.xr, devs)

    def _sum(self, own, got, n):
        for c in self.c:
            c.wait_recv()
        total = own[...]
        for d in range(n):
            total = total + got[d]
        return total

    def start_z(self):
        pc = self.pc
        self.tx[...] = self._sum(self.t0, self.lx, pc.X - 1)
        devs = [pc.at_z((pc.z + d) % pc.Z) for d in range(1, pc.Z)]
        self.c = self._send(self.tx, self.lz, self.zs, self.zr, devs)

    def start_s(self):
        pc = self.pc
        self.tz[...] = self._sum(self.tx, self.lz, pc.Z - 1)
        self.c = self._send(self.tz, self.ls, self.ss, self.sr, seq_peers(pc))

    def total(self):
        return self._sum(self.tz, self.ls, self.pc.S - 1)

    def wait_sends(self):
        for c in self.all:
            c.wait_send()


def loss_scratch(X, Z, S):
    nz = max(Z - 1, 1)
    tile = lambda *n: pltpu.VMEM((*n, 8, 128), f32)
    return [
        tile(), tile(X - 1), tile(), tile(nz), tile(), tile(S - 1),
        dma(X - 1), dma(X - 1), dma(nz), dma(nz), dma(S - 1), dma(S - 1),
    ]


N_LOSS = 12


def loss_core(logits, target, live):
    m = jnp.where(target, -logits, logits)
    w = jnp.where(target, -beta_weight, live)
    e = jnp.exp(-jnp.abs(m))
    sig = jnp.where(m >= 0.0, 1.0, e) / (1.0 + e)
    return w * sig, jnp.abs(w), jnp.maximum(m, 0.0) + jnp.log1p(e)


def main_kernel(
    n_seq, n_item, ev_ref, w_ref, gain_ref, wo_ref, table_ref, lens_ref, neg_ref, owner_ref,
    msk_ref, tgt_ref, grad_ref, panel_all, total_ref, *scratch,
):
    pc = Place(n_seq, n_item)
    (ev_all, neg_all, out_all, table, w, wo, wh, wl, kvh, kvl, qs, gates, att, part, panel,
     acc, loss_acc, s_ev, s_table, s_w, s_wo) = scratch[:21]
    rest = scratch[21:]
    ev = SeqGather(pc, ev_all, rest[:4], causal=True)
    out = SeqGather(pc, out_all, rest[4:8])
    rest = rest[8:]
    neg = Reduce(pc, part, neg_all, *rest[:4], rest[4:N_REDUCE])
    rest = rest[N_REDUCE:]
    pan = Reduce(pc, panel, panel_all, *rest[:4], rest[4:N_REDUCE])
    loss = LossSum(pc, rest[N_REDUCE:])

    tok, D = grad_ref.shape[1], grad_ref.shape[2]
    half = D // 2
    step = 2 * tok
    rows = table.shape[0]
    X, Z, R = part.shape[0], part.shape[1], part.shape[2]
    share = X * Z * R
    hd = D // H
    hpg = 128 // hd

    ready = enter(plane_peers(pc) + seq_peers(pc))
    c_ev = pltpu.make_async_copy(ev_ref.at[0], ev_all.at[pc.s], s_ev)
    c_table = pltpu.make_async_copy(table_ref, table, s_table)
    c_w = pltpu.make_async_copy(w_ref, w, s_w)
    c_wo = pltpu.make_async_copy(wo_ref, wo, s_wo)
    for c in (c_ev, c_table, c_w, c_wo):
        c.start()

    per_panel = neg_ref.shape[1] // share
    p = pc.s // per_panel
    first = pl.multiple_of((pc.s % per_panel) * share, share)
    ids = neg_ref[pl.ds(p, 1), pl.ds(first, share)] + rows * owner_ref[pl.ds(p, 1), :]
    spot = pc.i * rows + lax.broadcasted_iota(jnp.int32, (rows, share), 0)
    pick = jnp.where(spot == jnp.broadcast_to(ids, spot.shape), 1.0, 0.0).astype(bf16)
    c_table.wait()
    hi, lo = split(table[...])
    part[...] = (mm(pick, hi, TN) + mm(pick, lo, TN)).reshape(part.shape)
    c_ev.wait()
    ready()
    ev.start()
    neg.start_x()

    c_w.wait()

    def split_w(n, _):
        wh[n], wl[n] = split(w[:, pl.ds(pl.multiple_of(n * half, half), half)])
        return 0

    lax.fori_loop(0, 8, split_w, 0)
    x_own = ev_all[pc.s]
    xo = split(x_own)

    def project(xs, n):
        r = mm3(xs, (wh[n], wl[n]))
        return r * sigmoid(r)

    for n in range(2):
        qs[n] = project(xo, 4 + n)
        gates[n] = project(xo, n)
    att[...] = jnp.zeros_like(att)
    ev.forward()

    lane_head = lax.broadcasted_iota(jnp.int32, (tok, 128), 1) // hd
    row = pc.s * tok + lax.broadcasted_iota(jnp.int32, (tok, step), 0)
    lane = lax.broadcasted_iota(jnp.int32, (tok, step), 1)
    begin = jnp.zeros((tok, step), jnp.int32)
    end = jnp.zeros((1, 1), jnp.int32)
    for u in range(lens_ref.shape[1]):
        end = end + lens_ref[0:1, u:u + 1]
        wide = jnp.broadcast_to(end, row.shape)
        begin = jnp.where(row >= wide, wide, begin)

    def attend(y):
        xs = split(jnp.concatenate([ev_all[2 * y], ev_all[2 * y + 1]], axis=0))

        def kv_step(n, _):
            kvh[n], kvl[n] = split(project(xs, jnp.where(n < 2, 2 + n, 4 + n)))
            return 0

        lax.fori_loop(0, 4, kv_step, 0)
        col = y * step + lane
        allow = jnp.where((col >= begin) & (col <= row), 1.0, 0.0)

        def heads(m, _):
            for g in range(half // 128):
                lanes = slice(g * 128, (g + 1) * 128)
                kh, kl = kvh[2 + m][:, lanes], kvl[2 + m][:, lanes]
                vh, vl = kvh[m][:, lanes], kvl[m][:, lanes]
                q = qs[m][:, lanes]
                stack = [jnp.where(lane_head == h, q, 0.0) for h in range(hpg)]
                qh, ql = split(jnp.concatenate(stack, axis=0))
                two = jnp.concatenate([qh, ql], axis=1)
                sc = mm(two, jnp.concatenate([kh, kh], axis=1), NT) + mm(qh, kl, NT)
                pr = (sc * sigmoid(sc)).reshape(hpg, tok, step) * allow[None]
                ph, plo = split(pr.reshape(hpg * tok, step))
                o = mm(ph, jnp.concatenate([vh, vl], axis=1))
                o = (o[:, :128] + o[:, 128:]) + mm(plo, vh)
                got = att[m, :, lanes]
                for h in range(hpg):
                    got = got + jnp.where(lane_head == h, o[h * tok:(h + 1) * tok], 0.0)
                att[m, :, lanes] = got
            return 0

        lax.fori_loop(0, 2, heads, 0)

    ev.pair(0)
    attend(pc.y)
    ev.near()
    neg.start_z()
    ev.far()
    ev.pair(1)
    attend(ev.ring.left)
    neg.start_gather()
    ev.pair(2)
    attend(ev.ring.opp)
    neg.rings_start()

    a = jnp.concatenate([att[0], att[1]], axis=1)
    centered = a - jnp.mean(a, axis=1, keepdims=True)
    var = jnp.mean(centered * centered, axis=1, keepdims=True)
    normed = centered * lax.rsqrt(var + epsilon) * gain_ref[...]
    gated = normed * jnp.concatenate([gates[0], gates[1]], axis=1)
    c_wo.wait()
    o_own = x_own + mm3(split(gated), split(wo[...]))
    pad = out_all.shape[1] - tok
    out_all[pc.s, :tok, :] = o_own
    out_all[pc.s, tok:, :] = jnp.zeros((pad, D), f32)
    out_all[pc.s, tok:tok + 1, :tok] = tgt_ref[...].astype(f32)
    out_all[pc.s, tok:tok + 1, tok:step] = jnp.broadcast_to(msk_ref[...], (1, tok)).astype(f32)
    out.start()
    neg.rings_forward()
    neg.b_start()
    out.forward()
    neg.a_wait()
    neg.forward(neg.bx)
    out.near()
    neg.near(neg.bx, neg.push_b)
    neg.far(neg.bx, neg.push_b)

    m0 = split(neg_all[0, pc.y, pc.c].reshape(share, half))
    m1 = split(neg_all[1, pc.y, pc.c].reshape(share, half))
    column = pc.s * share + lax.broadcasted_iota(jnp.int32, (share, step), 0)
    panel[...] = jnp.zeros_like(panel)
    loss_acc[...] = jnp.zeros_like(loss_acc)

    def own_columns(y):
        pair = [out_all[2 * y], out_all[2 * y + 1]]
        ob = jnp.concatenate([q[:tok] for q in pair], axis=0)
        tg = jnp.concatenate([q[tok:tok + 1, :tok] for q in pair], axis=1).astype(jnp.int32)
        mk = jnp.concatenate([q[tok:tok + 1, tok:step] for q in pair], axis=1).astype(jnp.int32)
        obh, obl = split(ob)
        logits = mm3(m0, (obh[:, :half], obl[:, :half]), NT)
        logits = logits + mm3(m1, (obh[:, half:], obl[:, half:]), NT)
        bits = jnp.right_shift(jnp.broadcast_to(mk, column.shape), column // 128) & 1
        g, wt, sp = loss_core(logits, column == jnp.broadcast_to(tg, column.shape), bits.astype(f32))
        loss_acc[...] += wt * sp
        panel[...] += mm3(split(g), (obh, obl)).reshape(panel.shape)

    out.pair(0)
    own_columns(pc.y)
    out.pair(1)
    own_columns(out.ring.left)
    out.far()
    neg.a_start()
    out.pair(2)
    own_columns(out.ring.right)
    out.pair(3)
    own_columns(out.ring.opp)
    loss.t0[...] = jnp.broadcast_to(jnp.sum(loss_acc[...]), loss.t0.shape)
    pan.start_x()
    loss.start_x()

    neg.forward(neg.ay)
    neg.near(neg.ay, neg.push_a)
    neg.far(neg.ay, neg.push_a)
    mine = out_all[pc.s]
    oh = [split(mine[:tok, k * half:(k + 1) * half]) for k in (0, 1)]
    tcol = jnp.transpose(jnp.broadcast_to(mine[tok:tok + 1, :tok], (tok, tok)))
    tcol = jnp.concatenate([tcol, tcol], axis=1).astype(jnp.int32)
    mcol = jnp.broadcast_to(mine[tok:tok + 1, tok:tok + 1], (tok, step)).astype(jnp.int32)
    acc[...] = jnp.zeros_like(acc)

    def own_tokens(j, _):
        n0 = split(neg_all[0, j // 2, j % 2].reshape(share, half))
        n1 = split(neg_all[1, j // 2, j % 2].reshape(share, half))
        logits = mm3(oh[0], n0, NT) + mm3(oh[1], n1, NT)
        live = (jnp.right_shift(mcol, 2 * j + lane // 128) & 1).astype(f32)
        g, _, _ = loss_core(logits, lane + j * share == tcol, live)
        gs = split(g)
        acc[0] += mm3(gs, n0)
        acc[1] += mm3(gs, n1)
        return 0

    pan.start_z()
    loss.start_z()
    neg.wait_core()
    lax.fori_loop(0, 3, own_tokens, 0)
    pan.start_gather()
    loss.start_s()
    lax.fori_loop(3, 7, own_tokens, 0)
    pan.rings_start()
    lax.fori_loop(7, 8, own_tokens, 0)
    grad_ref[0, :, :half] = acc[0]
    grad_ref[0, :, half:] = acc[1]
    pan.rings_forward()
    pan.a_wait()
    pan.a_start()
    pan.b_start()
    pan.forward(pan.ay)
    pan.forward(pan.bx)
    pan.near(pan.ay, pan.push_a)
    pan.near(pan.bx, pan.push_b)
    total_ref[...] = loss.total()
    pan.far(pan.ay, pan.push_a)
    pan.far(pan.bx, pan.push_b)
    pan.wait_core()
    for q in (ev, out, neg, pan, loss):
        q.wait_sends()


def scatter_kernel(n_item, scale, panel_all, neg_ref, owner_ref, total_ref, table_ref, loss_ref, buf, sem):
    item = lax.axis_index("item")
    rows = table_ref.shape[0]
    panel = neg_ref.shape[1]
    half = buf.shape[2]
    table_ref[...] = jnp.zeros_like(table_ref)
    loss_ref[...] = total_ref[...] * scale
    for p in range(neg_ref.shape[0]):

        @pl.when(owner_ref[p] == item)
        def _():
            copy = pltpu.make_async_copy(panel_all.at[:, pl.ds(p * panel, panel), :], buf, sem)
            copy.start()
            spot = lax.broadcasted_iota(jnp.int32, (rows, panel), 0)
            pick = jnp.where(spot == neg_ref[pl.ds(p, 1), :], 1.0, 0.0).astype(bf16)
            copy.wait()
            for k in (0, 1):
                hi, lo = split(buf[k])
                table_ref[:, k * half:(k + 1) * half] += mm(pick, hi) + mm(pick, lo)


def params(cid=None):
    if cid is None:
        return pltpu.CompilerParams(vmem_limit_bytes=VMEM_LIMIT)
    return pltpu.CompilerParams(
        vmem_limit_bytes=VMEM_LIMIT, collective_id=cid, has_side_effects=True
    )


def per_device(
    n_seq, n_item, events, w_uvqk, out_gain, w_out, item_table,
    user_lengths, neg_ids, panel_owner, block_mask, targets,
):
    _, tok, D = events.shape
    X, Z, Y = X_RING, n_item // X_RING, n_seq // 2
    n_neg = neg_ids.shape[0] * neg_ids.shape[1]
    share = n_neg // n_seq
    R = share // n_item
    half = D // 2
    shape = jax.ShapeDtypeStruct

    aug = tok + 16
    step = 2 * tok
    full = (2, Y, 2, X, Z * R, half)
    one = pltpu.SemaphoreType.DMA
    event_grad, panel_all, total = pl.pallas_call(
        functools.partial(main_kernel, n_seq, n_item),
        out_shape=(shape(events.shape, f32), shape(full, f32), shape((8, 128), f32)),
        in_specs=[ANY, ANY, VM, ANY, ANY, VM, VM, VM, VM, VM], out_specs=(VM, ANY, VM),
        scratch_shapes=[
            pltpu.VMEM((n_seq, tok, D), f32), pltpu.VMEM(full, f32),
            pltpu.VMEM((n_seq, aug, D), f32), pltpu.VMEM(item_table.shape, f32),
            pltpu.VMEM(w_uvqk.shape, f32), pltpu.VMEM(w_out.shape, f32),
            pltpu.VMEM((8, D, half), bf16), pltpu.VMEM((8, D, half), bf16),
            pltpu.VMEM((4, step, half), bf16), pltpu.VMEM((4, step, half), bf16),
            pltpu.VMEM((2, tok, half), f32), pltpu.VMEM((2, tok, half), f32),
            pltpu.VMEM((2, tok, half), f32),
            pltpu.VMEM((X, Z, R, D), f32), pltpu.VMEM((X, Z, R, D), f32),
            pltpu.VMEM((2, tok, half), f32), pltpu.VMEM((share, step), f32),
            one, one, one, one,
        ] + SEQ_SEMS * 2 + reduce_scratch(X, Z, R, D) * 2 + loss_scratch(X, Z, n_seq),
        compiler_params=params(1), name="main",
    )(events, w_uvqk, out_gain.reshape(1, D), w_out, item_table, user_lengths, neg_ids,
      panel_owner.reshape(-1, 1), block_mask, targets)

    scale = 1.0 / (tok * n_seq * n_item)
    table_grad, mean_loss = pl.pallas_call(
        functools.partial(scatter_kernel, n_item, scale),
        out_shape=(shape(item_table.shape, f32), shape((8, 128), f32)),
        in_specs=[ANY, VM, SM, VM], out_specs=(VM, VM),
        scratch_shapes=[pltpu.VMEM((2, neg_ids.shape[1], half), f32), pltpu.SemaphoreType.DMA],
        compiler_params=params(), name="scatter",
    )(panel_all.reshape(2, n_neg, half), neg_ids, panel_owner, total)
    return (mean_loss[0, 0], event_grad, table_grad)


def solution(mesh):
    placed = (
        P("item", "seq", None), P(), P(), P(), P("item", None), P("item", None),
        P(), P(), P("item", "seq"), P("item", "seq"),
    )
    body = functools.partial(per_device, mesh.shape["seq"], mesh.shape["item"])
    return jax.shard_map(
        body, mesh=mesh, in_specs=placed,
        out_specs=(P(), P("item", "seq", None), P("item", None)), check_vma=False,
    )
```

```python
import functools

import jax
import jax.numpy as jnp
from jax import lax
from jax.experimental import pallas as pl
from jax.experimental.pallas import tpu as pltpu
from jax.sharding import PartitionSpec as P

H = 16
X_RING = 4
beta_weight = 0.75
epsilon = 1e-05
f32, bf16 = jnp.float32, jnp.bfloat16
MESH = pl.DeviceIdType.MESH
VMEM_LIMIT = 60 * 1024 * 1024

VM = pl.BlockSpec(memory_space=pltpu.VMEM)
SM = pl.BlockSpec(memory_space=pltpu.SMEM)
ANY = pl.BlockSpec(memory_space=pl.ANY)
NN = (((1,), (0,)), ((), ()))
NT = (((1,), (1,)), ((), ()))
TN = (((0,), (0,)), ((), ()))


def split(x):
    hi = x.astype(bf16)
    return hi, (x - hi.astype(f32)).astype(bf16)


def mm(a, b, dims=NN):
    return lax.dot_general(a, b, dims, preferred_element_type=f32)


def mm3(a, b, dims=NN):
    (ah, al), (bh, bl) = a, b
    return mm(ah, bh, dims) + (mm(al, bh, dims) + mm(ah, bl, dims))


def sigmoid(x):
    return 0.5 + 0.5 * jnp.tanh(0.5 * x)


class Place:
    def __init__(self, n_seq, n_item):
        self.S, self.I = n_seq, n_item
        self.X = X_RING
        self.Z = n_item // self.X
        self.Y = n_seq // 2
        self.s = lax.axis_index("seq")
        self.i = lax.axis_index("item")
        self.y, self.c = self.s // 2, self.s % 2
        self.z, self.x = self.i // self.X, self.i % self.X

    def at_x(self, x):
        return (self.s, self.z * self.X + x)

    def at_z(self, z):
        return (self.s, z * self.X + self.x)

    def at_y(self, y):
        return (2 * y + self.c, self.i)

    def at_s(self, s):
        return (s, self.i)

    def partner(self):
        return (2 * self.y + 1 - self.c, self.i)


def rdma(src, dst, send, recv, dev):
    return pltpu.make_async_remote_copy(
        src_ref=src, dst_ref=dst, send_sem=send, recv_sem=recv, device_id=dev, device_id_type=MESH
    )


class Ring4:
    def __init__(self, me, dev, part, send, recv, causal=False):
        self.me, self.dev, self.part, self.causal = me, dev, part, causal
        self.send, self.recv = send, recv
        self.right, self.left = (me + 1) % 4, (me + 3) % 4
        self.opp = (me + 2) % 4

    def _c(self, slot, src, k, h, to):
        return rdma(src, self.part(k, h), self.send.at[slot], self.recv.at[slot], self.dev(to))

    def start(self):
        me = self.me
        self.r = [self._c(h, self.part(me, h), me, h, self.right) for h in (0, 1)]
        self.l1 = self._c(3, self.part(me, 1), me, 1, self.left)
        self.r[0].start()
        self.l1.start()
        self.r[1].start()
        self.l = [self.l1]
        if not self.causal:
            self.l.append(self._c(2, self.part(me, 0), me, 0, self.left))
            self.l[1].start()

    def forward_right(self):
        self.r[0].wait_recv()
        self.fr = self._c(4, self.part(self.left, 0), self.left, 0, self.right)
        self.fr.start()

    def forward_left(self):
        self.l1.wait_recv()
        self.fl = self._c(5, self.part(self.right, 1), self.right, 1, self.left)
        self.fl.start()

    def forward(self):
        self.forward_right()
        self.forward_left()

    def wait_left(self):
        self.r[1].wait_recv()

    def wait_right(self):
        self.l[1].wait_recv()

    def wait_opp(self):
        self.fr.wait_recv()
        self.fl.wait_recv()

    def wait_sends(self):
        for c in (*self.r, *self.l, self.fr, self.fl):
            c.wait_send()


class CoreSends:
    def __init__(self, dev, send, recv):
        self.dev, self.send, self.recv, self.copies = dev, send, recv, []

    def push(self, src, dst):
        n = len(self.copies)
        c = rdma(src, dst, self.send.at[n], self.recv.at[n], self.dev)
        c.start()
        self.copies.append(c)

    def wait_recv(self, n):
        self.copies[n].wait_recv()

    def wait_sends(self):
        for c in self.copies:
            c.wait_send()


def enter(devs):
    barrier = pltpu.get_barrier_semaphore()
    for d in devs:
        pl.semaphore_signal(barrier, inc=1, device_id=d, device_id_type=MESH)
    return lambda: pl.semaphore_wait(barrier, len(devs))


def seq_peers(pc):
    return [pc.at_s((pc.s + d) % pc.S) for d in range(1, pc.S)]


def plane_peers(pc):
    xs = [pc.at_x((pc.x + d) % pc.X) for d in range(1, pc.X)]
    zs = [pc.at_z((pc.z + d) % pc.Z) for d in range(1, pc.Z)]
    return xs + zs


class SeqGather:
    def __init__(self, pc, full, sems, causal=False):
        send, recv, csend, crecv = sems
        half = full.shape[1] // 2
        self.pc, self.full, self.causal = pc, full, causal
        part = lambda y, h: full.at[2 * y + pc.c, pl.ds(h * half, half)]
        self.ring = Ring4(pc.y, pc.at_y, part, send, recv, causal)
        self.core = CoreSends(pc.partner(), csend, crecv)

    def push(self, y):
        blk = self.full.at[2 * y + self.pc.c]
        self.core.push(blk, blk)

    def start(self):
        self.ring.start()
        self.push(self.pc.y)

    def forward(self):
        self.ring.forward()

    def near(self):
        r = self.ring
        r.wait_left()
        self.push(r.left)
        if not self.causal:
            r.wait_right()
            self.push(r.right)

    def far(self):
        self.ring.wait_opp()
        self.push(self.ring.opp)

    def pair(self, n):
        self.core.wait_recv(n)

    def wait_sends(self):
        self.ring.wait_sends()
        self.core.wait_sends()


def dma(n):
    return pltpu.SemaphoreType.DMA((n,))


SEQ_SEMS = [dma(6), dma(6), dma(4), dma(4)]


class Reduce:
    def __init__(self, pc, part, full, refs):
        self.pc, self.part, self.full = pc, part, full
        (self.rx, self.mid, self.sx, self.rz, self.own, self.xs, self.xr,
         self.zs, self.zr, self.gs, self.gr, self.lsem) = refs
        self.hz = part.shape[1] // 2
        self.right, self.left = (pc.x + 1) % 4, (pc.x + 3) % 4
        self.opp = (pc.x + 2) % 4

    def _half(self, k, h):
        return self.part.at[k, pl.ds(h * self.hz, self.hz)]

    def _x(self, slot, src, to):
        c = rdma(src, self.rx.at[slot], self.xs.at[slot], self.xr.at[slot], self.pc.at_x(to))
        c.start()
        self.cx.append(c)

    def start_x(self):
        self.cx = []
        self._x(0, self._half(self.opp, 0), self.right)
        self._x(1, self._half(self.opp, 1), self.left)
        self._x(2, self._half(self.right, 1), self.right)
        self._x(3, self._half(self.left, 0), self.left)

    def pass_x(self):
        h = self.hz
        self.cx[0].wait_recv()
        self.mid[0] = self.part[self.right, :h] + self.rx[0]
        self._x(4, self.mid.at[0], self.right)
        self.cx[1].wait_recv()
        self.mid[1] = self.part[self.left, h:] + self.rx[1]
        self._x(5, self.mid.at[1], self.left)

    def start_z(self):
        pc, h = self.pc, self.hz
        for c in self.cx[2:]:
            c.wait_recv()
        self.sx[:h] = self.part[pc.x, :h] + (self.rx[4] + self.rx[3])
        self.sx[h:] = self.part[pc.x, h:] + (self.rx[2] + self.rx[5])
        self.cz = []
        for d in range(1, pc.Z):
            to = (pc.z + d) % pc.Z
            c = rdma(self.sx.at[to], self.rz.at[d - 1], self.zs.at[d - 1], self.zr.at[d - 1], pc.at_z(to))
            c.start()
            self.cz.append(c)

    def start_gather(self):
        pc = self.pc
        total = self.sx[pc.z]
        for c in self.cz:
            c.wait_recv()
        for d in range(pc.Z - 1):
            total = total + self.rz[d]
        half = total.shape[1] // 2
        rows = total.shape[0]
        self.own[0] = total[:, :half]
        self.own[1] = total[:, half:]
        mine = self.full.at[:, pc.y, pc.c, pc.x, pl.ds(pl.multiple_of(pc.z * rows, rows), rows), :]
        self.local = pltpu.make_async_copy(self.own, mine, self.lsem)
        self.local.start()
        self.cg = []
        for d in range(1, pc.Z):
            to = (pc.z + d) % pc.Z
            c = rdma(self.own, mine, self.gs.at[d - 1], self.gr.at[d - 1], pc.at_z(to))
            c.start()
            self.cg.append(c)

    def wait_z(self):
        for c in self.cg:
            c.wait_recv()
        self.local.wait()

    def wait_sends(self):
        for c in (*self.cx, *self.cz, *self.cg):
            c.wait_send()


def reduce_scratch(X, Z, R, D):
    nz = max(Z - 1, 1)
    return [
        pltpu.VMEM((6, Z // 2, R, D), f32),
        pltpu.VMEM((2, Z // 2, R, D), f32),
        pltpu.VMEM((Z, R, D), f32),
        pltpu.VMEM((nz, R, D), f32),
        pltpu.VMEM((2, R, D // 2), f32),
        dma(6), dma(6), dma(nz), dma(nz), dma(nz), dma(nz), pltpu.SemaphoreType.DMA,
    ]


N_REDUCE = 12


class SpreadXY:
    def __init__(self, pc, full, sems):
        xs, xr, ys, yr, cs, cr = sems
        self.pc, self.full = pc, full
        self.rx = Ring4(pc.x, pc.at_x, lambda k, h: full.at[h, pc.y, pc.c, k], xs, xr)
        self.ry = Ring4(pc.y, pc.at_y, lambda k, h: full.at[h, k, pc.c], ys, yr)
        self.core = CoreSends(pc.partner(), cs, cr)

    def push(self, k):
        blk = self.full.at[:, k, self.pc.c]
        self.core.push(blk, blk)

    def x_wait(self):
        self.rx.wait_left()
        self.rx.wait_right()
        self.rx.wait_opp()

    def y_start(self):
        self.ry.start()

    def near(self):
        self.ry.wait_left()
        self.push(self.ry.left)
        self.ry.wait_right()
        self.push(self.ry.right)

    def far(self):
        self.ry.wait_opp()
        self.push(self.ry.opp)

    def wait_sends(self):
        for q in (self.rx, self.ry, self.core):
            q.wait_sends()


SPREAD_XY_SEMS = [dma(6), dma(6), dma(6), dma(6), dma(4), dma(4)]


class Lane:
    def __init__(self, pc, first, second, blk, sems):
        (f, fdev), (g, gdev) = first, second
        self.f, self.g, self.blk = f, g, blk
        rows = blk(0, 0).shape[0] // 2
        part = lambda ref, h: ref.at[pl.ds(h * rows, rows), :]
        self.one = Ring4(f, fdev, lambda k, h: part(blk(k, g), h), sems[0], sems[1])
        self.two = []
        for n, k in enumerate((f, (f + 3) % 4, (f + 1) % 4, (f + 2) % 4)):
            ring = Ring4(
                g, gdev, lambda j, h, k=k: part(blk(k, j), h), sems[2 + 2 * n], sems[3 + 2 * n]
            )
            ring.piece = k
            self.two.append(ring)
        self.core = CoreSends(pc.partner(), sems[10], sems[11])

    def push(self, k, j):
        self.core.push(self.blk(k, j), self.blk(k, j))

    def begin(self, n):
        ring = self.two[n]
        ring.start()
        self.push(ring.piece, self.g)

    def near(self, n):
        ring = self.two[n]
        ring.wait_left()
        self.push(ring.piece, ring.left)
        ring.wait_right()
        self.push(ring.piece, ring.right)

    def far(self, n):
        ring = self.two[n]
        ring.wait_opp()
        self.push(ring.piece, ring.opp)

    def steps(self):
        one, two = self.one, self.two
        return [
            lambda: (one.start(), self.begin(0)),
            lambda: one.forward(),
            lambda: (one.wait_left(), self.begin(1)),
            lambda: (one.wait_right(), self.begin(2)),
            lambda: two[0].forward(),
            lambda: (one.wait_opp(), self.begin(3)),
            lambda: two[1].forward(),
            lambda: two[2].forward(),
            lambda: self.near(0),
            lambda: two[3].forward(),
            lambda: self.near(1),
            lambda: self.near(2),
            lambda: self.far(0),
            lambda: self.near(3),
            lambda: self.far(1),
            lambda: self.far(2),
            lambda: self.far(3),
        ]

    def wait_core(self):
        for n in range(16):
            self.core.wait_recv(n)

    def wait_sends(self):
        for q in (self.one, *self.two, self.core):
            q.wait_sends()


LANE_SEMS = [dma(6)] * 10 + [dma(16)] * 2


class LossSum:
    def __init__(self, pc, refs):
        self.pc = pc
        (self.t0, self.lx, self.tx, self.lz, self.tz, self.ls,
         self.xs, self.xr, self.zs, self.zr, self.ss, self.sr) = refs
        self.all = []

    def _send(self, src, dst, send, recv, devs):
        out = []
        for d, dev in enumerate(devs):
            c = rdma(src, dst.at[d], send.at[d], recv.at[d], dev)
            c.start()
            out.append(c)
        self.all += out
        return out

    def start_x(self):
        pc = self.pc
        devs = [pc.at_x((pc.x + d) % pc.X) for d in range(1, pc.X)]
        self.c = self._send(self.t0, self.lx, self.xs, self.xr, devs)

    def _sum(self, own, got, n):
        for c in self.c:
            c.wait_recv()
        total = own[...]
        for d in range(n):
            total = total + got[d]
        return total

    def start_z(self):
        pc = self.pc
        self.tx[...] = self._sum(self.t0, self.lx, pc.X - 1)
        devs = [pc.at_z((pc.z + d) % pc.Z) for d in range(1, pc.Z)]
        self.c = self._send(self.tx, self.lz, self.zs, self.zr, devs)

    def start_s(self):
        pc = self.pc
        self.tz[...] = self._sum(self.tx, self.lz, pc.Z - 1)
        self.c = self._send(self.tz, self.ls, self.ss, self.sr, seq_peers(pc))

    def total(self):
        return self._sum(self.tz, self.ls, self.pc.S - 1)

    def wait_sends(self):
        for c in self.all:
            c.wait_send()


def loss_scratch(X, Z, S):
    nz = max(Z - 1, 1)
    tile = lambda *n: pltpu.VMEM((*n, 8, 128), f32)
    return [
        tile(), tile(X - 1), tile(), tile(nz), tile(), tile(S - 1),
        dma(X - 1), dma(X - 1), dma(nz), dma(nz), dma(S - 1), dma(S - 1),
    ]


N_LOSS = 12


def loss_core(logits, target, live):
    m = jnp.where(target, -logits, logits)
    w = jnp.where(target, -beta_weight, live)
    e = jnp.exp(-jnp.abs(m))
    sig = jnp.where(m >= 0.0, 1.0, e) / (1.0 + e)
    return w * sig, jnp.abs(w), jnp.maximum(m, 0.0) + jnp.log1p(e)


def main_kernel(
    n_seq, n_item, ev_ref, w_ref, gain_ref, wo_ref, table_ref, lens_ref, neg_ref, owner_ref,
    msk_ref, tgt_ref, grad_ref, panel_all, total_ref, *scratch,
):
    pc = Place(n_seq, n_item)
    (ev_all, neg_all, out_all, table, w, wo, wh, wl, kvh, kvl, qs, gates, att, part, panel,
     acc, loss_acc, s_ev, s_table, s_w, s_wo) = scratch[:21]
    rest = scratch[21:]
    ev = SeqGather(pc, ev_all, rest[:4], causal=True)
    out = SeqGather(pc, out_all, rest[4:8])
    rest = rest[8:]
    neg = Reduce(pc, part, neg_all, rest[:N_REDUCE])
    pan = Reduce(pc, panel, panel_all, rest[N_REDUCE:2 * N_REDUCE])
    rest = rest[2 * N_REDUCE:]
    spread = SpreadXY(pc, neg_all, rest[:6])
    along_x, along_y = (pc.x, pc.at_x), (pc.y, pc.at_y)
    lane_a = Lane(pc, along_x, along_y, lambda k, j: panel_all.at[0, j, pc.c, k], rest[6:18])
    lane_b = Lane(pc, along_y, along_x, lambda k, j: panel_all.at[1, k, pc.c, j], rest[18:30])
    loss = LossSum(pc, rest[30:])

    tok, D = grad_ref.shape[1], grad_ref.shape[2]
    half = D // 2
    step = 2 * tok
    rows = table.shape[0]
    X, Z, R = part.shape[0], part.shape[1], part.shape[2]
    share = X * Z * R
    hd = D // H
    hpg = 128 // hd

    ready = enter(plane_peers(pc) + seq_peers(pc))
    c_ev = pltpu.make_async_copy(ev_ref.at[0], ev_all.at[pc.s], s_ev)
    c_table = pltpu.make_async_copy(table_ref, table, s_table)
    c_w = pltpu.make_async_copy(w_ref, w, s_w)
    c_wo = pltpu.make_async_copy(wo_ref, wo, s_wo)
    for c in (c_ev, c_table, c_w, c_wo):
        c.start()

    per_panel = neg_ref.shape[1] // share
    p = pc.s // per_panel
    first = pl.multiple_of((pc.s % per_panel) * share, share)
    slot = lax.broadcasted_iota(jnp.int32, owner_ref.shape, 1)
    owner = jnp.sum(jnp.where(slot == p, owner_ref[...], 0), axis=1, keepdims=True)
    ids = neg_ref[pl.ds(p, 1), pl.ds(first, share)] + rows * jnp.broadcast_to(owner, (1, share))
    spot = pc.i * rows + lax.broadcasted_iota(jnp.int32, (rows, share), 0)
    pick = jnp.where(spot == jnp.broadcast_to(ids, spot.shape), 1.0, 0.0).astype(bf16)
    c_table.wait()
    hi, lo = split(table[...])
    part[...] = (mm(pick, hi, TN) + mm(pick, lo, TN)).reshape(part.shape)
    c_ev.wait()
    ready()
    ev.start()
    neg.start_x()

    c_w.wait()

    def split_w(n, _):
        wh[n], wl[n] = split(w[:, pl.ds(pl.multiple_of(n * half, half), half)])
        return 0

    lax.fori_loop(0, 8, split_w, 0)
    x_own = ev_all[pc.s]
    xo = split(x_own)

    def project(xs, n):
        r = mm3(xs, (wh[n], wl[n]))
        return r * sigmoid(r)

    for n in range(2):
        qs[n] = project(xo, 4 + n)
        gates[n] = project(xo, n)
    att[...] = jnp.zeros_like(att)
    neg.pass_x()
    ev.forward()

    lane_head = lax.broadcasted_iota(jnp.int32, (tok, 128), 1) // hd
    row = pc.s * tok + lax.broadcasted_iota(jnp.int32, (tok, step), 0)
    lane = lax.broadcasted_iota(jnp.int32, (tok, step), 1)
    begin = jnp.zeros((tok, step), jnp.int32)
    end = jnp.zeros((1, 1), jnp.int32)
    for u in range(lens_ref.shape[1]):
        end = end + lens_ref[0:1, u:u + 1]
        wide = jnp.broadcast_to(end, row.shape)
        begin = jnp.where(row >= wide, wide, begin)

    def attend(y):
        xs = split(jnp.concatenate([ev_all[2 * y], ev_all[2 * y + 1]], axis=0))

        def kv_step(n, _):
            kvh[n], kvl[n] = split(project(xs, jnp.where(n < 2, 2 + n, 4 + n)))
            return 0

        lax.fori_loop(0, 4, kv_step, 0)
        col = y * step + lane
        allow = jnp.where((col >= begin) & (col <= row), 1.0, 0.0)

        def heads(m, _):
            for g in range(half // 128):
                lanes = slice(g * 128, (g + 1) * 128)
                kh, kl = kvh[2 + m][:, lanes], kvl[2 + m][:, lanes]
                vh, vl = kvh[m][:, lanes], kvl[m][:, lanes]
                q = qs[m][:, lanes]
                stack = [jnp.where(lane_head == h, q, 0.0) for h in range(hpg)]
                qh, ql = split(jnp.concatenate(stack, axis=0))
                two = jnp.concatenate([qh, ql], axis=1)
                sc = mm(two, jnp.concatenate([kh, kh], axis=1), NT) + mm(qh, kl, NT)
                pr = (sc * sigmoid(sc)).reshape(hpg, tok, step) * allow[None]
                ph, plo = split(pr.reshape(hpg * tok, step))
                o = mm(ph, jnp.concatenate([vh, vl], axis=1))
                o = (o[:, :128] + o[:, 128:]) + mm(plo, vh)
                got = att[m, :, lanes]
                for h in range(hpg):
                    got = got + jnp.where(lane_head == h, o[h * tok:(h + 1) * tok], 0.0)
                att[m, :, lanes] = got
            return 0

        lax.fori_loop(0, 2, heads, 0)

    ev.pair(0)
    attend(pc.y)
    ev.near()
    neg.start_z()
    ev.far()
    ev.pair(1)
    attend(ev.ring.left)
    neg.start_gather()
    ev.pair(2)
    attend(ev.ring.opp)
    neg.wait_z()
    spread.rx.start()

    a = jnp.concatenate([att[0], att[1]], axis=1)
    centered = a - jnp.mean(a, axis=1, keepdims=True)
    var = jnp.mean(centered * centered, axis=1, keepdims=True)
    normed = centered * lax.rsqrt(var + epsilon) * gain_ref[...]
    gated = normed * jnp.concatenate([gates[0], gates[1]], axis=1)
    c_wo.wait()
    o_own = x_own + mm3(split(gated), split(wo[...]))
    pad = out_all.shape[1] - tok
    out_all[pc.s, :tok, :] = o_own
    out_all[pc.s, tok:, :] = jnp.zeros((pad, D), f32)
    out_all[pc.s, tok:tok + 1, :tok] = tgt_ref[...].astype(f32)
    out_all[pc.s, tok:tok + 1, tok:step] = jnp.broadcast_to(msk_ref[...], (1, tok)).astype(f32)
    out.start()
    spread.rx.forward()
    out.forward()
    spread.x_wait()
    spread.push(pc.y)

    m0 = split(neg_all[0, pc.y, pc.c].reshape(share, half))
    m1 = split(neg_all[1, pc.y, pc.c].reshape(share, half))
    column = pc.s * share + lax.broadcasted_iota(jnp.int32, (share, step), 0)
    panel[...] = jnp.zeros_like(panel)
    loss_acc[...] = jnp.zeros_like(loss_acc)

    def own_columns(y):
        pair = [out_all[2 * y], out_all[2 * y + 1]]
        ob = jnp.concatenate([q[:tok] for q in pair], axis=0)
        tg = jnp.concatenate([q[tok:tok + 1, :tok] for q in pair], axis=1).astype(jnp.int32)
        mk = jnp.concatenate([q[tok:tok + 1, tok:step] for q in pair], axis=1).astype(jnp.int32)
        obh, obl = split(ob)
        logits = mm3(m0, (obh[:, :half], obl[:, :half]), NT)
        logits = logits + mm3(m1, (obh[:, half:], obl[:, half:]), NT)
        bits = jnp.right_shift(jnp.broadcast_to(mk, column.shape), column // 128) & 1
        g, wt, sp = loss_core(logits, column == jnp.broadcast_to(tg, column.shape), bits.astype(f32))
        loss_acc[...] += wt * sp
        panel[...] += mm3(split(g), (obh, obl)).reshape(panel.shape)

    out.pair(0)
    own_columns(pc.y)
    out.near()
    out.pair(1)
    own_columns(out.ring.left)
    out.far()
    spread.y_start()
    out.pair(2)
    own_columns(out.ring.right)
    out.pair(3)
    own_columns(out.ring.opp)
    pan.start_x()
    loss.t0[...] = jnp.broadcast_to(jnp.sum(loss_acc[...]), loss.t0.shape)
    loss.start_x()

    mine = out_all[pc.s]
    oh = [split(mine[:tok, k * half:(k + 1) * half]) for k in (0, 1)]
    tcol = jnp.transpose(jnp.broadcast_to(mine[tok:tok + 1, :tok], (tok, tok)))
    tcol = jnp.concatenate([tcol, tcol], axis=1).astype(jnp.int32)
    mcol = jnp.broadcast_to(mine[tok:tok + 1, tok:tok + 1], (tok, step)).astype(jnp.int32)
    acc[...] = jnp.zeros_like(acc)

    def own_tokens(j):
        n0 = split(neg_all[0, j // 2, j % 2].reshape(share, half))
        n1 = split(neg_all[1, j // 2, j % 2].reshape(share, half))
        logits = mm3(oh[0], n0, NT) + mm3(oh[1], n1, NT)
        live = (jnp.right_shift(mcol, 2 * j + lane // 128) & 1).astype(f32)
        g, _, _ = loss_core(logits, lane + j * share == tcol, live)
        gs = split(g)
        acc[0] += mm3(gs, n0)
        acc[1] += mm3(gs, n1)

    def own_pair(n, y):
        def one(c, _):
            own_tokens(2 * y + c)
            return 0

        spread.core.wait_recv(n)
        lax.fori_loop(0, 2, one, 0)

    own_pair(0, pc.y)
    pan.pass_x()
    spread.ry.forward()
    pan.start_z()
    loss.start_z()
    spread.near()
    own_pair(1, spread.ry.left)
    pan.start_gather()
    loss.start_s()
    own_pair(2, spread.ry.right)
    pan.wait_z()
    steps = list(zip(lane_a.steps(), lane_b.steps()))
    for n, pair in enumerate(steps):
        for step_of in pair:
            step_of()
        if n == 0:
            spread.far()
            own_pair(3, spread.ry.opp)
            grad_ref[0, :, :half] = acc[0]
            grad_ref[0, :, half:] = acc[1]
    total_ref[...] = loss.total()
    lane_a.wait_core()
    lane_b.wait_core()
    for q in (ev, out, neg, pan, spread, lane_a, lane_b, loss):
        q.wait_sends()


def scatter_kernel(n_item, scale, panel_all, neg_ref, owner_ref, total_ref, table_ref, loss_ref, buf, sem):
    item = lax.axis_index("item")
    rows = table_ref.shape[0]
    panel = neg_ref.shape[1]
    half = buf.shape[2]
    table_ref[...] = jnp.zeros_like(table_ref)
    loss_ref[0, 0] = jnp.max(total_ref[...]) * scale
    for p in range(neg_ref.shape[0]):

        @pl.when(owner_ref[p] == item)
        def _():
            copy = pltpu.make_async_copy(panel_all.at[:, pl.ds(p * panel, panel), :], buf, sem)
            copy.start()
            spot = lax.broadcasted_iota(jnp.int32, (rows, panel), 0)
            pick = jnp.where(spot == neg_ref[pl.ds(p, 1), :], 1.0, 0.0).astype(bf16)
            copy.wait()
            for k in (0, 1):
                hi, lo = split(buf[k])
                table_ref[:, k * half:(k + 1) * half] += mm(pick, hi) + mm(pick, lo)


def params(cid=None):
    if cid is None:
        return pltpu.CompilerParams(vmem_limit_bytes=VMEM_LIMIT)
    return pltpu.CompilerParams(
        vmem_limit_bytes=VMEM_LIMIT, collective_id=cid, has_side_effects=True
    )


def per_device(
    n_seq, n_item, events, w_uvqk, out_gain, w_out, item_table,
    user_lengths, neg_ids, panel_owner, block_mask, targets,
):
    _, tok, D = events.shape
    X, Z, Y = X_RING, n_item // X_RING, n_seq // 2
    n_neg = neg_ids.shape[0] * neg_ids.shape[1]
    share = n_neg // n_seq
    R = share // n_item
    half = D // 2
    shape = jax.ShapeDtypeStruct

    aug = tok + 16
    step = 2 * tok
    full = (2, Y, 2, X, Z * R, half)
    one = pltpu.SemaphoreType.DMA
    event_grad, panel_all, total = pl.pallas_call(
        functools.partial(main_kernel, n_seq, n_item),
        out_shape=(shape(events.shape, f32), shape(full, f32), shape((8, 128), f32)),
        in_specs=[ANY, ANY, VM, ANY, ANY, VM, VM, VM, VM, VM], out_specs=(VM, ANY, VM),
        scratch_shapes=[
            pltpu.VMEM((n_seq, tok, D), f32), pltpu.VMEM(full, f32),
            pltpu.VMEM((n_seq, aug, D), f32), pltpu.VMEM(item_table.shape, f32),
            pltpu.VMEM(w_uvqk.shape, f32), pltpu.VMEM(w_out.shape, f32),
            pltpu.VMEM((8, D, half), bf16), pltpu.VMEM((8, D, half), bf16),
            pltpu.VMEM((4, step, half), bf16), pltpu.VMEM((4, step, half), bf16),
            pltpu.VMEM((2, tok, half), f32), pltpu.VMEM((2, tok, half), f32),
            pltpu.VMEM((2, tok, half), f32),
            pltpu.VMEM((X, Z, R, D), f32), pltpu.VMEM((X, Z, R, D), f32),
            pltpu.VMEM((2, tok, half), f32), pltpu.VMEM((share, step), f32),
            one, one, one, one,
        ] + SEQ_SEMS * 2 + reduce_scratch(X, Z, R, D) * 2 + SPREAD_XY_SEMS + LANE_SEMS * 2 + loss_scratch(X, Z, n_seq),
        compiler_params=params(1), name="main",
    )(events, w_uvqk, out_gain.reshape(1, D), w_out, item_table, user_lengths, neg_ids,
      panel_owner.reshape(1, -1), block_mask, targets)

    scale = 1.0 / (tok * n_seq * n_item)
    table_grad, mean_loss = pl.pallas_call(
        functools.partial(scatter_kernel, n_item, scale),
        out_shape=(shape(item_table.shape, f32), shape((1, 1), f32)),
        in_specs=[ANY, VM, SM, VM], out_specs=(VM, SM),
        scratch_shapes=[pltpu.VMEM((2, neg_ids.shape[1], half), f32), pltpu.SemaphoreType.DMA],
        compiler_params=params(), name="scatter",
    )(panel_all.reshape(2, n_neg, half), neg_ids, panel_owner, total)
    return (mean_loss.reshape(()), event_grad, table_grad)


def solution(mesh):
    placed = (
        P("item", "seq", None), P(), P(), P(), P("item", None), P("item", None),
        P(), P(), P("item", "seq"), P("item", "seq"),
    )
    body = functools.partial(per_device, mesh.shape["seq"], mesh.shape["item"])
    return jax.shard_map(
        body, mesh=mesh, in_specs=placed,
        out_specs=(P(), P("item", "seq", None), P("item", None)), check_vma=False,
    )
```

```python
import functools

import jax
import jax.numpy as jnp
from jax import lax
from jax.experimental import pallas as pl
from jax.experimental.pallas import tpu as pltpu
from jax.sharding import PartitionSpec as P

H = 16
X_RING = 4
beta_weight = 0.75
epsilon = 1e-05
f32, bf16 = jnp.float32, jnp.bfloat16
MESH = pl.DeviceIdType.MESH
VMEM_LIMIT = 60 * 1024 * 1024

VM = pl.BlockSpec(memory_space=pltpu.VMEM)
SM = pl.BlockSpec(memory_space=pltpu.SMEM)
ANY = pl.BlockSpec(memory_space=pl.ANY)
NN = (((1,), (0,)), ((), ()))
NT = (((1,), (1,)), ((), ()))


def split(x):
    hi = x.astype(bf16)
    return hi, (x - hi.astype(f32)).astype(bf16)


def mm(a, b, dims=NN):
    return lax.dot_general(a, b, dims, preferred_element_type=f32)


def mm3(a, b, dims=NN):
    (ah, al), (bh, bl) = a, b
    return mm(ah, bh, dims) + (mm(al, bh, dims) + mm(ah, bl, dims))


def sigmoid(x):
    return 0.5 + 0.5 * jnp.tanh(0.5 * x)


class Place:
    def __init__(self, n_seq, n_item):
        self.S, self.I = n_seq, n_item
        self.X = X_RING
        self.Z = n_item // self.X
        self.Y = n_seq // 2
        self.s = lax.axis_index("seq")
        self.i = lax.axis_index("item")
        self.y, self.c = self.s // 2, self.s % 2
        self.z, self.x = self.i // self.X, self.i % self.X

    def at_x(self, x):
        return (self.s, self.z * self.X + x)

    def at_z(self, z):
        return (self.s, z * self.X + self.x)

    def at_y(self, y):
        return (2 * y + self.c, self.i)

    def at_s(self, s):
        return (s, self.i)

    def partner(self):
        return (2 * self.y + 1 - self.c, self.i)


def rdma(src, dst, send, recv, dev):
    return pltpu.make_async_remote_copy(
        src_ref=src, dst_ref=dst, send_sem=send, recv_sem=recv, device_id=dev, device_id_type=MESH
    )


class Ring4:
    def __init__(self, me, dev, part, send, recv, causal=False):
        self.me, self.dev, self.part, self.causal = me, dev, part, causal
        self.send, self.recv = send, recv
        self.right, self.left = (me + 1) % 4, (me + 3) % 4
        self.opp = (me + 2) % 4

    def _c(self, slot, src, k, h, to):
        return rdma(src, self.part(k, h), self.send.at[slot], self.recv.at[slot], self.dev(to))

    def start(self):
        me = self.me
        self.r = [self._c(h, self.part(me, h), me, h, self.right) for h in (0, 1)]
        self.l1 = self._c(3, self.part(me, 1), me, 1, self.left)
        self.r[0].start()
        self.l1.start()
        self.r[1].start()
        self.l = [self.l1]
        if not self.causal:
            self.l.append(self._c(2, self.part(me, 0), me, 0, self.left))
            self.l[1].start()

    def forward_right(self):
        self.r[0].wait_recv()
        self.fr = self._c(4, self.part(self.left, 0), self.left, 0, self.right)
        self.fr.start()

    def forward_left(self):
        self.l1.wait_recv()
        self.fl = self._c(5, self.part(self.right, 1), self.right, 1, self.left)
        self.fl.start()

    def forward(self):
        self.forward_right()
        self.forward_left()

    def wait_left(self):
        self.r[1].wait_recv()

    def wait_right(self):
        self.l[1].wait_recv()

    def wait_opp(self):
        self.fr.wait_recv()
        self.fl.wait_recv()

    def wait_sends(self):
        for c in (*self.r, *self.l, self.fr, self.fl):
            c.wait_send()


class CoreSends:
    def __init__(self, dev, send, recv):
        self.dev, self.send, self.recv, self.copies = dev, send, recv, []

    def push(self, src, dst):
        n = len(self.copies)
        c = rdma(src, dst, self.send.at[n], self.recv.at[n], self.dev)
        c.start()
        self.copies.append(c)

    def wait_recv(self, n):
        self.copies[n].wait_recv()

    def wait_sends(self):
        for c in self.copies:
            c.wait_send()


def enter(devs):
    barrier = pltpu.get_barrier_semaphore()
    for d in devs:
        pl.semaphore_signal(barrier, inc=1, device_id=d, device_id_type=MESH)
    return lambda: pl.semaphore_wait(barrier, len(devs))


def seq_peers(pc):
    return [pc.at_s((pc.s + d) % pc.S) for d in range(1, pc.S)]


def plane_peers(pc):
    xs = [pc.at_x((pc.x + d) % pc.X) for d in range(1, pc.X)]
    zs = [pc.at_z((pc.z + d) % pc.Z) for d in range(1, pc.Z)]
    return xs + zs


class SeqGather:
    def __init__(self, pc, full, sems, causal=False):
        send, recv, csend, crecv = sems
        half = full.shape[1] // 2
        self.pc, self.full, self.causal = pc, full, causal
        part = lambda y, h: full.at[2 * y + pc.c, pl.ds(h * half, half)]
        self.ring = Ring4(pc.y, pc.at_y, part, send, recv, causal)
        self.core = CoreSends(pc.partner(), csend, crecv)

    def push(self, y):
        blk = self.full.at[2 * y + self.pc.c]
        self.core.push(blk, blk)

    def start(self):
        self.ring.start()
        self.push(self.pc.y)

    def forward(self):
        self.ring.forward()

    def near(self):
        r = self.ring
        r.wait_left()
        self.push(r.left)
        if not self.causal:
            r.wait_right()
            self.push(r.right)

    def far(self):
        self.ring.wait_opp()
        self.push(self.ring.opp)

    def pair(self, n):
        self.core.wait_recv(n)

    def wait_sends(self):
        self.ring.wait_sends()
        self.core.wait_sends()


def dma(n):
    return pltpu.SemaphoreType.DMA((n,))


SEQ_SEMS = [dma(6), dma(6), dma(4), dma(4)]


class Reduce:
    def __init__(self, pc, part, full, refs):
        self.pc, self.part, self.full = pc, part, full
        (self.rx, self.mid, self.sx, self.rz, self.own, self.xs, self.xr,
         self.zs, self.zr, self.gs, self.gr, self.lsem) = refs
        self.hz = part.shape[1] // 2
        self.right, self.left = (pc.x + 1) % 4, (pc.x + 3) % 4
        self.opp = (pc.x + 2) % 4

    def _half(self, k, h):
        return self.part.at[k, pl.ds(h * self.hz, self.hz)]

    def _x(self, slot, src, to):
        c = rdma(src, self.rx.at[slot], self.xs.at[slot], self.xr.at[slot], self.pc.at_x(to))
        c.start()
        self.cx.append(c)

    def start_x(self):
        self.cx = []
        self._x(0, self._half(self.opp, 0), self.right)
        self._x(1, self._half(self.opp, 1), self.left)
        self._x(2, self._half(self.right, 1), self.right)
        self._x(3, self._half(self.left, 0), self.left)

    def pass_x(self):
        h = self.hz
        self.cx[0].wait_recv()
        self.mid[0] = self.part[self.right, :h] + self.rx[0]
        self._x(4, self.mid.at[0], self.right)
        self.cx[1].wait_recv()
        self.mid[1] = self.part[self.left, h:] + self.rx[1]
        self._x(5, self.mid.at[1], self.left)

    def start_z(self):
        pc, h = self.pc, self.hz
        for c in self.cx[2:]:
            c.wait_recv()
        self.sx[:h] = self.part[pc.x, :h] + (self.rx[4] + self.rx[3])
        self.sx[h:] = self.part[pc.x, h:] + (self.rx[2] + self.rx[5])
        self.cz = []
        for d in range(1, pc.Z):
            to = (pc.z + d) % pc.Z
            c = rdma(self.sx.at[to], self.rz.at[d - 1], self.zs.at[d - 1], self.zr.at[d - 1], pc.at_z(to))
            c.start()
            self.cz.append(c)

    def start_gather(self):
        pc = self.pc
        total = self.sx[pc.z]
        for c in self.cz:
            c.wait_recv()
        for d in range(pc.Z - 1):
            total = total + self.rz[d]
        half = total.shape[1] // 2
        rows = total.shape[0]
        self.own[0] = total[:, :half]
        self.own[1] = total[:, half:]
        mine = self.full.at[:, pc.y, pc.c, pc.x, pl.ds(pl.multiple_of(pc.z * rows, rows), rows), :]
        self.local = pltpu.make_async_copy(self.own, mine, self.lsem)
        self.local.start()
        self.cg = []
        for d in range(1, pc.Z):
            to = (pc.z + d) % pc.Z
            c = rdma(self.own, mine, self.gs.at[d - 1], self.gr.at[d - 1], pc.at_z(to))
            c.start()
            self.cg.append(c)

    def wait_z(self):
        for c in self.cg:
            c.wait_recv()
        self.local.wait()

    def wait_sends(self):
        for c in (*self.cx, *self.cz, *self.cg):
            c.wait_send()


def reduce_scratch(X, Z, R, D):
    nz = max(Z - 1, 1)
    return [
        pltpu.VMEM((6, Z // 2, R, D), f32),
        pltpu.VMEM((2, Z // 2, R, D), f32),
        pltpu.VMEM((Z, R, D), f32),
        pltpu.VMEM((nz, R, D), f32),
        pltpu.VMEM((2, R, D // 2), f32),
        dma(6), dma(6), dma(nz), dma(nz), dma(nz), dma(nz), pltpu.SemaphoreType.DMA,
    ]


N_REDUCE = 12


class SpreadXY:
    def __init__(self, pc, full, sems):
        xs, xr, ys, yr, cs, cr = sems
        self.pc, self.full = pc, full
        self.rx = Ring4(pc.x, pc.at_x, lambda k, h: full.at[h, pc.y, pc.c, k], xs, xr)
        self.ry = Ring4(pc.y, pc.at_y, lambda k, h: full.at[h, k, pc.c], ys, yr)
        self.core = CoreSends(pc.partner(), cs, cr)

    def push(self, k):
        blk = self.full.at[:, k, self.pc.c]
        self.core.push(blk, blk)

    def x_wait(self):
        self.rx.wait_left()
        self.rx.wait_right()
        self.rx.wait_opp()

    def y_start(self):
        self.ry.start()

    def near(self):
        self.ry.wait_left()
        self.push(self.ry.left)
        self.ry.wait_right()
        self.push(self.ry.right)

    def far(self):
        self.ry.wait_opp()
        self.push(self.ry.opp)

    def wait_sends(self):
        for q in (self.rx, self.ry, self.core):
            q.wait_sends()


SPREAD_XY_SEMS = [dma(6), dma(6), dma(6), dma(6), dma(4), dma(4)]


class Lane:
    def __init__(self, pc, first, second, blk, sems):
        (f, fdev), (g, gdev) = first, second
        self.f, self.g, self.blk = f, g, blk
        rows = blk(0, 0).shape[0] // 2
        part = lambda ref, h: ref.at[pl.ds(h * rows, rows), :]
        self.one = Ring4(f, fdev, lambda k, h: part(blk(k, g), h), sems[0], sems[1])
        self.two = []
        for n, k in enumerate((f, (f + 3) % 4, (f + 1) % 4, (f + 2) % 4)):
            ring = Ring4(
                g, gdev, lambda j, h, k=k: part(blk(k, j), h), sems[2 + 2 * n], sems[3 + 2 * n]
            )
            ring.piece = k
            self.two.append(ring)
        self.core = CoreSends(pc.partner(), sems[10], sems[11])

    def push(self, k, j):
        self.core.push(self.blk(k, j), self.blk(k, j))

    def begin(self, n):
        ring = self.two[n]
        ring.start()
        self.push(ring.piece, self.g)

    def near(self, n):
        ring = self.two[n]
        ring.wait_left()
        self.push(ring.piece, ring.left)
        ring.wait_right()
        self.push(ring.piece, ring.right)

    def far(self, n):
        ring = self.two[n]
        ring.wait_opp()
        self.push(ring.piece, ring.opp)

    def steps(self):
        one, two = self.one, self.two
        return [
            lambda: (one.start(), self.begin(0)),
            lambda: one.forward(),
            lambda: (one.wait_left(), self.begin(1)),
            lambda: (one.wait_right(), self.begin(2)),
            lambda: two[0].forward(),
            lambda: (one.wait_opp(), self.begin(3)),
            lambda: two[1].forward(),
            lambda: two[2].forward(),
            lambda: self.near(0),
            lambda: two[3].forward(),
            lambda: self.near(1),
            lambda: self.near(2),
            lambda: self.far(0),
            lambda: self.near(3),
            lambda: self.far(1),
            lambda: self.far(2),
            lambda: self.far(3),
        ]

    def wait_core(self):
        for n in range(16):
            self.core.wait_recv(n)

    def wait_sends(self):
        for q in (self.one, *self.two, self.core):
            q.wait_sends()


LANE_SEMS = [dma(6)] * 10 + [dma(16)] * 2


class LossSum:
    def __init__(self, pc, refs):
        self.pc = pc
        (self.t0, self.lx, self.tx, self.lz, self.tz, self.ls,
         self.xs, self.xr, self.zs, self.zr, self.ss, self.sr) = refs
        self.all = []

    def _send(self, src, dst, send, recv, devs):
        out = []
        for d, dev in enumerate(devs):
            c = rdma(src, dst.at[d], send.at[d], recv.at[d], dev)
            c.start()
            out.append(c)
        self.all += out
        return out

    def start_x(self):
        pc = self.pc
        devs = [pc.at_x((pc.x + d) % pc.X) for d in range(1, pc.X)]
        self.c = self._send(self.t0, self.lx, self.xs, self.xr, devs)

    def _sum(self, own, got, n):
        for c in self.c:
            c.wait_recv()
        total = own[...]
        for d in range(n):
            total = total + got[d]
        return total

    def start_z(self):
        pc = self.pc
        self.tx[...] = self._sum(self.t0, self.lx, pc.X - 1)
        devs = [pc.at_z((pc.z + d) % pc.Z) for d in range(1, pc.Z)]
        self.c = self._send(self.tx, self.lz, self.zs, self.zr, devs)

    def start_s(self):
        pc = self.pc
        self.tz[...] = self._sum(self.tx, self.lz, pc.Z - 1)
        self.c = self._send(self.tz, self.ls, self.ss, self.sr, seq_peers(pc))

    def total(self):
        return self._sum(self.tz, self.ls, self.pc.S - 1)

    def wait_sends(self):
        for c in self.all:
            c.wait_send()


def loss_scratch(X, Z, S):
    nz = max(Z - 1, 1)
    tile = lambda *n: pltpu.VMEM((*n, 8, 128), f32)
    return [
        tile(), tile(X - 1), tile(), tile(nz), tile(), tile(S - 1),
        dma(X - 1), dma(X - 1), dma(nz), dma(nz), dma(S - 1), dma(S - 1),
    ]


N_LOSS = 12


def loss_core(logits, target, live):
    m = jnp.where(target, -logits, logits)
    w = jnp.where(target, -beta_weight, live)
    e = jnp.exp(-jnp.abs(m))
    sig = jnp.where(m >= 0.0, 1.0, e) / (1.0 + e)
    return w * sig, jnp.abs(w), jnp.maximum(m, 0.0) + jnp.log1p(e)


def main_kernel(
    n_seq, n_item, ev_ref, w_ref, gain_ref, wo_ref, table_ref, lens_ref, neg_ref, owner_ref,
    msk_ref, tgt_ref, grad_ref, panel_all, total_ref, *scratch,
):
    pc = Place(n_seq, n_item)
    (ev_all, neg_all, out_all, table, w, wo, wh, wl, kvh, kvl, qs, gates, att, part, panel,
     acc, loss_acc, s_ev, s_table, s_w, s_wo) = scratch[:21]
    rest = scratch[21:]
    ev = SeqGather(pc, ev_all, rest[:4], causal=True)
    out = SeqGather(pc, out_all, rest[4:8])
    rest = rest[8:]
    neg = Reduce(pc, part, neg_all, rest[:N_REDUCE])
    pan = Reduce(pc, panel, panel_all, rest[N_REDUCE:2 * N_REDUCE])
    rest = rest[2 * N_REDUCE:]
    spread = SpreadXY(pc, neg_all, rest[:6])
    along_x, along_y = (pc.x, pc.at_x), (pc.y, pc.at_y)
    lane_a = Lane(pc, along_x, along_y, lambda k, j: panel_all.at[0, j, pc.c, k], rest[6:18])
    lane_b = Lane(pc, along_y, along_x, lambda k, j: panel_all.at[1, k, pc.c, j], rest[18:30])
    loss = LossSum(pc, rest[30:])

    tok, D = grad_ref.shape[1], grad_ref.shape[2]
    half = D // 2
    step = 2 * tok
    rows = table.shape[0]
    X, Z, R = part.shape[0], part.shape[1], part.shape[2]
    share = X * Z * R
    hd = D // H
    hpg = 128 // hd

    ready = enter(plane_peers(pc) + seq_peers(pc))
    c_ev = pltpu.make_async_copy(ev_ref.at[0], ev_all.at[pc.s], s_ev)
    c_table = pltpu.make_async_copy(table_ref, table, s_table)
    c_w = pltpu.make_async_copy(w_ref, w, s_w)
    c_wo = pltpu.make_async_copy(wo_ref, wo, s_wo)
    for c in (c_ev, c_table, c_w, c_wo):
        c.start()

    c_ev.wait()
    ready()
    ev.start()

    per_panel = neg_ref.shape[1] // share
    p = pc.s // per_panel
    first = pl.multiple_of((pc.s % per_panel) * share, share)
    slot = lax.broadcasted_iota(jnp.int32, owner_ref.shape, 1)
    owner = jnp.sum(jnp.where(slot == p, owner_ref[...], 0), axis=1, keepdims=True)
    ids = neg_ref[pl.ds(p, 1), pl.ds(first, share)] + rows * jnp.broadcast_to(owner, (1, share))
    ids = jnp.transpose(jnp.broadcast_to(ids - pc.i * rows, (128, share)).astype(f32))
    spot = lax.broadcasted_iota(jnp.int32, (share, 128), 1).astype(f32)
    picks = [jnp.where(ids == spot + float(k), 1.0, 0.0).astype(bf16) for k in range(0, rows, 128)]
    pick = jnp.concatenate(picks, axis=1)
    c_table.wait()
    hi, lo = split(table[...])
    part[...] = (mm(pick, hi) + mm(pick, lo)).reshape(part.shape)
    neg.start_x()

    c_w.wait()

    def split_w(n, _):
        wh[n], wl[n] = split(w[:, pl.ds(pl.multiple_of(n * half, half), half)])
        return 0

    lax.fori_loop(0, 8, split_w, 0)
    x_own = ev_all[pc.s]
    xo = split(x_own)

    def project(xs, n):
        r = mm3(xs, (wh[n], wl[n]))
        return r * sigmoid(r)

    for n in range(2):
        qs[n] = project(xo, 4 + n)
        gates[n] = project(xo, n)
    att[...] = jnp.zeros_like(att)
    neg.pass_x()
    ev.forward()

    lane_head = lax.broadcasted_iota(jnp.int32, (tok, 128), 1) // hd
    row = pc.s * tok + lax.broadcasted_iota(jnp.int32, (tok, step), 0)
    lane = lax.broadcasted_iota(jnp.int32, (tok, step), 1)
    begin = jnp.zeros((tok, step), jnp.int32)
    end = jnp.zeros((1, 1), jnp.int32)
    for u in range(lens_ref.shape[1]):
        end = end + lens_ref[0:1, u:u + 1]
        wide = jnp.broadcast_to(end, row.shape)
        begin = jnp.where(row >= wide, wide, begin)

    def attend(y):
        xs = split(jnp.concatenate([ev_all[2 * y], ev_all[2 * y + 1]], axis=0))

        def kv_step(n, _):
            kvh[n], kvl[n] = split(project(xs, jnp.where(n < 2, 2 + n, 4 + n)))
            return 0

        lax.fori_loop(0, 4, kv_step, 0)
        col = y * step + lane
        allow = jnp.where((col >= begin) & (col <= row), 1.0, 0.0)

        def heads(m, _):
            for g in range(half // 128):
                lanes = slice(g * 128, (g + 1) * 128)
                kh, kl = kvh[2 + m][:, lanes], kvl[2 + m][:, lanes]
                vh, vl = kvh[m][:, lanes], kvl[m][:, lanes]
                q = qs[m][:, lanes]
                stack = [jnp.where(lane_head == h, q, 0.0) for h in range(hpg)]
                qh, ql = split(jnp.concatenate(stack, axis=0))
                two = jnp.concatenate([qh, ql], axis=1)
                sc = mm(two, jnp.concatenate([kh, kh], axis=1), NT) + mm(qh, kl, NT)
                pr = (sc * sigmoid(sc)).reshape(hpg, tok, step) * allow[None]
                ph, plo = split(pr.reshape(hpg * tok, step))
                o = mm(ph, jnp.concatenate([vh, vl], axis=1))
                o = (o[:, :128] + o[:, 128:]) + mm(plo, vh)
                got = att[m, :, lanes]
                for h in range(hpg):
                    got = got + jnp.where(lane_head == h, o[h * tok:(h + 1) * tok], 0.0)
                att[m, :, lanes] = got
            return 0

        lax.fori_loop(0, 2, heads, 0)

    ev.pair(0)
    attend(pc.y)
    ev.near()
    neg.start_z()
    ev.far()
    ev.pair(1)
    attend(ev.ring.left)
    neg.start_gather()
    ev.pair(2)
    attend(ev.ring.opp)
    neg.wait_z()
    spread.rx.start()

    a = jnp.concatenate([att[0], att[1]], axis=1)
    centered = a - jnp.mean(a, axis=1, keepdims=True)
    var = jnp.mean(centered * centered, axis=1, keepdims=True)
    normed = centered * lax.rsqrt(var + epsilon) * gain_ref[...]
    gated = normed * jnp.concatenate([gates[0], gates[1]], axis=1)
    c_wo.wait()
    o_own = x_own + mm3(split(gated), split(wo[...]))
    pad = out_all.shape[1] - tok
    out_all[pc.s, :tok, :] = o_own
    out_all[pc.s, tok:, :] = jnp.zeros((pad, D), f32)
    out_all[pc.s, tok:tok + 1, :tok] = tgt_ref[...].astype(f32)
    out_all[pc.s, tok:tok + 1, tok:step] = jnp.broadcast_to(msk_ref[...], (1, tok)).astype(f32)
    out.start()
    spread.rx.forward()
    out.forward()
    spread.x_wait()
    spread.push(pc.y)

    m0 = split(neg_all[0, pc.y, pc.c].reshape(share, half))
    m1 = split(neg_all[1, pc.y, pc.c].reshape(share, half))
    column = pc.s * share + lax.broadcasted_iota(jnp.int32, (share, step), 0)
    panel[...] = jnp.zeros_like(panel)
    loss_acc[...] = jnp.zeros_like(loss_acc)

    def own_columns(y):
        pair = [out_all[2 * y], out_all[2 * y + 1]]
        ob = jnp.concatenate([q[:tok] for q in pair], axis=0)
        tg = jnp.concatenate([q[tok:tok + 1, :tok] for q in pair], axis=1).astype(jnp.int32)
        mk = jnp.concatenate([q[tok:tok + 1, tok:step] for q in pair], axis=1).astype(jnp.int32)
        obh, obl = split(ob)
        logits = mm3(m0, (obh[:, :half], obl[:, :half]), NT)
        logits = logits + mm3(m1, (obh[:, half:], obl[:, half:]), NT)
        bits = jnp.right_shift(jnp.broadcast_to(mk, column.shape), column // 128) & 1
        g, wt, sp = loss_core(logits, column == jnp.broadcast_to(tg, column.shape), bits.astype(f32))
        loss_acc[...] += wt * sp
        panel[...] += mm3(split(g), (obh, obl)).reshape(panel.shape)

    out.pair(0)
    own_columns(pc.y)
    out.near()
    out.pair(1)
    own_columns(out.ring.left)
    out.pair(2)
    own_columns(out.ring.right)
    out.far()
    spread.y_start()
    out.pair(3)
    own_columns(out.ring.opp)
    pan.start_x()
    loss.t0[...] = jnp.broadcast_to(jnp.sum(loss_acc[...]), loss.t0.shape)
    loss.start_x()

    mine = out_all[pc.s]
    oh = [split(mine[:tok, k * half:(k + 1) * half]) for k in (0, 1)]
    tcol = jnp.transpose(jnp.broadcast_to(mine[tok:tok + 1, :tok], (tok, tok)))
    tcol = jnp.concatenate([tcol, tcol], axis=1).astype(jnp.int32)
    mcol = jnp.broadcast_to(mine[tok:tok + 1, tok:tok + 1], (tok, step)).astype(jnp.int32)
    acc[...] = jnp.zeros_like(acc)

    def own_tokens(j):
        n0 = split(neg_all[0, j // 2, j % 2].reshape(share, half))
        n1 = split(neg_all[1, j // 2, j % 2].reshape(share, half))
        logits = mm3(oh[0], n0, NT) + mm3(oh[1], n1, NT)
        live = (jnp.right_shift(mcol, 2 * j + lane // 128) & 1).astype(f32)
        g, _, _ = loss_core(logits, lane + j * share == tcol, live)
        gs = split(g)
        acc[0] += mm3(gs, n0)
        acc[1] += mm3(gs, n1)

    def own_pair(n, y):
        def one(c, _):
            own_tokens(2 * y + c)
            return 0

        spread.core.wait_recv(n)
        lax.fori_loop(0, 2, one, 0)

    own_pair(0, pc.y)
    pan.pass_x()
    spread.ry.forward()
    pan.start_z()
    loss.start_z()
    spread.near()
    own_pair(1, spread.ry.left)
    pan.start_gather()
    loss.start_s()
    own_pair(2, spread.ry.right)
    pan.wait_z()
    steps = list(zip(lane_a.steps(), lane_b.steps()))
    for n, pair in enumerate(steps):
        for step_of in pair:
            step_of()
        if n == 9:
            spread.far()
            own_pair(3, spread.ry.opp)
            grad_ref[0, :, :half] = acc[0]
            grad_ref[0, :, half:] = acc[1]
    total_ref[...] = loss.total()
    lane_a.wait_core()
    lane_b.wait_core()
    for q in (ev, out, neg, pan, spread, lane_a, lane_b, loss):
        q.wait_sends()


def scatter_kernel(n_item, scale, panel_all, neg_ref, owner_ref, total_ref, table_ref, loss_ref, buf, sem):
    item = lax.axis_index("item")
    rows = table_ref.shape[0]
    panel = neg_ref.shape[1]
    half = buf.shape[2]
    table_ref[...] = jnp.zeros_like(table_ref)
    loss_ref[0, 0] = jnp.max(total_ref[...]) * scale
    for p in range(neg_ref.shape[0]):

        @pl.when(owner_ref[p] == item)
        def _():
            copy = pltpu.make_async_copy(panel_all.at[:, pl.ds(p * panel, panel), :], buf, sem)
            copy.start()
            spot = lax.broadcasted_iota(jnp.int32, (rows, panel), 0)
            pick = jnp.where(spot == neg_ref[pl.ds(p, 1), :], 1.0, 0.0).astype(bf16)
            copy.wait()
            for k in (0, 1):
                hi, lo = split(buf[k])
                table_ref[:, k * half:(k + 1) * half] += mm(pick, hi) + mm(pick, lo)


def params(cid=None):
    if cid is None:
        return pltpu.CompilerParams(vmem_limit_bytes=VMEM_LIMIT)
    return pltpu.CompilerParams(
        vmem_limit_bytes=VMEM_LIMIT, collective_id=cid, has_side_effects=True
    )


def per_device(
    n_seq, n_item, events, w_uvqk, out_gain, w_out, item_table,
    user_lengths, neg_ids, panel_owner, block_mask, targets,
):
    _, tok, D = events.shape
    X, Z, Y = X_RING, n_item // X_RING, n_seq // 2
    n_neg = neg_ids.shape[0] * neg_ids.shape[1]
    share = n_neg // n_seq
    R = share // n_item
    half = D // 2
    shape = jax.ShapeDtypeStruct

    aug = tok + 16
    step = 2 * tok
    full = (2, Y, 2, X, Z * R, half)
    one = pltpu.SemaphoreType.DMA
    event_grad, panel_all, total = pl.pallas_call(
        functools.partial(main_kernel, n_seq, n_item),
        out_shape=(shape(events.shape, f32), shape(full, f32), shape((8, 128), f32)),
        in_specs=[ANY, ANY, VM, ANY, ANY, VM, VM, VM, VM, VM], out_specs=(VM, ANY, VM),
        scratch_shapes=[
            pltpu.VMEM((n_seq, tok, D), f32), pltpu.VMEM(full, f32),
            pltpu.VMEM((n_seq, aug, D), f32), pltpu.VMEM(item_table.shape, f32),
            pltpu.VMEM(w_uvqk.shape, f32), pltpu.VMEM(w_out.shape, f32),
            pltpu.VMEM((8, D, half), bf16), pltpu.VMEM((8, D, half), bf16),
            pltpu.VMEM((4, step, half), bf16), pltpu.VMEM((4, step, half), bf16),
            pltpu.VMEM((2, tok, half), f32), pltpu.VMEM((2, tok, half), f32),
            pltpu.VMEM((2, tok, half), f32),
            pltpu.VMEM((X, Z, R, D), f32), pltpu.VMEM((X, Z, R, D), f32),
            pltpu.VMEM((2, tok, half), f32), pltpu.VMEM((share, step), f32),
            one, one, one, one,
        ] + SEQ_SEMS * 2 + reduce_scratch(X, Z, R, D) * 2 + SPREAD_XY_SEMS + LANE_SEMS * 2 + loss_scratch(X, Z, n_seq),
        compiler_params=params(1), name="main",
    )(events, w_uvqk, out_gain.reshape(1, D), w_out, item_table, user_lengths, neg_ids,
      panel_owner.reshape(1, -1), block_mask, targets)

    scale = 1.0 / (tok * n_seq * n_item)
    table_grad, mean_loss = pl.pallas_call(
        functools.partial(scatter_kernel, n_item, scale),
        out_shape=(shape(item_table.shape, f32), shape((1, 1), f32)),
        in_specs=[ANY, VM, SM, VM], out_specs=(VM, SM),
        scratch_shapes=[pltpu.VMEM((2, neg_ids.shape[1], half), f32), pltpu.SemaphoreType.DMA],
        compiler_params=params(), name="scatter",
    )(panel_all.reshape(2, n_neg, half), neg_ids, panel_owner, total)
    return (mean_loss.reshape(()), event_grad, table_grad)


def solution(mesh):
    placed = (
        P("item", "seq", None), P(), P(), P(), P("item", None), P("item", None),
        P(), P(), P("item", "seq"), P("item", "seq"),
    )
    body = functools.partial(per_device, mesh.shape["seq"], mesh.shape["item"])
    return jax.shard_map(
        body, mesh=mesh, in_specs=placed,
        out_specs=(P(), P("item", "seq", None), P("item", None)), check_vma=False,
    )
```

```python
import functools

import jax
import jax.numpy as jnp
from jax import lax
from jax.experimental import pallas as pl
from jax.experimental.pallas import tpu as pltpu
from jax.sharding import PartitionSpec as P

H = 16
X_RING = 4
beta_weight = 0.75
epsilon = 1e-05
f32, bf16 = jnp.float32, jnp.bfloat16
MESH = pl.DeviceIdType.MESH
VMEM_LIMIT = 60 * 1024 * 1024

VM = pl.BlockSpec(memory_space=pltpu.VMEM)
SM = pl.BlockSpec(memory_space=pltpu.SMEM)
ANY = pl.BlockSpec(memory_space=pl.ANY)
NN = (((1,), (0,)), ((), ()))
NT = (((1,), (1,)), ((), ()))


def split(x):
    hi = x.astype(bf16)
    return hi, (x - hi.astype(f32)).astype(bf16)


def mm(a, b, dims=NN):
    return lax.dot_general(a, b, dims, preferred_element_type=f32)


def mm3(a, b, dims=NN):
    (ah, al), (bh, bl) = a, b
    return mm(ah, bh, dims) + (mm(al, bh, dims) + mm(ah, bl, dims))


def sigmoid(x):
    return 0.5 + 0.5 * jnp.tanh(0.5 * x)


class Place:
    def __init__(self, n_seq, n_item):
        self.S, self.I = n_seq, n_item
        self.X = X_RING
        self.Z = n_item // self.X
        self.Y = n_seq // 2
        self.s = lax.axis_index("seq")
        self.i = lax.axis_index("item")
        self.y, self.c = self.s // 2, self.s % 2
        self.z, self.x = self.i // self.X, self.i % self.X

    def at_x(self, x):
        return (self.s, self.z * self.X + x)

    def at_z(self, z):
        return (self.s, z * self.X + self.x)

    def at_y(self, y):
        return (2 * y + self.c, self.i)

    def at_s(self, s):
        return (s, self.i)

    def partner(self):
        return (2 * self.y + 1 - self.c, self.i)


def rdma(src, dst, send, recv, dev):
    return pltpu.make_async_remote_copy(
        src_ref=src, dst_ref=dst, send_sem=send, recv_sem=recv, device_id=dev, device_id_type=MESH
    )


class Ring4:
    def __init__(self, me, dev, part, send, recv, causal=False):
        self.me, self.dev, self.part, self.causal = me, dev, part, causal
        self.send, self.recv = send, recv
        self.right, self.left = (me + 1) % 4, (me + 3) % 4
        self.opp = (me + 2) % 4

    def _c(self, slot, src, k, h, to):
        return rdma(src, self.part(k, h), self.send.at[slot], self.recv.at[slot], self.dev(to))

    def start(self):
        me = self.me
        self.r = [self._c(h, self.part(me, h), me, h, self.right) for h in (0, 1)]
        self.l1 = self._c(3, self.part(me, 1), me, 1, self.left)
        self.r[0].start()
        self.l1.start()
        self.r[1].start()
        self.l = [self.l1]
        if not self.causal:
            self.l.append(self._c(2, self.part(me, 0), me, 0, self.left))
            self.l[1].start()

    def forward_right(self):
        self.r[0].wait_recv()
        self.fr = self._c(4, self.part(self.left, 0), self.left, 0, self.right)
        self.fr.start()

    def forward_left(self):
        self.l1.wait_recv()
        self.fl = self._c(5, self.part(self.right, 1), self.right, 1, self.left)
        self.fl.start()

    def forward(self):
        self.forward_right()
        self.forward_left()

    def wait_left(self):
        self.r[1].wait_recv()

    def wait_right(self):
        self.l[1].wait_recv()

    def wait_opp(self):
        self.fr.wait_recv()
        self.fl.wait_recv()

    def wait_sends(self):
        for c in (*self.r, *self.l, self.fr, self.fl):
            c.wait_send()


class CoreSends:
    def __init__(self, dev, send, recv):
        self.dev, self.send, self.recv, self.copies = dev, send, recv, []

    def push(self, blk):
        n = len(self.copies)
        c = rdma(blk, blk, self.send.at[n], self.recv.at[n], self.dev)
        c.start()
        self.copies.append(c)

    def wait_recv(self, n):
        self.copies[n].wait_recv()

    def wait_sends(self):
        for c in self.copies:
            c.wait_send()


def enter(devs):
    barrier = pltpu.get_barrier_semaphore()
    for d in devs:
        pl.semaphore_signal(barrier, inc=1, device_id=d, device_id_type=MESH)
    return lambda: pl.semaphore_wait(barrier, len(devs))


def seq_peers(pc):
    return [pc.at_s((pc.s + d) % pc.S) for d in range(1, pc.S)]


def plane_peers(pc):
    xs = [pc.at_x((pc.x + d) % pc.X) for d in range(1, pc.X)]
    zs = [pc.at_z((pc.z + d) % pc.Z) for d in range(1, pc.Z)]
    return xs + zs


class SeqGather:
    def __init__(self, pc, full, sems, causal=False):
        send, recv, csend, crecv = sems
        half = full.shape[1] // 2
        self.pc, self.full, self.causal = pc, full, causal
        part = lambda y, h: full.at[2 * y + pc.c, pl.ds(h * half, half)]
        self.ring = Ring4(pc.y, pc.at_y, part, send, recv, causal)
        self.core = CoreSends(pc.partner(), csend, crecv)

    def push(self, y):
        self.core.push(self.full.at[2 * y + self.pc.c])

    def start(self):
        self.ring.start()
        self.push(self.pc.y)

    def forward(self):
        self.ring.forward()

    def near(self):
        r = self.ring
        r.wait_left()
        self.push(r.left)
        if not self.causal:
            r.wait_right()
            self.push(r.right)

    def far(self):
        self.ring.wait_opp()
        self.push(self.ring.opp)

    def pair(self, n):
        self.core.wait_recv(n)

    def wait_sends(self):
        self.ring.wait_sends()
        self.core.wait_sends()


def dma(n):
    return pltpu.SemaphoreType.DMA((n,))


SEQ_SEMS = [dma(6), dma(6), dma(4), dma(4)]


class Reduce:
    def __init__(self, pc, part, full, refs):
        self.pc, self.part, self.full = pc, part, full
        (self.rx, self.mid, self.sx, self.rz, self.own, self.xs, self.xr,
         self.zs, self.zr, self.gs, self.gr, self.lsem) = refs
        self.hz = part.shape[1] // 2
        self.right, self.left = (pc.x + 1) % 4, (pc.x + 3) % 4
        self.opp = (pc.x + 2) % 4

    def _half(self, k, h):
        return self.part.at[k, pl.ds(h * self.hz, self.hz)]

    def _x(self, slot, src, to):
        c = rdma(src, self.rx.at[slot], self.xs.at[slot], self.xr.at[slot], self.pc.at_x(to))
        c.start()
        self.cx.append(c)

    def start_x(self):
        self.cx = []
        self._x(0, self._half(self.opp, 0), self.right)
        self._x(1, self._half(self.opp, 1), self.left)
        self._x(2, self._half(self.right, 1), self.right)
        self._x(3, self._half(self.left, 0), self.left)

    def pass_x(self):
        h = self.hz
        self.cx[0].wait_recv()
        self.mid[0] = self.part[self.right, :h] + self.rx[0]
        self._x(4, self.mid.at[0], self.right)
        self.cx[1].wait_recv()
        self.mid[1] = self.part[self.left, h:] + self.rx[1]
        self._x(5, self.mid.at[1], self.left)

    def start_z(self):
        pc, h = self.pc, self.hz
        for c in self.cx[2:]:
            c.wait_recv()
        self.sx[:h] = self.part[pc.x, :h] + (self.rx[4] + self.rx[3])
        self.sx[h:] = self.part[pc.x, h:] + (self.rx[2] + self.rx[5])
        self.cz = []
        for d in range(1, pc.Z):
            to = (pc.z + d) % pc.Z
            c = rdma(self.sx.at[to], self.rz.at[d - 1], self.zs.at[d - 1], self.zr.at[d - 1], pc.at_z(to))
            c.start()
            self.cz.append(c)

    def start_gather(self):
        pc = self.pc
        total = self.sx[pc.z]
        for c in self.cz:
            c.wait_recv()
        for d in range(pc.Z - 1):
            total = total + self.rz[d]
        half = total.shape[1] // 2
        rows = total.shape[0]
        self.own[0] = total[:, :half]
        self.own[1] = total[:, half:]
        mine = self.full.at[:, pc.y, pc.c, pc.x, pl.ds(pl.multiple_of(pc.z * rows, rows), rows), :]
        self.local = pltpu.make_async_copy(self.own, mine, self.lsem)
        self.local.start()
        self.cg = []
        for d in range(1, pc.Z):
            to = (pc.z + d) % pc.Z
            c = rdma(self.own, mine, self.gs.at[d - 1], self.gr.at[d - 1], pc.at_z(to))
            c.start()
            self.cg.append(c)

    def wait_z(self):
        for c in self.cg:
            c.wait_recv()
        self.local.wait()

    def wait_sends(self):
        for c in (*self.cx, *self.cz, *self.cg):
            c.wait_send()


def reduce_scratch(X, Z, R, D):
    nz = max(Z - 1, 1)
    return [
        pltpu.VMEM((6, Z // 2, R, D), f32),
        pltpu.VMEM((2, Z // 2, R, D), f32),
        pltpu.VMEM((Z, R, D), f32),
        pltpu.VMEM((nz, R, D), f32),
        pltpu.VMEM((2, R, D // 2), f32),
        dma(6), dma(6), dma(nz), dma(nz), dma(nz), dma(nz), pltpu.SemaphoreType.DMA,
    ]


N_REDUCE = 12


class Lane:
    def __init__(self, pc, first, second, blk, sems):
        (f, fdev), (g, gdev) = first, second
        self.f, self.g, self.blk = f, g, blk
        rows = blk(0, 0).shape[0] // 2
        part = lambda ref, h: ref.at[pl.ds(h * rows, rows), :]
        self.one = Ring4(f, fdev, lambda k, h: part(blk(k, g), h), sems[0], sems[1])
        self.two = []
        for n, k in enumerate((f, (f + 3) % 4, (f + 1) % 4, (f + 2) % 4)):
            ring = Ring4(
                g, gdev, lambda j, h, k=k: part(blk(k, j), h), sems[2 + 2 * n], sems[3 + 2 * n]
            )
            ring.piece = k
            self.two.append(ring)
        self.core = CoreSends(pc.partner(), sems[10], sems[11])
        self.at = {}

    def push(self, n, to):
        self.at[n, to] = len(self.core.copies)
        self.core.push(self.blk(self.two[n].piece, (self.g + to) % 4))

    def begin(self, n):
        self.two[n].start()
        self.push(n, 0)

    def near(self, n):
        ring = self.two[n]
        ring.wait_left()
        self.push(n, 3)
        ring.wait_right()
        self.push(n, 1)

    def far(self, n):
        self.two[n].wait_opp()
        self.push(n, 2)

    def arrived(self, n, to):
        self.core.wait_recv(self.at[n, to])

    def steps(self):
        one, two = self.one, self.two
        return [
            lambda: (one.start(), self.begin(0)),
            lambda: one.forward(),
            lambda: (one.wait_left(), self.begin(1)),
            lambda: (one.wait_right(), self.begin(2)),
            lambda: two[0].forward(),
            lambda: (one.wait_opp(), self.begin(3)),
            lambda: two[1].forward(),
            lambda: two[2].forward(),
            lambda: self.near(0),
            lambda: two[3].forward(),
            lambda: self.near(1),
            lambda: self.near(2),
            lambda: self.far(0),
            lambda: self.near(3),
            lambda: self.far(1),
            lambda: self.far(2),
            lambda: self.far(3),
        ]

    def wait_core(self):
        for n in range(16):
            self.core.wait_recv(n)

    def wait_sends(self):
        for q in (self.one, *self.two, self.core):
            q.wait_sends()


LANE_SEMS = [dma(6)] * 10 + [dma(16)] * 2


class LossSum:
    def __init__(self, pc, refs):
        self.pc = pc
        (self.t0, self.lx, self.tx, self.lz, self.tz, self.ls,
         self.xs, self.xr, self.zs, self.zr, self.ss, self.sr) = refs
        self.all = []

    def _send(self, src, dst, send, recv, devs):
        out = []
        for d, dev in enumerate(devs):
            c = rdma(src, dst.at[d], send.at[d], recv.at[d], dev)
            c.start()
            out.append(c)
        self.all += out
        return out

    def start_x(self):
        pc = self.pc
        devs = [pc.at_x((pc.x + d) % pc.X) for d in range(1, pc.X)]
        self.c = self._send(self.t0, self.lx, self.xs, self.xr, devs)

    def _sum(self, own, got, n):
        for c in self.c:
            c.wait_recv()
        total = own[...]
        for d in range(n):
            total = total + got[d]
        return total

    def start_z(self):
        pc = self.pc
        self.tx[...] = self._sum(self.t0, self.lx, pc.X - 1)
        devs = [pc.at_z((pc.z + d) % pc.Z) for d in range(1, pc.Z)]
        self.c = self._send(self.tx, self.lz, self.zs, self.zr, devs)

    def start_s(self):
        pc = self.pc
        self.tz[...] = self._sum(self.tx, self.lz, pc.Z - 1)
        self.c = self._send(self.tz, self.ls, self.ss, self.sr, seq_peers(pc))

    def total(self):
        return self._sum(self.tz, self.ls, self.pc.S - 1)

    def wait_sends(self):
        for c in self.all:
            c.wait_send()


def loss_scratch(X, Z, S):
    nz = max(Z - 1, 1)
    tile = lambda *n: pltpu.VMEM((*n, 8, 128), f32)
    return [
        tile(), tile(X - 1), tile(), tile(nz), tile(), tile(S - 1),
        dma(X - 1), dma(X - 1), dma(nz), dma(nz), dma(S - 1), dma(S - 1),
    ]


N_LOSS = 12


def loss_core(logits, target, live):
    m = jnp.where(target, -logits, logits)
    w = jnp.where(target, -beta_weight, live)
    e = jnp.exp(-jnp.abs(m))
    sig = jnp.where(m >= 0.0, 1.0, e) / (1.0 + e)
    return w * sig, jnp.abs(w), jnp.maximum(m, 0.0) + jnp.log1p(e)


def main_kernel(
    n_seq, n_item, ev_ref, w_ref, gain_ref, wo_ref, table_ref, lens_ref, neg_ref, owner_ref,
    msk_ref, tgt_ref, grad_ref, panel_all, total_ref, *scratch,
):
    pc = Place(n_seq, n_item)
    (ev_all, neg_all, out_all, table, w, wo, wh, wl, kvh, kvl, qs, gates, att, part, panel,
     acc, loss_acc, s_ev, s_table, s_w, s_wo) = scratch[:21]
    rest = scratch[21:]
    ev = SeqGather(pc, ev_all, rest[:4], causal=True)
    out = SeqGather(pc, out_all, rest[4:8])
    rest = rest[8:]
    neg = Reduce(pc, part, neg_all, rest[:N_REDUCE])
    pan = Reduce(pc, panel, panel_all, rest[N_REDUCE:2 * N_REDUCE])
    rest = rest[2 * N_REDUCE:]
    along_x, along_y = (pc.x, pc.at_x), (pc.y, pc.at_y)

    def lanes_of(full, sems):
        a = Lane(pc, along_x, along_y, lambda k, j: full.at[0, j, pc.c, k], sems[:12])
        b = Lane(pc, along_y, along_x, lambda k, j: full.at[1, k, pc.c, j], sems[12:])
        return a, b

    na, nb = lanes_of(neg_all, rest[:24])
    lane_a, lane_b = lanes_of(panel_all, rest[24:48])
    loss = LossSum(pc, rest[48:])

    tok, D = grad_ref.shape[1], grad_ref.shape[2]
    half = D // 2
    step = 2 * tok
    rows = table.shape[0]
    X, Z, R = part.shape[0], part.shape[1], part.shape[2]
    share = X * Z * R
    hd = D // H
    hpg = 128 // hd

    ready = enter(plane_peers(pc) + seq_peers(pc))
    c_ev = pltpu.make_async_copy(ev_ref.at[0], ev_all.at[pc.s], s_ev)
    c_table = pltpu.make_async_copy(table_ref, table, s_table)
    c_w = pltpu.make_async_copy(w_ref, w, s_w)
    c_wo = pltpu.make_async_copy(wo_ref, wo, s_wo)
    for c in (c_ev, c_table, c_w, c_wo):
        c.start()

    per_panel = neg_ref.shape[1] // share
    p = pc.s // per_panel
    first = pl.multiple_of((pc.s % per_panel) * share, share)
    slot = lax.broadcasted_iota(jnp.int32, owner_ref.shape, 1)
    owner = jnp.sum(jnp.where(slot == p, owner_ref[...], 0), axis=1, keepdims=True)
    ids = neg_ref[pl.ds(p, 1), pl.ds(first, share)] + rows * jnp.broadcast_to(owner, (1, share))
    ids = jnp.transpose(jnp.broadcast_to(ids - pc.i * rows, (128, share)).astype(f32))
    spot = lax.broadcasted_iota(jnp.int32, (share, 128), 1).astype(f32)
    picks = [jnp.where(ids == spot + float(k), 1.0, 0.0).astype(bf16) for k in range(0, rows, 128)]
    pick = jnp.concatenate(picks, axis=1)
    c_table.wait()
    hi, lo = split(table[...])
    part[...] = (mm(pick, hi) + mm(pick, lo)).reshape(part.shape)
    c_ev.wait()
    ready()
    ev.start()
    neg.start_x()

    c_w.wait()

    def split_w(n, _):
        wh[n], wl[n] = split(w[:, pl.ds(pl.multiple_of(n * half, half), half)])
        return 0

    lax.fori_loop(0, 8, split_w, 0)
    x_own = ev_all[pc.s]
    xo = split(x_own)

    def project(xs, n):
        r = mm3(xs, (wh[n], wl[n]))
        return r * sigmoid(r)

    for n in range(2):
        qs[n] = project(xo, 4 + n)
        gates[n] = project(xo, n)
    neg.pass_x()

    lane_head = lax.broadcasted_iota(jnp.int32, (tok, 128), 1) // hd
    sub = lax.broadcasted_iota(jnp.int32, (tok, tok), 0)
    lane = lax.broadcasted_iota(jnp.int32, (tok, tok), 1)
    row = pc.s * tok + sub
    begin = jnp.zeros((tok, tok), jnp.int32)
    end = jnp.zeros((1, 1), jnp.int32)
    for u in range(lens_ref.shape[1]):
        end = end + lens_ref[0:1, u:u + 1]
        wide = jnp.broadcast_to(end, row.shape)
        begin = jnp.where(row >= wide, wide, begin)

    def stacked(m, lanes):
        q = qs[m][:, lanes]
        parts = [jnp.where(lane_head == h, q, 0.0) for h in range(hpg)]
        return split(jnp.concatenate(parts, axis=0))

    def collect(m, lanes, o, base):
        got = base
        for h in range(hpg):
            got = got + jnp.where(lane_head == h, o[h * tok:(h + 1) * tok], 0.0)
        att[m, :, lanes] = got

    def weigh(sc, allow):
        pr = (sc * sigmoid(sc)).reshape(hpg, tok, sc.shape[1]) * allow[None]
        return split(pr.reshape(sc.shape))

    def keys_values(xs, n_rows):
        def kv_step(n, _):
            hi, lo = split(project(xs, jnp.where(n < 2, 2 + n, 4 + n)))
            kvh[n, :n_rows], kvl[n, :n_rows] = hi, lo
            return 0

        lax.fori_loop(0, 4, kv_step, 0)

    def attend_own():
        keys_values(xo, tok)
        allow = jnp.where((lane <= sub) & (pc.s * tok + lane >= begin), 1.0, 0.0)

        def heads(m, _):
            for g in range(half // 128):
                lanes = slice(g * 128, (g + 1) * 128)
                kh, kl = kvh[2 + m, :tok, lanes], kvl[2 + m, :tok, lanes]
                vh, vl = kvh[m, :tok, lanes], kvl[m, :tok, lanes]
                both = jnp.concatenate(stacked(m, lanes), axis=1)
                kk = jnp.concatenate([kh, kh], axis=1)
                k0 = jnp.concatenate([kl, jnp.zeros_like(kl)], axis=1)
                sc = mm(both, jnp.concatenate([kk, k0], axis=0), NT)
                pp = jnp.concatenate(weigh(sc[:, :tok] + sc[:, tok:], allow), axis=1)
                vv = jnp.concatenate([vh, vl], axis=1)
                o = mm(pp, jnp.concatenate([vv, vv], axis=0))
                collect(m, lanes, o[:, :128] + o[:, 128:], jnp.zeros((tok, 128), f32))
            return 0

        lax.fori_loop(0, 2, heads, 0)

    def attend(back):
        blocks = [(pc.s + pc.S - back - d) % pc.S for d in (0, 1)]
        keys_values(split(jnp.concatenate([ev_all[b] for b in blocks], axis=0)), step)
        cols = [b * tok + lane for b in blocks]
        allow = [jnp.where((c >= begin) & (c <= row), 1.0, 0.0) for c in cols]
        allow = jnp.concatenate(allow, axis=1)

        def heads(m, _):
            for g in range(half // 128):
                lanes = slice(g * 128, (g + 1) * 128)
                kh, kl = kvh[2 + m][:, lanes], kvl[2 + m][:, lanes]
                vh, vl = kvh[m][:, lanes], kvl[m][:, lanes]
                qh, ql = stacked(m, lanes)
                two = jnp.concatenate([qh, ql], axis=1)
                sc = mm(two, jnp.concatenate([kh, kh], axis=1), NT) + mm(qh, kl, NT)
                ph, plo = weigh(sc, allow)
                o = mm(ph, jnp.concatenate([vh, vl], axis=1))
                o = (o[:, :128] + o[:, 128:]) + mm(plo, vh)
                collect(m, lanes, o, att[m, :, lanes])
            return 0

        lax.fori_loop(0, 2, heads, 0)

    ev.forward()
    attend_own()
    ev.near()
    neg.start_z()
    ev.pair(0)
    ev.pair(1)
    attend(1)
    ev.far()
    neg.start_gather()
    ev.pair(2)
    attend(3)
    neg.wait_z()
    nb.one.start()
    nb.begin(0)
    na.one.start()
    na.push(0, 0)

    a = jnp.concatenate([att[0], att[1]], axis=1)
    centered = a - jnp.mean(a, axis=1, keepdims=True)
    var = jnp.mean(centered * centered, axis=1, keepdims=True)
    normed = centered * lax.rsqrt(var + epsilon) * gain_ref[...]
    gated = normed * jnp.concatenate([gates[0], gates[1]], axis=1)
    c_wo.wait()
    o_own = x_own + mm3(split(gated), split(wo[...]))
    pad = out_all.shape[1] - tok
    out_all[pc.s, :tok, :] = o_own
    out_all[pc.s, tok:, :] = jnp.zeros((pad, D), f32)
    out_all[pc.s, tok:tok + 1, :tok] = tgt_ref[...].astype(f32)
    out_all[pc.s, tok:tok + 1, tok:step] = jnp.broadcast_to(msk_ref[...], (1, tok)).astype(f32)
    out.start()
    na.one.forward()
    nb.one.forward()
    nb.two[0].forward()
    na.one.wait_left()
    na.push(1, 0)
    na.one.wait_right()
    na.push(2, 0)
    out.forward()
    nb.one.wait_left()
    nb.begin(1)
    nb.one.wait_right()
    nb.begin(2)
    na.one.wait_opp()
    na.push(3, 0)
    nb.near(0)
    nb.one.wait_opp()
    nb.begin(3)
    nb.far(0)

    m0 = split(neg_all[0, pc.y, pc.c].reshape(share, half))
    m1 = split(neg_all[1, pc.y, pc.c].reshape(share, half))
    column = pc.s * share + lax.broadcasted_iota(jnp.int32, (share, step), 0)
    panel[...] = jnp.zeros_like(panel)
    loss_acc[...] = jnp.zeros_like(loss_acc)

    def own_columns(y):
        pair = [out_all[2 * y], out_all[2 * y + 1]]
        ob = jnp.concatenate([q[:tok] for q in pair], axis=0)
        tg = jnp.concatenate([q[tok:tok + 1, :tok] for q in pair], axis=1).astype(jnp.int32)
        mk = jnp.concatenate([q[tok:tok + 1, tok:step] for q in pair], axis=1).astype(jnp.int32)
        obh, obl = split(ob)
        logits = mm3(m0, (obh[:, :half], obl[:, :half]), NT)
        logits = logits + mm3(m1, (obh[:, half:], obl[:, half:]), NT)
        bits = jnp.right_shift(jnp.broadcast_to(mk, column.shape), column // 128) & 1
        g, wt, sp = loss_core(logits, column == jnp.broadcast_to(tg, column.shape), bits.astype(f32))
        loss_acc[...] += wt * sp
        panel[...] += mm3(split(g), (obh, obl)).reshape(panel.shape)

    out.pair(0)
    own_columns(pc.y)
    for n in (1, 2, 3):
        nb.two[n].forward()
    out.near()
    out.pair(1)
    own_columns(out.ring.left)
    out.pair(2)
    own_columns(out.ring.right)
    out.far()
    for n in range(4):
        na.two[n].start()
    out.pair(3)
    own_columns(out.ring.opp)
    pan.start_x()
    loss.t0[...] = jnp.broadcast_to(jnp.sum(loss_acc[...]), loss.t0.shape)
    loss.start_x()

    mine = out_all[pc.s]
    oh = [split(mine[:tok, k * half:(k + 1) * half]) for k in (0, 1)]
    tcol = jnp.transpose(jnp.broadcast_to(mine[tok:tok + 1, :tok], (tok, tok)))
    tcol = jnp.concatenate([tcol, tcol], axis=1).astype(jnp.int32)
    mcol = jnp.broadcast_to(mine[tok:tok + 1, tok:tok + 1], (tok, step)).astype(jnp.int32)
    acc[...] = jnp.zeros_like(acc)

    lane2 = lax.broadcasted_iota(jnp.int32, (tok, step), 1)

    def own_tokens(j):
        n0 = split(neg_all[0, j // 2, j % 2].reshape(share, half))
        n1 = split(neg_all[1, j // 2, j % 2].reshape(share, half))
        logits = mm3(oh[0], n0, NT) + mm3(oh[1], n1, NT)
        live = (jnp.right_shift(mcol, 2 * j + lane2 // 128) & 1).astype(f32)
        g, _, _ = loss_core(logits, lane2 + j * share == tcol, live)
        gs = split(g)
        acc[0] += mm3(gs, n0)
        acc[1] += mm3(gs, n1)

    def own_pair(to):
        y = (pc.y + to) % pc.Y
        piece = (0, 2, 3, 1)[to]

        def one(c, _):
            own_tokens(2 * y + c)
            return 0

        for n in range(4):
            na.arrived(n, to)
            nb.arrived(piece, n)
        lax.fori_loop(0, 2, one, 0)

    for n in range(4):
        na.two[n].forward()
    for n in (1, 2, 3):
        nb.near(n)
    own_pair(0)
    pan.pass_x()
    for n in (1, 2, 3):
        nb.far(n)
    for n in range(4):
        na.near(n)
    pan.start_z()
    loss.start_z()
    own_pair(3)
    for n in range(4):
        na.far(n)
    own_pair(1)
    pan.start_gather()
    loss.start_s()
    own_pair(2)
    grad_ref[0, :, :half] = acc[0]
    grad_ref[0, :, half:] = acc[1]
    pan.wait_z()
    for pair in zip(lane_a.steps(), lane_b.steps()):
        for step_of in pair:
            step_of()
    total_ref[...] = loss.total()
    lane_a.wait_core()
    lane_b.wait_core()
    for q in (ev, out, neg, na, nb, pan, lane_a, lane_b, loss):
        q.wait_sends()


def scatter_kernel(n_item, scale, panel_all, neg_ref, owner_ref, total_ref, table_ref, loss_ref, buf, sem):
    item = lax.axis_index("item")
    rows = table_ref.shape[0]
    panel = neg_ref.shape[1]
    half = buf.shape[2]
    table_ref[...] = jnp.zeros_like(table_ref)
    loss_ref[0, 0] = jnp.max(total_ref[...]) * scale
    for p in range(neg_ref.shape[0]):

        @pl.when(owner_ref[p] == item)
        def _():
            copy = pltpu.make_async_copy(panel_all.at[:, pl.ds(p * panel, panel), :], buf, sem)
            copy.start()
            spot = lax.broadcasted_iota(jnp.int32, (rows, panel), 0)
            pick = jnp.where(spot == neg_ref[pl.ds(p, 1), :], 1.0, 0.0).astype(bf16)
            copy.wait()
            for k in (0, 1):
                hi, lo = split(buf[k])
                table_ref[:, k * half:(k + 1) * half] += mm(pick, hi) + mm(pick, lo)


def params(cid=None):
    if cid is None:
        return pltpu.CompilerParams(vmem_limit_bytes=VMEM_LIMIT)
    return pltpu.CompilerParams(
        vmem_limit_bytes=VMEM_LIMIT, collective_id=cid, has_side_effects=True
    )


def per_device(
    n_seq, n_item, events, w_uvqk, out_gain, w_out, item_table,
    user_lengths, neg_ids, panel_owner, block_mask, targets,
):
    _, tok, D = events.shape
    X, Z, Y = X_RING, n_item // X_RING, n_seq // 2
    n_neg = neg_ids.shape[0] * neg_ids.shape[1]
    share = n_neg // n_seq
    R = share // n_item
    half = D // 2
    shape = jax.ShapeDtypeStruct

    aug = tok + 16
    step = 2 * tok
    full = (2, Y, 2, X, Z * R, half)
    one = pltpu.SemaphoreType.DMA
    event_grad, panel_all, total = pl.pallas_call(
        functools.partial(main_kernel, n_seq, n_item),
        out_shape=(shape(events.shape, f32), shape(full, f32), shape((8, 128), f32)),
        in_specs=[ANY, ANY, VM, ANY, ANY, VM, VM, VM, VM, VM], out_specs=(VM, ANY, VM),
        scratch_shapes=[
            pltpu.VMEM((n_seq, tok, D), f32), pltpu.VMEM(full, f32),
            pltpu.VMEM((n_seq, aug, D), f32), pltpu.VMEM(item_table.shape, f32),
            pltpu.VMEM(w_uvqk.shape, f32), pltpu.VMEM(w_out.shape, f32),
            pltpu.VMEM((8, D, half), bf16), pltpu.VMEM((8, D, half), bf16),
            pltpu.VMEM((4, step, half), bf16), pltpu.VMEM((4, step, half), bf16),
            pltpu.VMEM((2, tok, half), f32), pltpu.VMEM((2, tok, half), f32),
            pltpu.VMEM((2, tok, half), f32),
            pltpu.VMEM((X, Z, R, D), f32), pltpu.VMEM((X, Z, R, D), f32),
            pltpu.VMEM((2, tok, half), f32), pltpu.VMEM((share, step), f32),
            one, one, one, one,
        ] + SEQ_SEMS * 2 + reduce_scratch(X, Z, R, D) * 2 + LANE_SEMS * 4 + loss_scratch(X, Z, n_seq),
        compiler_params=params(1), name="main",
    )(events, w_uvqk, out_gain.reshape(1, D), w_out, item_table, user_lengths, neg_ids,
      panel_owner.reshape(1, -1), block_mask, targets)

    scale = 1.0 / (tok * n_seq * n_item)
    table_grad, mean_loss = pl.pallas_call(
        functools.partial(scatter_kernel, n_item, scale),
        out_shape=(shape(item_table.shape, f32), shape((1, 1), f32)),
        in_specs=[ANY, VM, SM, VM], out_specs=(VM, SM),
        scratch_shapes=[pltpu.VMEM((2, neg_ids.shape[1], half), f32), pltpu.SemaphoreType.DMA],
        compiler_params=params(), name="scatter",
    )(panel_all.reshape(2, n_neg, half), neg_ids, panel_owner, total)
    return (mean_loss.reshape(()), event_grad, table_grad)


def solution(mesh):
    placed = (
        P("item", "seq", None), P(), P(), P(), P("item", None), P("item", None),
        P(), P(), P("item", "seq"), P("item", "seq"),
    )
    body = functools.partial(per_device, mesh.shape["seq"], mesh.shape["item"])
    return jax.shard_map(
        body, mesh=mesh, in_specs=placed,
        out_specs=(P(), P("item", "seq", None), P("item", None)), check_vma=False,
    )
```

```python
import functools

import jax
import jax.numpy as jnp
from jax import lax
from jax.experimental import pallas as pl
from jax.experimental.pallas import tpu as pltpu
from jax.sharding import PartitionSpec as P

H = 16
X_RING = 4
beta_weight = 0.75
epsilon = 1e-05
f32, bf16 = jnp.float32, jnp.bfloat16
MESH = pl.DeviceIdType.MESH
VMEM_LIMIT = 60 * 1024 * 1024

VM = pl.BlockSpec(memory_space=pltpu.VMEM)
SM = pl.BlockSpec(memory_space=pltpu.SMEM)
ANY = pl.BlockSpec(memory_space=pl.ANY)
NN = (((1,), (0,)), ((), ()))
NT = (((1,), (1,)), ((), ()))


def split(x):
    hi = x.astype(bf16)
    return hi, (x - hi.astype(f32)).astype(bf16)


def mm(a, b, dims=NN):
    return lax.dot_general(a, b, dims, preferred_element_type=f32)


def mm3(a, b, dims=NN):
    (ah, al), (bh, bl) = a, b
    return mm(ah, bh, dims) + (mm(al, bh, dims) + mm(ah, bl, dims))


def sigmoid(x):
    return 0.5 + 0.5 * jnp.tanh(0.5 * x)


class Place:
    def __init__(self, n_seq, n_item):
        self.S, self.I = n_seq, n_item
        self.X = X_RING
        self.Z = n_item // self.X
        self.Y = n_seq // 2
        self.s = lax.axis_index("seq")
        self.i = lax.axis_index("item")
        self.y, self.c = self.s // 2, self.s % 2
        self.z, self.x = self.i // self.X, self.i % self.X

    def at_x(self, x):
        return (self.s, self.z * self.X + x)

    def at_z(self, z):
        return (self.s, z * self.X + self.x)

    def at_y(self, y):
        return (2 * y + self.c, self.i)

    def at_s(self, s):
        return (s, self.i)

    def partner(self):
        return (2 * self.y + 1 - self.c, self.i)


def rdma(src, dst, send, recv, dev):
    return pltpu.make_async_remote_copy(
        src_ref=src, dst_ref=dst, send_sem=send, recv_sem=recv, device_id=dev, device_id_type=MESH
    )


class Ring4:
    def __init__(self, me, dev, part, send, recv, causal=False):
        self.me, self.dev, self.part, self.causal = me, dev, part, causal
        self.send, self.recv = send, recv
        self.right, self.left = (me + 1) % 4, (me + 3) % 4
        self.opp = (me + 2) % 4

    def _c(self, slot, src, k, h, to):
        return rdma(src, self.part(k, h), self.send.at[slot], self.recv.at[slot], self.dev(to))

    def start(self):
        me = self.me
        self.r = [self._c(h, self.part(me, h), me, h, self.right) for h in (0, 1)]
        self.l1 = self._c(3, self.part(me, 1), me, 1, self.left)
        self.r[0].start()
        self.l1.start()
        self.r[1].start()
        self.l = [self.l1]
        if not self.causal:
            self.l.append(self._c(2, self.part(me, 0), me, 0, self.left))
            self.l[1].start()

    def forward_right(self):
        self.r[0].wait_recv()
        self.fr = self._c(4, self.part(self.left, 0), self.left, 0, self.right)
        self.fr.start()

    def forward_left(self):
        self.l1.wait_recv()
        self.fl = self._c(5, self.part(self.right, 1), self.right, 1, self.left)
        self.fl.start()

    def forward(self):
        self.forward_right()
        self.forward_left()

    def wait_left(self):
        self.r[1].wait_recv()

    def wait_right(self):
        self.l[1].wait_recv()

    def wait_opp(self):
        self.fr.wait_recv()
        self.fl.wait_recv()

    def wait_sends(self):
        for c in (*self.r, *self.l, self.fr, self.fl):
            c.wait_send()


class CoreSends:
    def __init__(self, dev, send, recv):
        self.dev, self.send, self.recv, self.copies = dev, send, recv, []

    def push(self, blk):
        n = len(self.copies)
        c = rdma(blk, blk, self.send.at[n], self.recv.at[n], self.dev)
        c.start()
        self.copies.append(c)

    def wait_recv(self, n):
        self.copies[n].wait_recv()

    def wait_sends(self):
        for c in self.copies:
            c.wait_send()


def enter(devs):
    barrier = pltpu.get_barrier_semaphore()
    for d in devs:
        pl.semaphore_signal(barrier, inc=1, device_id=d, device_id_type=MESH)
    return lambda: pl.semaphore_wait(barrier, len(devs))


def seq_peers(pc):
    return [pc.at_s((pc.s + d) % pc.S) for d in range(1, pc.S)]


def plane_peers(pc):
    xs = [pc.at_x((pc.x + d) % pc.X) for d in range(1, pc.X)]
    zs = [pc.at_z((pc.z + d) % pc.Z) for d in range(1, pc.Z)]
    return xs + zs


class SeqGather:
    def __init__(self, pc, full, sems, causal=False):
        send, recv, csend, crecv = sems
        half = full.shape[1] // 2
        self.pc, self.full, self.causal = pc, full, causal
        part = lambda y, h: full.at[2 * y + pc.c, pl.ds(h * half, half)]
        self.ring = Ring4(pc.y, pc.at_y, part, send, recv, causal)
        self.core = CoreSends(pc.partner(), csend, crecv)

    def push(self, y):
        self.core.push(self.full.at[2 * y + self.pc.c])

    def start(self):
        self.ring.start()
        self.push(self.pc.y)

    def forward(self):
        self.ring.forward()

    def near(self):
        r = self.ring
        r.wait_left()
        self.push(r.left)
        if not self.causal:
            r.wait_right()
            self.push(r.right)

    def far(self):
        self.ring.wait_opp()
        self.push(self.ring.opp)

    def pair(self, n):
        self.core.wait_recv(n)

    def wait_sends(self):
        self.ring.wait_sends()
        self.core.wait_sends()


def dma(n):
    return pltpu.SemaphoreType.DMA((n,))


SEQ_SEMS = [dma(6), dma(6), dma(4), dma(4)]


class Reduce:
    def __init__(self, pc, part, full, refs):
        self.pc, self.part, self.full = pc, part, full
        (self.rx, self.mid, self.sx, self.rz, self.own, self.xs, self.xr,
         self.zs, self.zr, self.gs, self.gr, self.lsem) = refs
        self.hz = part.shape[1] // 2
        self.right, self.left = (pc.x + 1) % 4, (pc.x + 3) % 4
        self.opp = (pc.x + 2) % 4

    def _half(self, k, h):
        return self.part.at[k, pl.ds(h * self.hz, self.hz)]

    def _x(self, slot, src, to):
        c = rdma(src, self.rx.at[slot], self.xs.at[slot], self.xr.at[slot], self.pc.at_x(to))
        c.start()
        self.cx.append(c)

    def start_x(self):
        self.cx = []
        self._x(0, self._half(self.opp, 0), self.right)
        self._x(1, self._half(self.opp, 1), self.left)
        self._x(2, self._half(self.right, 1), self.right)
        self._x(3, self._half(self.left, 0), self.left)

    def pass_x(self):
        h = self.hz
        self.cx[0].wait_recv()
        self.mid[0] = self.part[self.right, :h] + self.rx[0]
        self._x(4, self.mid.at[0], self.right)
        self.cx[1].wait_recv()
        self.mid[1] = self.part[self.left, h:] + self.rx[1]
        self._x(5, self.mid.at[1], self.left)

    def start_z(self):
        pc, h = self.pc, self.hz
        for c in self.cx[2:]:
            c.wait_recv()
        self.sx[:h] = self.part[pc.x, :h] + (self.rx[4] + self.rx[3])
        self.sx[h:] = self.part[pc.x, h:] + (self.rx[2] + self.rx[5])
        self.cz = []
        for d in range(1, pc.Z):
            to = (pc.z + d) % pc.Z
            c = rdma(self.sx.at[to], self.rz.at[d - 1], self.zs.at[d - 1], self.zr.at[d - 1], pc.at_z(to))
            c.start()
            self.cz.append(c)

    def start_gather(self):
        pc = self.pc
        total = self.sx[pc.z]
        for c in self.cz:
            c.wait_recv()
        for d in range(pc.Z - 1):
            total = total + self.rz[d]
        half = total.shape[1] // 2
        rows = total.shape[0]
        self.own[0] = total[:, :half]
        self.own[1] = total[:, half:]
        mine = self.full.at[:, pc.y, pc.c, pc.x, pl.ds(pl.multiple_of(pc.z * rows, rows), rows), :]
        self.local = pltpu.make_async_copy(self.own, mine, self.lsem)
        self.local.start()
        self.cg = []
        for d in range(1, pc.Z):
            to = (pc.z + d) % pc.Z
            c = rdma(self.own, mine, self.gs.at[d - 1], self.gr.at[d - 1], pc.at_z(to))
            c.start()
            self.cg.append(c)

    def wait_z(self):
        for c in self.cg:
            c.wait_recv()
        self.local.wait()

    def wait_sends(self):
        for c in (*self.cx, *self.cz, *self.cg):
            c.wait_send()


def reduce_scratch(X, Z, R, D):
    nz = max(Z - 1, 1)
    return [
        pltpu.VMEM((6, Z // 2, R, D), f32),
        pltpu.VMEM((2, Z // 2, R, D), f32),
        pltpu.VMEM((Z, R, D), f32),
        pltpu.VMEM((nz, R, D), f32),
        pltpu.VMEM((2, R, D // 2), f32),
        dma(6), dma(6), dma(nz), dma(nz), dma(nz), dma(nz), pltpu.SemaphoreType.DMA,
    ]


N_REDUCE = 12


class Lane:
    def __init__(self, pc, first, second, blk, sems):
        (f, fdev), (g, gdev) = first, second
        self.f, self.g, self.blk = f, g, blk
        rows = blk(0, 0).shape[0] // 2
        part = lambda ref, h: ref.at[pl.ds(h * rows, rows), :]
        self.one = Ring4(f, fdev, lambda k, h: part(blk(k, g), h), sems[0], sems[1])
        self.two = []
        for n, k in enumerate((f, (f + 3) % 4, (f + 1) % 4, (f + 2) % 4)):
            ring = Ring4(
                g, gdev, lambda j, h, k=k: part(blk(k, j), h), sems[2 + 2 * n], sems[3 + 2 * n]
            )
            ring.piece = k
            self.two.append(ring)
        self.core = CoreSends(pc.partner(), sems[10], sems[11])
        self.at = {}

    def push(self, n, to):
        self.at[n, to] = len(self.core.copies)
        self.core.push(self.blk(self.two[n].piece, (self.g + to) % 4))

    def begin(self, n):
        self.two[n].start()
        self.push(n, 0)

    def near(self, n):
        ring = self.two[n]
        ring.wait_left()
        self.push(n, 3)
        ring.wait_right()
        self.push(n, 1)

    def far(self, n):
        self.two[n].wait_opp()
        self.push(n, 2)

    def arrived(self, n, to):
        self.core.wait_recv(self.at[n, to])

    def steps(self):
        one, two = self.one, self.two
        return [
            lambda: (one.start(), self.begin(0)),
            lambda: one.forward(),
            lambda: (one.wait_left(), self.begin(1)),
            lambda: (one.wait_right(), self.begin(2)),
            lambda: two[0].forward(),
            lambda: (one.wait_opp(), self.begin(3)),
            lambda: two[1].forward(),
            lambda: two[2].forward(),
            lambda: self.near(0),
            lambda: two[3].forward(),
            lambda: self.near(1),
            lambda: self.near(2),
            lambda: self.far(0),
            lambda: self.near(3),
            lambda: self.far(1),
            lambda: self.far(2),
            lambda: self.far(3),
        ]

    def wait_core(self):
        for n in range(16):
            self.core.wait_recv(n)

    def wait_sends(self):
        for q in (self.one, *self.two, self.core):
            q.wait_sends()


LANE_SEMS = [dma(6)] * 10 + [dma(16)] * 2


class LossSum:
    def __init__(self, pc, refs):
        self.pc = pc
        (self.t0, self.lx, self.tx, self.lz, self.tz, self.ls,
         self.xs, self.xr, self.zs, self.zr, self.ss, self.sr) = refs
        self.all = []

    def _send(self, src, dst, send, recv, devs):
        out = []
        for d, dev in enumerate(devs):
            c = rdma(src, dst.at[d], send.at[d], recv.at[d], dev)
            c.start()
            out.append(c)
        self.all += out
        return out

    def start_x(self):
        pc = self.pc
        devs = [pc.at_x((pc.x + d) % pc.X) for d in range(1, pc.X)]
        self.c = self._send(self.t0, self.lx, self.xs, self.xr, devs)

    def _sum(self, own, got, n):
        for c in self.c:
            c.wait_recv()
        total = own[...]
        for d in range(n):
            total = total + got[d]
        return total

    def start_z(self):
        pc = self.pc
        self.tx[...] = self._sum(self.t0, self.lx, pc.X - 1)
        devs = [pc.at_z((pc.z + d) % pc.Z) for d in range(1, pc.Z)]
        self.c = self._send(self.tx, self.lz, self.zs, self.zr, devs)

    def start_s(self):
        pc = self.pc
        self.tz[...] = self._sum(self.tx, self.lz, pc.Z - 1)
        self.c = self._send(self.tz, self.ls, self.ss, self.sr, seq_peers(pc))

    def total(self):
        return self._sum(self.tz, self.ls, self.pc.S - 1)

    def wait_sends(self):
        for c in self.all:
            c.wait_send()


def loss_scratch(X, Z, S):
    nz = max(Z - 1, 1)
    tile = lambda *n: pltpu.VMEM((*n, 8, 128), f32)
    return [
        tile(), tile(X - 1), tile(), tile(nz), tile(), tile(S - 1),
        dma(X - 1), dma(X - 1), dma(nz), dma(nz), dma(S - 1), dma(S - 1),
    ]


N_LOSS = 12


def loss_core(logits, target, live):
    m = jnp.where(target, -logits, logits)
    w = jnp.where(target, -beta_weight, live)
    e = jnp.exp(-jnp.abs(m))
    sig = jnp.where(m >= 0.0, 1.0, e) / (1.0 + e)
    return w * sig, jnp.abs(w), jnp.maximum(m, 0.0) + jnp.log1p(e)


def main_kernel(
    n_seq, n_item, ev_ref, w_ref, gain_ref, wo_ref, table_ref, lens_ref, neg_ref, owner_ref,
    msk_ref, tgt_ref, grad_ref, panel_all, total_ref, *scratch,
):
    pc = Place(n_seq, n_item)
    (ev_all, neg_all, out_all, table, w, wo, wh, wl, kvh, kvl, qs, gates, att, part, panel,
     acc, loss_acc, s_ev, s_table, s_w, s_wo) = scratch[:21]
    rest = scratch[21:]
    ev = SeqGather(pc, ev_all, rest[:4], causal=True)
    out = SeqGather(pc, out_all, rest[4:8])
    rest = rest[8:]
    neg = Reduce(pc, part, neg_all, rest[:N_REDUCE])
    pan = Reduce(pc, panel, panel_all, rest[N_REDUCE:2 * N_REDUCE])
    rest = rest[2 * N_REDUCE:]
    along_x, along_y = (pc.x, pc.at_x), (pc.y, pc.at_y)

    def lanes_of(full, sems):
        a = Lane(pc, along_x, along_y, lambda k, j: full.at[0, j, pc.c, k], sems[:12])
        b = Lane(pc, along_y, along_x, lambda k, j: full.at[1, k, pc.c, j], sems[12:])
        return a, b

    na, nb = lanes_of(neg_all, rest[:24])
    lane_a, lane_b = lanes_of(panel_all, rest[24:48])
    loss = LossSum(pc, rest[48:])

    tok, D = grad_ref.shape[1], grad_ref.shape[2]
    half = D // 2
    step = 2 * tok
    rows = table.shape[0]
    X, Z, R = part.shape[0], part.shape[1], part.shape[2]
    share = X * Z * R
    hd = D // H
    hpg = 128 // hd

    ready = enter(plane_peers(pc) + seq_peers(pc))
    c_ev = pltpu.make_async_copy(ev_ref.at[0], ev_all.at[pc.s], s_ev)
    c_table = pltpu.make_async_copy(table_ref, table, s_table)
    c_w = pltpu.make_async_copy(w_ref, w, s_w)
    c_wo = pltpu.make_async_copy(wo_ref, wo, s_wo)
    for c in (c_ev, c_table, c_w, c_wo):
        c.start()

    per_panel = neg_ref.shape[1] // share
    p = pc.s // per_panel
    first = pl.multiple_of((pc.s % per_panel) * share, share)
    slot = lax.broadcasted_iota(jnp.int32, owner_ref.shape, 1)
    owner = jnp.sum(jnp.where(slot == p, owner_ref[...], 0), axis=1, keepdims=True)
    ids = neg_ref[pl.ds(p, 1), pl.ds(first, share)] + rows * jnp.broadcast_to(owner, (1, share))
    ids = jnp.transpose(jnp.broadcast_to(ids - pc.i * rows, (128, share)).astype(f32))
    spot = lax.broadcasted_iota(jnp.int32, (share, 128), 1).astype(f32)
    picks = [jnp.where(ids == spot + float(k), 1.0, 0.0).astype(bf16) for k in range(0, rows, 128)]
    pick = jnp.concatenate(picks, axis=1)
    c_table.wait()
    hi, lo = split(table[...])
    part[...] = (mm(pick, hi) + mm(pick, lo)).reshape(part.shape)
    c_ev.wait()
    ready()
    ev.start()
    neg.start_x()

    c_w.wait()

    def split_w(n, _):
        wh[n], wl[n] = split(w[:, pl.ds(pl.multiple_of(n * half, half), half)])
        return 0

    lax.fori_loop(0, 8, split_w, 0)
    x_own = ev_all[pc.s]
    xo = split(x_own)

    def project(xs, n):
        r = mm3(xs, (wh[n], wl[n]))
        return r * sigmoid(r)

    for n in range(2):
        qs[n] = project(xo, 4 + n)
        gates[n] = project(xo, n)
    neg.pass_x()

    lane_head = lax.broadcasted_iota(jnp.int32, (tok, 128), 1) // hd
    sub = lax.broadcasted_iota(jnp.int32, (tok, tok), 0)
    lane = lax.broadcasted_iota(jnp.int32, (tok, tok), 1)
    row = pc.s * tok + sub
    begin = jnp.zeros((tok, tok), jnp.int32)
    end = jnp.zeros((1, 1), jnp.int32)
    for u in range(lens_ref.shape[1]):
        end = end + lens_ref[0:1, u:u + 1]
        wide = jnp.broadcast_to(end, row.shape)
        begin = jnp.where(row >= wide, wide, begin)

    def stacked(m, lanes):
        q = qs[m][:, lanes]
        parts = [jnp.where(lane_head == h, q, 0.0) for h in range(hpg)]
        return split(jnp.concatenate(parts, axis=0))

    def collect(m, lanes, o, base):
        got = base
        for h in range(hpg):
            got = got + jnp.where(lane_head == h, o[h * tok:(h + 1) * tok], 0.0)
        att[m, :, lanes] = got

    def weigh(sc, allow):
        pr = (sc * sigmoid(sc)).reshape(hpg, tok, sc.shape[1]) * allow[None]
        return split(pr.reshape(sc.shape))

    def keys_values(xs, n_rows):
        def kv_step(n, _):
            hi, lo = split(project(xs, jnp.where(n < 2, 2 + n, 4 + n)))
            kvh[n, :n_rows], kvl[n, :n_rows] = hi, lo
            return 0

        lax.fori_loop(0, 4, kv_step, 0)

    def attend_own():
        keys_values(xo, tok)
        ev.forward()
        allow = jnp.where((lane <= sub) & (pc.s * tok + lane >= begin), 1.0, 0.0)

        def heads(m, _):
            for g in range(half // 128):
                lanes = slice(g * 128, (g + 1) * 128)
                kh, kl = kvh[2 + m, :tok, lanes], kvl[2 + m, :tok, lanes]
                vh, vl = kvh[m, :tok, lanes], kvl[m, :tok, lanes]
                both = jnp.concatenate(stacked(m, lanes), axis=1)
                kk = jnp.concatenate([kh, kh], axis=1)
                k0 = jnp.concatenate([kl, jnp.zeros_like(kl)], axis=1)
                sc = mm(both, jnp.concatenate([kk, k0], axis=0), NT)
                pp = jnp.concatenate(weigh(sc[:, :tok] + sc[:, tok:], allow), axis=1)
                vv = jnp.concatenate([vh, vl], axis=1)
                o = mm(pp, jnp.concatenate([vv, vv], axis=0))
                collect(m, lanes, o[:, :128] + o[:, 128:], jnp.zeros((tok, 128), f32))
            return 0

        lax.fori_loop(0, 2, heads, 0)

    def attend(back, between):
        blocks = [(pc.s + pc.S - back - d) % pc.S for d in (0, 1)]
        keys_values(split(jnp.concatenate([ev_all[b] for b in blocks], axis=0)), step)
        between()
        cols = [b * tok + lane for b in blocks]
        allow = [jnp.where((c >= begin) & (c <= row), 1.0, 0.0) for c in cols]
        allow = jnp.concatenate(allow, axis=1)

        def heads(m, _):
            for g in range(half // 128):
                lanes = slice(g * 128, (g + 1) * 128)
                kh, kl = kvh[2 + m][:, lanes], kvl[2 + m][:, lanes]
                vh, vl = kvh[m][:, lanes], kvl[m][:, lanes]
                qh, ql = stacked(m, lanes)
                two = jnp.concatenate([qh, ql], axis=1)
                sc = mm(two, jnp.concatenate([kh, kh], axis=1), NT) + mm(qh, kl, NT)
                ph, plo = weigh(sc, allow)
                o = mm(ph, jnp.concatenate([vh, vl], axis=1))
                o = (o[:, :128] + o[:, 128:]) + mm(plo, vh)
                collect(m, lanes, o, att[m, :, lanes])
            return 0

        lax.fori_loop(0, 2, heads, 0)

    attend_own()
    neg.start_z()
    ev.near()
    ev.pair(0)
    ev.pair(1)
    attend(1, neg.start_gather)
    ev.far()
    ev.pair(2)

    def spread_start():
        neg.wait_z()
        nb.one.start()
        na.one.start()
        nb.begin(0)
        na.push(0, 0)

    attend(3, spread_start)
    nb.one.forward()
    na.one.forward()
    nb.two[0].forward()

    a = jnp.concatenate([att[0], att[1]], axis=1)
    centered = a - jnp.mean(a, axis=1, keepdims=True)
    var = jnp.mean(centered * centered, axis=1, keepdims=True)
    normed = centered * lax.rsqrt(var + epsilon) * gain_ref[...]
    gated = normed * jnp.concatenate([gates[0], gates[1]], axis=1)
    c_wo.wait()
    o_own = x_own + mm3(split(gated), split(wo[...]))
    pad = out_all.shape[1] - tok
    out_all[pc.s, :tok, :] = o_own
    out_all[pc.s, tok:, :] = jnp.zeros((pad, D), f32)
    out_all[pc.s, tok:tok + 1, :tok] = tgt_ref[...].astype(f32)
    out_all[pc.s, tok:tok + 1, tok:step] = jnp.broadcast_to(msk_ref[...], (1, tok)).astype(f32)
    out.start()
    na.one.wait_left()
    na.push(1, 0)
    na.one.wait_right()
    na.push(2, 0)
    na.one.wait_opp()
    na.push(3, 0)
    nb.near(0)
    nb.far(0)
    out.forward()

    m0 = split(neg_all[0, pc.y, pc.c].reshape(share, half))
    m1 = split(neg_all[1, pc.y, pc.c].reshape(share, half))
    column = pc.s * share + lax.broadcasted_iota(jnp.int32, (share, step), 0)
    panel[...] = jnp.zeros_like(panel)
    loss_acc[...] = jnp.zeros_like(loss_acc)

    def own_columns(y):
        pair = [out_all[2 * y], out_all[2 * y + 1]]
        ob = jnp.concatenate([q[:tok] for q in pair], axis=0)
        tg = jnp.concatenate([q[tok:tok + 1, :tok] for q in pair], axis=1).astype(jnp.int32)
        mk = jnp.concatenate([q[tok:tok + 1, tok:step] for q in pair], axis=1).astype(jnp.int32)
        obh, obl = split(ob)
        logits = mm3(m0, (obh[:, :half], obl[:, :half]), NT)
        logits = logits + mm3(m1, (obh[:, half:], obl[:, half:]), NT)
        bits = jnp.right_shift(jnp.broadcast_to(mk, column.shape), column // 128) & 1
        g, wt, sp = loss_core(logits, column == jnp.broadcast_to(tg, column.shape), bits.astype(f32))
        loss_acc[...] += wt * sp
        panel[...] += mm3(split(g), (obh, obl)).reshape(panel.shape)

    out.pair(0)
    own_columns(pc.y)
    nb.one.wait_left()
    nb.begin(1)
    nb.one.wait_right()
    nb.begin(2)
    nb.one.wait_opp()
    nb.begin(3)
    out.near()
    out.pair(1)
    own_columns(out.ring.left)
    for n in (1, 2, 3):
        nb.two[n].forward()
    out.pair(2)
    own_columns(out.ring.right)
    out.far()
    for n in range(4):
        na.two[n].start()
    out.pair(3)
    own_columns(out.ring.opp)
    pan.start_x()
    loss.t0[...] = jnp.broadcast_to(jnp.sum(loss_acc[...]), loss.t0.shape)
    loss.start_x()

    mine = out_all[pc.s]
    oh = [split(mine[:tok, k * half:(k + 1) * half]) for k in (0, 1)]
    tcol = jnp.transpose(jnp.broadcast_to(mine[tok:tok + 1, :tok], (tok, tok)))
    tcol = jnp.concatenate([tcol, tcol], axis=1).astype(jnp.int32)
    mcol = jnp.broadcast_to(mine[tok:tok + 1, tok:tok + 1], (tok, step)).astype(jnp.int32)
    acc[...] = jnp.zeros_like(acc)

    lane2 = lax.broadcasted_iota(jnp.int32, (tok, step), 1)

    def own_tokens(j):
        n0 = split(neg_all[0, j // 2, j % 2].reshape(share, half))
        n1 = split(neg_all[1, j // 2, j % 2].reshape(share, half))
        logits = mm3(oh[0], n0, NT) + mm3(oh[1], n1, NT)
        live = (jnp.right_shift(mcol, 2 * j + lane2 // 128) & 1).astype(f32)
        g, _, _ = loss_core(logits, lane2 + j * share == tcol, live)
        gs = split(g)
        acc[0] += mm3(gs, n0)
        acc[1] += mm3(gs, n1)

    def own_pair(to):
        y = (pc.y + to) % pc.Y
        piece = (0, 2, 3, 1)[to]

        def one(c, _):
            own_tokens(2 * y + c)
            return 0

        for n in range(4):
            na.arrived(n, to)
            nb.arrived(piece, n)
        lax.fori_loop(0, 2, one, 0)

    own_pair(0)
    pan.pass_x()
    for n in range(4):
        na.two[n].forward()
    for n in (1, 2, 3):
        nb.near(n)
    pan.start_z()
    loss.start_z()
    for n in (1, 2, 3):
        nb.far(n)
    for n in range(4):
        na.near(n)
    own_pair(3)
    for n in range(4):
        na.far(n)
    own_pair(1)
    pan.start_gather()
    loss.start_s()
    own_pair(2)
    grad_ref[0, :, :half] = acc[0]
    grad_ref[0, :, half:] = acc[1]
    pan.wait_z()
    for pair in zip(lane_a.steps(), lane_b.steps()):
        for step_of in pair:
            step_of()
    total_ref[...] = loss.total()
    lane_a.wait_core()
    lane_b.wait_core()
    for q in (ev, out, neg, na, nb, pan, lane_a, lane_b, loss):
        q.wait_sends()


def scatter_kernel(n_item, scale, panel_all, neg_ref, owner_ref, total_ref, table_ref, loss_ref, buf, sem):
    item = lax.axis_index("item")
    rows = table_ref.shape[0]
    panel = neg_ref.shape[1]
    half = buf.shape[3]
    def fetch(p):
        return pltpu.make_async_copy(
            panel_all.at[:, pl.ds(p * panel, panel), :], buf.at[p], sem.at[p]
        )

    for p in range(neg_ref.shape[0]):
        pl.when(owner_ref[p] == item)(fetch(p).start)
    table_ref[...] = jnp.zeros_like(table_ref)
    loss_ref[0, 0] = jnp.max(total_ref[...]) * scale
    for p in range(neg_ref.shape[0]):

        @pl.when(owner_ref[p] == item)
        def _():
            spot = lax.broadcasted_iota(jnp.int32, (rows, panel), 0)
            pick = jnp.where(spot == neg_ref[pl.ds(p, 1), :], 1.0, 0.0).astype(bf16)
            fetch(p).wait()
            for k in (0, 1):
                hi, lo = split(buf[p, k])
                table_ref[:, k * half:(k + 1) * half] += mm(pick, hi) + mm(pick, lo)


def params(cid=None):
    if cid is None:
        return pltpu.CompilerParams(vmem_limit_bytes=VMEM_LIMIT)
    return pltpu.CompilerParams(
        vmem_limit_bytes=VMEM_LIMIT, collective_id=cid, has_side_effects=True
    )


def per_device(
    n_seq, n_item, events, w_uvqk, out_gain, w_out, item_table,
    user_lengths, neg_ids, panel_owner, block_mask, targets,
):
    _, tok, D = events.shape
    X, Z, Y = X_RING, n_item // X_RING, n_seq // 2
    n_neg = neg_ids.shape[0] * neg_ids.shape[1]
    share = n_neg // n_seq
    R = share // n_item
    half = D // 2
    shape = jax.ShapeDtypeStruct

    aug = tok + 16
    step = 2 * tok
    full = (2, Y, 2, X, Z * R, half)
    one = pltpu.SemaphoreType.DMA
    event_grad, panel_all, total = pl.pallas_call(
        functools.partial(main_kernel, n_seq, n_item),
        out_shape=(shape(events.shape, f32), shape(full, f32), shape((8, 128), f32)),
        in_specs=[ANY, ANY, VM, ANY, ANY, VM, VM, VM, VM, VM], out_specs=(VM, ANY, VM),
        scratch_shapes=[
            pltpu.VMEM((n_seq, tok, D), f32), pltpu.VMEM(full, f32),
            pltpu.VMEM((n_seq, aug, D), f32), pltpu.VMEM(item_table.shape, f32),
            pltpu.VMEM(w_uvqk.shape, f32), pltpu.VMEM(w_out.shape, f32),
            pltpu.VMEM((8, D, half), bf16), pltpu.VMEM((8, D, half), bf16),
            pltpu.VMEM((4, step, half), bf16), pltpu.VMEM((4, step, half), bf16),
            pltpu.VMEM((2, tok, half), f32), pltpu.VMEM((2, tok, half), f32),
            pltpu.VMEM((2, tok, half), f32),
            pltpu.VMEM((X, Z, R, D), f32), pltpu.VMEM((X, Z, R, D), f32),
            pltpu.VMEM((2, tok, half), f32), pltpu.VMEM((share, step), f32),
            one, one, one, one,
        ] + SEQ_SEMS * 2 + reduce_scratch(X, Z, R, D) * 2 + LANE_SEMS * 4 + loss_scratch(X, Z, n_seq),
        compiler_params=params(1), name="main",
    )(events, w_uvqk, out_gain.reshape(1, D), w_out, item_table, user_lengths, neg_ids,
      panel_owner.reshape(1, -1), block_mask, targets)

    scale = 1.0 / (tok * n_seq * n_item)
    table_grad, mean_loss = pl.pallas_call(
        functools.partial(scatter_kernel, n_item, scale),
        out_shape=(shape(item_table.shape, f32), shape((1, 1), f32)),
        in_specs=[ANY, VM, SM, VM], out_specs=(VM, SM),
        scratch_shapes=[pltpu.VMEM((neg_ids.shape[0], 2, neg_ids.shape[1], half), f32), dma(neg_ids.shape[0])],
        compiler_params=params(), name="scatter",
    )(panel_all.reshape(2, n_neg, half), neg_ids, panel_owner, total)
    return (mean_loss.reshape(()), event_grad, table_grad)


def solution(mesh):
    placed = (
        P("item", "seq", None), P(), P(), P(), P("item", None), P("item", None),
        P(), P(), P("item", "seq"), P("item", "seq"),
    )
    body = functools.partial(per_device, mesh.shape["seq"], mesh.shape["item"])
    return jax.shard_map(
        body, mesh=mesh, in_specs=placed,
        out_specs=(P(), P("item", "seq", None), P("item", None)), check_vma=False,
    )
```

```python
import functools

import jax
import jax.numpy as jnp
from jax import lax
from jax.experimental import pallas as pl
from jax.experimental.pallas import tpu as pltpu
from jax.sharding import PartitionSpec as P

H = 16
X_RING = 4
beta_weight = 0.75
epsilon = 1e-05
f32, bf16 = jnp.float32, jnp.bfloat16
MESH = pl.DeviceIdType.MESH
VMEM_LIMIT = 60 * 1024 * 1024

VM = pl.BlockSpec(memory_space=pltpu.VMEM)
SM = pl.BlockSpec(memory_space=pltpu.SMEM)
ANY = pl.BlockSpec(memory_space=pl.ANY)
NN = (((1,), (0,)), ((), ()))
NT = (((1,), (1,)), ((), ()))
TN = (((0,), (0,)), ((), ()))


def split(x):
    hi = x.astype(bf16)
    return hi, (x - hi.astype(f32)).astype(bf16)


def mm(a, b, dims=NN):
    return lax.dot_general(a, b, dims, preferred_element_type=f32)


def mm3(a, b, dims=NN):
    (ah, al), (bh, bl) = a, b
    return mm(ah, bh, dims) + (mm(al, bh, dims) + mm(ah, bl, dims))


def sigmoid(x):
    return 0.5 + 0.5 * jnp.tanh(0.5 * x)


class Place:
    def __init__(self, n_seq, n_item):
        self.S, self.I = n_seq, n_item
        self.X = X_RING
        self.Z = n_item // self.X
        self.Y = n_seq // 2
        self.s = lax.axis_index("seq")
        self.i = lax.axis_index("item")
        self.y, self.c = self.s // 2, self.s % 2
        self.z, self.x = self.i // self.X, self.i % self.X

    def at_x(self, x):
        return (self.s, self.z * self.X + x)

    def at_z(self, z):
        return (self.s, z * self.X + self.x)

    def at_y(self, y):
        return (2 * y + self.c, self.i)

    def at_s(self, s):
        return (s, self.i)

    def partner(self):
        return (2 * self.y + 1 - self.c, self.i)


def rdma(src, dst, send, recv, dev):
    return pltpu.make_async_remote_copy(
        src_ref=src, dst_ref=dst, send_sem=send, recv_sem=recv, device_id=dev, device_id_type=MESH
    )


class Ring4:
    def __init__(self, me, dev, part, send, recv, causal=False):
        self.me, self.dev, self.part, self.causal = me, dev, part, causal
        self.send, self.recv = send, recv
        self.right, self.left = (me + 1) % 4, (me + 3) % 4
        self.opp = (me + 2) % 4

    def _c(self, slot, src, k, h, to):
        return rdma(src, self.part(k, h), self.send.at[slot], self.recv.at[slot], self.dev(to))

    def start(self):
        me = self.me
        self.r = [self._c(h, self.part(me, h), me, h, self.right) for h in (0, 1)]
        self.l1 = self._c(3, self.part(me, 1), me, 1, self.left)
        self.r[0].start()
        self.l1.start()
        self.r[1].start()
        self.l = [self.l1]
        if not self.causal:
            self.l.append(self._c(2, self.part(me, 0), me, 0, self.left))
            self.l[1].start()

    def forward_right(self):
        self.r[0].wait_recv()
        self.fr = self._c(4, self.part(self.left, 0), self.left, 0, self.right)
        self.fr.start()

    def forward_left(self):
        self.l1.wait_recv()
        self.fl = self._c(5, self.part(self.right, 1), self.right, 1, self.left)
        self.fl.start()

    def forward(self):
        self.forward_right()
        self.forward_left()

    def wait_left(self):
        self.r[1].wait_recv()

    def wait_right(self):
        self.l[1].wait_recv()

    def wait_opp(self):
        self.fr.wait_recv()
        self.fl.wait_recv()

    def wait_sends(self):
        for c in (*self.r, *self.l, self.fr, self.fl):
            c.wait_send()


class CoreSends:
    def __init__(self, dev, send, recv):
        self.dev, self.send, self.recv, self.copies = dev, send, recv, []

    def push(self, src, dst):
        n = len(self.copies)
        c = rdma(src, dst, self.send.at[n], self.recv.at[n], self.dev)
        c.start()
        self.copies.append(c)

    def wait_recv(self, n):
        self.copies[n].wait_recv()

    def wait_sends(self):
        for c in self.copies:
            c.wait_send()


def enter(devs):
    barrier = pltpu.get_barrier_semaphore()
    for d in devs:
        pl.semaphore_signal(barrier, inc=1, device_id=d, device_id_type=MESH)
    return lambda: pl.semaphore_wait(barrier, len(devs))


def seq_peers(pc):
    return [pc.at_s((pc.s + d) % pc.S) for d in range(1, pc.S)]


def plane_peers(pc):
    xs = [pc.at_x((pc.x + d) % pc.X) for d in range(1, pc.X)]
    zs = [pc.at_z((pc.z + d) % pc.Z) for d in range(1, pc.Z)]
    return xs + zs


class SeqGather:
    def __init__(self, pc, full, sems, causal=False):
        send, recv, csend, crecv = sems
        half = full.shape[1] // 2
        self.pc, self.full, self.causal = pc, full, causal
        part = lambda y, h: full.at[2 * y + pc.c, pl.ds(h * half, half)]
        self.ring = Ring4(pc.y, pc.at_y, part, send, recv, causal)
        self.core = CoreSends(pc.partner(), csend, crecv)

    def push(self, y):
        blk = self.full.at[2 * y + self.pc.c]
        self.core.push(blk, blk)

    def start(self):
        self.ring.start()
        self.push(self.pc.y)

    def forward(self):
        self.ring.forward()

    def near(self):
        r = self.ring
        r.wait_left()
        self.push(r.left)
        if not self.causal:
            r.wait_right()
            self.push(r.right)

    def far(self):
        self.ring.wait_opp()
        self.push(self.ring.opp)

    def pair(self, n):
        self.core.wait_recv(n)

    def wait_sends(self):
        self.ring.wait_sends()
        self.core.wait_sends()


def dma(n):
    return pltpu.SemaphoreType.DMA((n,))


SEQ_SEMS = [dma(6), dma(6), dma(4), dma(4)]


class Reduce:
    def __init__(self, pc, part, full, refs):
        self.pc, self.part, self.full = pc, part, full
        (self.rx, self.mid, self.sx, self.rz, self.own, self.xs, self.xr,
         self.zs, self.zr, self.gs, self.gr, self.lsem) = refs
        self.hz = part.shape[1] // 2
        self.right, self.left = (pc.x + 1) % 4, (pc.x + 3) % 4
        self.opp = (pc.x + 2) % 4

    def _half(self, k, h):
        return self.part.at[k, pl.ds(h * self.hz, self.hz)]

    def _x(self, slot, src, to):
        c = rdma(src, self.rx.at[slot], self.xs.at[slot], self.xr.at[slot], self.pc.at_x(to))
        c.start()
        self.cx.append(c)

    def start_x(self):
        self.cx = []
        self._x(0, self._half(self.opp, 0), self.right)
        self._x(1, self._half(self.opp, 1), self.left)
        self._x(2, self._half(self.right, 1), self.right)
        self._x(3, self._half(self.left, 0), self.left)

    def pass_x(self):
        h = self.hz
        self.cx[0].wait_recv()
        self.mid[0] = self.part[self.right, :h] + self.rx[0]
        self._x(4, self.mid.at[0], self.right)
        self.cx[1].wait_recv()
        self.mid[1] = self.part[self.left, h:] + self.rx[1]
        self._x(5, self.mid.at[1], self.left)

    def start_z(self):
        pc, h = self.pc, self.hz
        for c in self.cx[2:]:
            c.wait_recv()
        self.sx[:h] = self.part[pc.x, :h] + (self.rx[4] + self.rx[3])
        self.sx[h:] = self.part[pc.x, h:] + (self.rx[2] + self.rx[5])
        self.cz = []
        for d in range(1, pc.Z):
            to = (pc.z + d) % pc.Z
            c = rdma(self.sx.at[to], self.rz.at[d - 1], self.zs.at[d - 1], self.zr.at[d - 1], pc.at_z(to))
            c.start()
            self.cz.append(c)

    def start_gather(self):
        pc = self.pc
        total = self.sx[pc.z]
        for c in self.cz:
            c.wait_recv()
        for d in range(pc.Z - 1):
            total = total + self.rz[d]
        half = total.shape[1] // 2
        rows = total.shape[0]
        self.own[0] = total[:, :half]
        self.own[1] = total[:, half:]
        mine = self.full.at[:, pc.y, pc.c, pc.x, pl.ds(pl.multiple_of(pc.z * rows, rows), rows), :]
        self.local = pltpu.make_async_copy(self.own, mine, self.lsem)
        self.local.start()
        self.cg = []
        for d in range(1, pc.Z):
            to = (pc.z + d) % pc.Z
            c = rdma(self.own, mine, self.gs.at[d - 1], self.gr.at[d - 1], pc.at_z(to))
            c.start()
            self.cg.append(c)

    def wait_z(self):
        for c in self.cg:
            c.wait_recv()
        self.local.wait()

    def wait_sends(self):
        for c in (*self.cx, *self.cz, *self.cg):
            c.wait_send()


def reduce_scratch(X, Z, R, D):
    nz = max(Z - 1, 1)
    return [
        pltpu.VMEM((6, Z // 2, R, D), f32),
        pltpu.VMEM((2, Z // 2, R, D), f32),
        pltpu.VMEM((Z, R, D), f32),
        pltpu.VMEM((nz, R, D), f32),
        pltpu.VMEM((2, R, D // 2), f32),
        dma(6), dma(6), dma(nz), dma(nz), dma(nz), dma(nz), pltpu.SemaphoreType.DMA,
    ]


N_REDUCE = 12


class SpreadXY:
    def __init__(self, pc, full, sems):
        xs, xr, ys, yr, cs, cr = sems
        self.pc, self.full = pc, full
        self.rx = Ring4(pc.x, pc.at_x, lambda k, h: full.at[h, pc.y, pc.c, k], xs, xr)
        self.ry = Ring4(pc.y, pc.at_y, lambda k, h: full.at[h, k, pc.c], ys, yr)
        self.core = CoreSends(pc.partner(), cs, cr)

    def push(self, k):
        blk = self.full.at[:, k, self.pc.c]
        self.core.push(blk, blk)

    def x_wait(self):
        self.rx.wait_left()
        self.rx.wait_right()
        self.rx.wait_opp()

    def y_start(self):
        self.ry.start()

    def near(self):
        self.ry.wait_left()
        self.push(self.ry.left)
        self.ry.wait_right()
        self.push(self.ry.right)

    def far(self):
        self.ry.wait_opp()
        self.push(self.ry.opp)

    def wait_sends(self):
        for q in (self.rx, self.ry, self.core):
            q.wait_sends()


SPREAD_XY_SEMS = [dma(6), dma(6), dma(6), dma(6), dma(4), dma(4)]


class Lane:
    def __init__(self, pc, first, second, blk, sems):
        (f, fdev), (g, gdev) = first, second
        self.f, self.g, self.blk = f, g, blk
        rows = blk(0, 0).shape[0] // 2
        part = lambda ref, h: ref.at[pl.ds(h * rows, rows), :]
        self.one = Ring4(f, fdev, lambda k, h: part(blk(k, g), h), sems[0], sems[1])
        self.two = []
        for n, k in enumerate((f, (f + 3) % 4, (f + 1) % 4, (f + 2) % 4)):
            ring = Ring4(
                g, gdev, lambda j, h, k=k: part(blk(k, j), h), sems[2 + 2 * n], sems[3 + 2 * n]
            )
            ring.piece = k
            self.two.append(ring)
        self.core = CoreSends(pc.partner(), sems[10], sems[11])

    def push(self, k, j):
        self.core.push(self.blk(k, j), self.blk(k, j))

    def begin(self, n):
        ring = self.two[n]
        ring.start()
        self.push(ring.piece, self.g)

    def near(self, n):
        ring = self.two[n]
        ring.wait_left()
        self.push(ring.piece, ring.left)
        ring.wait_right()
        self.push(ring.piece, ring.right)

    def far(self, n):
        ring = self.two[n]
        ring.wait_opp()
        self.push(ring.piece, ring.opp)

    def steps(self):
        one, two = self.one, self.two
        return [
            lambda: (one.start(), self.begin(0)),
            lambda: one.forward(),
            lambda: (one.wait_left(), self.begin(1)),
            lambda: (one.wait_right(), self.begin(2)),
            lambda: two[0].forward(),
            lambda: (one.wait_opp(), self.begin(3)),
            lambda: two[1].forward(),
            lambda: two[2].forward(),
            lambda: self.near(0),
            lambda: two[3].forward(),
            lambda: self.near(1),
            lambda: self.near(2),
            lambda: self.far(0),
            lambda: self.near(3),
            lambda: self.far(1),
            lambda: self.far(2),
            lambda: self.far(3),
        ]

    def wait_core(self):
        for n in range(16):
            self.core.wait_recv(n)

    def wait_sends(self):
        for q in (self.one, *self.two, self.core):
            q.wait_sends()


LANE_SEMS = [dma(6)] * 10 + [dma(16)] * 2


class LossSum:
    def __init__(self, pc, refs):
        self.pc = pc
        (self.t0, self.lx, self.tx, self.lz, self.tz, self.ls,
         self.xs, self.xr, self.zs, self.zr, self.ss, self.sr) = refs
        self.all = []

    def _send(self, src, dst, send, recv, devs):
        out = []
        for d, dev in enumerate(devs):
            c = rdma(src, dst.at[d], send.at[d], recv.at[d], dev)
            c.start()
            out.append(c)
        self.all += out
        return out

    def start_x(self):
        pc = self.pc
        devs = [pc.at_x((pc.x + d) % pc.X) for d in range(1, pc.X)]
        self.c = self._send(self.t0, self.lx, self.xs, self.xr, devs)

    def _sum(self, own, got, n):
        for c in self.c:
            c.wait_recv()
        total = own[...]
        for d in range(n):
            total = total + got[d]
        return total

    def start_z(self):
        pc = self.pc
        self.tx[...] = self._sum(self.t0, self.lx, pc.X - 1)
        devs = [pc.at_z((pc.z + d) % pc.Z) for d in range(1, pc.Z)]
        self.c = self._send(self.tx, self.lz, self.zs, self.zr, devs)

    def start_s(self):
        pc = self.pc
        self.tz[...] = self._sum(self.tx, self.lz, pc.Z - 1)
        self.c = self._send(self.tz, self.ls, self.ss, self.sr, seq_peers(pc))

    def total(self):
        return self._sum(self.tz, self.ls, self.pc.S - 1)

    def wait_sends(self):
        for c in self.all:
            c.wait_send()


def loss_scratch(X, Z, S):
    nz = max(Z - 1, 1)
    tile = lambda *n: pltpu.VMEM((*n, 8, 128), f32)
    return [
        tile(), tile(X - 1), tile(), tile(nz), tile(), tile(S - 1),
        dma(X - 1), dma(X - 1), dma(nz), dma(nz), dma(S - 1), dma(S - 1),
    ]


N_LOSS = 12


def loss_core(logits, target, live):
    m = jnp.where(target, -logits, logits)
    w = jnp.where(target, -beta_weight, live)
    e = jnp.exp(-jnp.abs(m))
    sig = jnp.where(m >= 0.0, 1.0, e) / (1.0 + e)
    return w * sig, jnp.abs(w), jnp.maximum(m, 0.0) + jnp.log1p(e)


def main_kernel(
    n_seq, n_item, ev_ref, w_ref, gain_ref, wo_ref, table_ref, lens_ref, neg_ref, owner_ref,
    msk_ref, tgt_ref, grad_ref, panel_all, total_ref, *scratch,
):
    pc = Place(n_seq, n_item)
    (ev_all, neg_all, out_all, table, w, wo, wh, wl, kvh, kvl, qs, gates, att, part, panel,
     acc, loss_acc, s_ev, s_table, s_w, s_wo) = scratch[:21]
    rest = scratch[21:]
    ev = SeqGather(pc, ev_all, rest[:4], causal=True)
    out = SeqGather(pc, out_all, rest[4:8])
    rest = rest[8:]
    neg = Reduce(pc, part, neg_all, rest[:N_REDUCE])
    pan = Reduce(pc, panel, panel_all, rest[N_REDUCE:2 * N_REDUCE])
    rest = rest[2 * N_REDUCE:]
    spread = SpreadXY(pc, neg_all, rest[:6])
    along_x, along_y = (pc.x, pc.at_x), (pc.y, pc.at_y)
    lane_a = Lane(pc, along_x, along_y, lambda k, j: panel_all.at[0, j, pc.c, k], rest[6:18])
    lane_b = Lane(pc, along_y, along_x, lambda k, j: panel_all.at[1, k, pc.c, j], rest[18:30])
    loss = LossSum(pc, rest[30:])

    tok, D = grad_ref.shape[1], grad_ref.shape[2]
    half = D // 2
    step = 2 * tok
    rows = table.shape[0]
    X, Z, R = part.shape[0], part.shape[1], part.shape[2]
    share = X * Z * R
    hd = D // H
    hpg = 128 // hd

    ready = enter(plane_peers(pc) + seq_peers(pc))
    c_ev = pltpu.make_async_copy(ev_ref.at[0], ev_all.at[pc.s], s_ev)
    c_table = pltpu.make_async_copy(table_ref, table, s_table)
    c_w = pltpu.make_async_copy(w_ref, w, s_w)
    c_wo = pltpu.make_async_copy(wo_ref, wo, s_wo)
    for c in (c_ev, c_table, c_w, c_wo):
        c.start()

    per_panel = neg_ref.shape[1] // share
    p = pc.s // per_panel
    first = pl.multiple_of((pc.s % per_panel) * share, share)
    slot = lax.broadcasted_iota(jnp.int32, owner_ref.shape, 1)
    owner = jnp.sum(jnp.where(slot == p, owner_ref[...], 0), axis=1, keepdims=True)
    ids = neg_ref[pl.ds(p, 1), pl.ds(first, share)] + rows * jnp.broadcast_to(owner, (1, share))
    spot = pc.i * rows + lax.broadcasted_iota(jnp.int32, (rows, share), 0)
    pick = jnp.where(spot == jnp.broadcast_to(ids, spot.shape), 1.0, 0.0).astype(bf16)
    c_table.wait()
    hi, lo = split(table[...])
    part[...] = (mm(pick, hi, TN) + mm(pick, lo, TN)).reshape(part.shape)
    c_ev.wait()
    ready()
    ev.start()
    neg.start_x()

    c_w.wait()

    def split_w(n, _):
        wh[n], wl[n] = split(w[:, pl.ds(pl.multiple_of(n * half, half), half)])
        return 0

    lax.fori_loop(0, 8, split_w, 0)
    x_own = ev_all[pc.s]
    xo = split(x_own)

    def project(xs, n):
        r = mm3(xs, (wh[n], wl[n]))
        return r * sigmoid(r)

    for n in range(2):
        qs[n] = project(xo, 4 + n)
        gates[n] = project(xo, n)
    neg.pass_x()

    lane_head = lax.broadcasted_iota(jnp.int32, (tok, 128), 1) // hd
    sub = lax.broadcasted_iota(jnp.int32, (tok, tok), 0)
    lane = lax.broadcasted_iota(jnp.int32, (tok, tok), 1)
    row = pc.s * tok + sub
    begin = jnp.zeros((tok, tok), jnp.int32)
    end = jnp.zeros((1, 1), jnp.int32)
    for u in range(lens_ref.shape[1]):
        end = end + lens_ref[0:1, u:u + 1]
        wide = jnp.broadcast_to(end, row.shape)
        begin = jnp.where(row >= wide, wide, begin)

    def stacked(m, lanes):
        q = qs[m][:, lanes]
        parts = [jnp.where(lane_head == h, q, 0.0) for h in range(hpg)]
        return split(jnp.concatenate(parts, axis=0))

    def collect(m, lanes, o, base):
        got = base
        for h in range(hpg):
            got = got + jnp.where(lane_head == h, o[h * tok:(h + 1) * tok], 0.0)
        att[m, :, lanes] = got

    def weigh(sc, allow):
        pr = (sc * sigmoid(sc)).reshape(hpg, tok, sc.shape[1]) * allow[None]
        return split(pr.reshape(sc.shape))

    def keys_values(xs, n_rows):
        def kv_step(n, _):
            hi, lo = split(project(xs, jnp.where(n < 2, 2 + n, 4 + n)))
            kvh[n, :n_rows], kvl[n, :n_rows] = hi, lo
            return 0

        lax.fori_loop(0, 4, kv_step, 0)

    def attend_own():
        keys_values(xo, tok)
        ev.forward()
        allow = jnp.where((lane <= sub) & (pc.s * tok + lane >= begin), 1.0, 0.0)

        def heads(m, _):
            for g in range(half // 128):
                lanes = slice(g * 128, (g + 1) * 128)
                kh, kl = kvh[2 + m, :tok, lanes], kvl[2 + m, :tok, lanes]
                vh, vl = kvh[m, :tok, lanes], kvl[m, :tok, lanes]
                both = jnp.concatenate(stacked(m, lanes), axis=1)
                kk = jnp.concatenate([kh, kh], axis=1)
                k0 = jnp.concatenate([kl, jnp.zeros_like(kl)], axis=1)
                sc = mm(both, jnp.concatenate([kk, k0], axis=0), NT)
                pp = jnp.concatenate(weigh(sc[:, :tok] + sc[:, tok:], allow), axis=1)
                vv = jnp.concatenate([vh, vl], axis=1)
                o = mm(pp, jnp.concatenate([vv, vv], axis=0))
                collect(m, lanes, o[:, :128] + o[:, 128:], jnp.zeros((tok, 128), f32))
            return 0

        lax.fori_loop(0, 2, heads, 0)

    def attend(back, between):
        blocks = [(pc.s + pc.S - back - d) % pc.S for d in (0, 1)]
        keys_values(split(jnp.concatenate([ev_all[b] for b in blocks], axis=0)), step)
        between()
        cols = [b * tok + lane for b in blocks]
        allow = [jnp.where((c >= begin) & (c <= row), 1.0, 0.0) for c in cols]
        allow = jnp.concatenate(allow, axis=1)

        def heads(m, _):
            for g in range(half // 128):
                lanes = slice(g * 128, (g + 1) * 128)
                kh, kl = kvh[2 + m][:, lanes], kvl[2 + m][:, lanes]
                vh, vl = kvh[m][:, lanes], kvl[m][:, lanes]
                qh, ql = stacked(m, lanes)
                two = jnp.concatenate([qh, ql], axis=1)
                sc = mm(two, jnp.concatenate([kh, kh], axis=1), NT) + mm(qh, kl, NT)
                ph, plo = weigh(sc, allow)
                o = mm(ph, jnp.concatenate([vh, vl], axis=1))
                o = (o[:, :128] + o[:, 128:]) + mm(plo, vh)
                collect(m, lanes, o, att[m, :, lanes])
            return 0

        lax.fori_loop(0, 2, heads, 0)

    attend_own()
    ev.near()
    neg.start_z()
    ev.pair(0)
    ev.pair(1)
    attend(1, lambda: None)
    ev.far()
    neg.start_gather()
    ev.pair(2)
    attend(3, lambda: None)
    neg.wait_z()
    spread.rx.start()

    a = jnp.concatenate([att[0], att[1]], axis=1)
    centered = a - jnp.mean(a, axis=1, keepdims=True)
    var = jnp.mean(centered * centered, axis=1, keepdims=True)
    normed = centered * lax.rsqrt(var + epsilon) * gain_ref[...]
    gated = normed * jnp.concatenate([gates[0], gates[1]], axis=1)
    c_wo.wait()
    o_own = x_own + mm3(split(gated), split(wo[...]))
    pad = out_all.shape[1] - tok
    out_all[pc.s, :tok, :] = o_own
    out_all[pc.s, tok:, :] = jnp.zeros((pad, D), f32)
    out_all[pc.s, tok:tok + 1, :tok] = tgt_ref[...].astype(f32)
    out_all[pc.s, tok:tok + 1, tok:step] = jnp.broadcast_to(msk_ref[...], (1, tok)).astype(f32)
    out.start()
    spread.rx.forward()
    out.forward()
    spread.x_wait()
    spread.push(pc.y)

    m0 = split(neg_all[0, pc.y, pc.c].reshape(share, half))
    m1 = split(neg_all[1, pc.y, pc.c].reshape(share, half))
    column = pc.s * share + lax.broadcasted_iota(jnp.int32, (share, step), 0)
    panel[...] = jnp.zeros_like(panel)
    loss_acc[...] = jnp.zeros_like(loss_acc)

    def own_columns(y):
        pair = [out_all[2 * y], out_all[2 * y + 1]]
        ob = jnp.concatenate([q[:tok] for q in pair], axis=0)
        tg = jnp.concatenate([q[tok:tok + 1, :tok] for q in pair], axis=1).astype(jnp.int32)
        mk = jnp.concatenate([q[tok:tok + 1, tok:step] for q in pair], axis=1).astype(jnp.int32)
        obh, obl = split(ob)
        logits = mm3(m0, (obh[:, :half], obl[:, :half]), NT)
        logits = logits + mm3(m1, (obh[:, half:], obl[:, half:]), NT)
        bits = jnp.right_shift(jnp.broadcast_to(mk, column.shape), column // 128) & 1
        g, wt, sp = loss_core(logits, column == jnp.broadcast_to(tg, column.shape), bits.astype(f32))
        loss_acc[...] += wt * sp
        panel[...] += mm3(split(g), (obh, obl)).reshape(panel.shape)

    out.pair(0)
    own_columns(pc.y)
    out.near()
    out.pair(1)
    own_columns(out.ring.left)
    out.far()
    spread.y_start()
    out.pair(2)
    own_columns(out.ring.right)
    out.pair(3)
    own_columns(out.ring.opp)
    pan.start_x()
    loss.t0[...] = jnp.broadcast_to(jnp.sum(loss_acc[...]), loss.t0.shape)
    loss.start_x()

    mine = out_all[pc.s]
    oh = [split(mine[:tok, k * half:(k + 1) * half]) for k in (0, 1)]
    tcol = jnp.transpose(jnp.broadcast_to(mine[tok:tok + 1, :tok], (tok, tok)))
    tcol = jnp.concatenate([tcol, tcol], axis=1).astype(jnp.int32)
    mcol = jnp.broadcast_to(mine[tok:tok + 1, tok:tok + 1], (tok, step)).astype(jnp.int32)
    acc[...] = jnp.zeros_like(acc)

    lane2 = lax.broadcasted_iota(jnp.int32, (tok, step), 1)

    def own_tokens(j):
        n0 = split(neg_all[0, j // 2, j % 2].reshape(share, half))
        n1 = split(neg_all[1, j // 2, j % 2].reshape(share, half))
        logits = mm3(oh[0], n0, NT) + mm3(oh[1], n1, NT)
        live = (jnp.right_shift(mcol, 2 * j + lane2 // 128) & 1).astype(f32)
        g, _, _ = loss_core(logits, lane2 + j * share == tcol, live)
        gs = split(g)
        acc[0] += mm3(gs, n0)
        acc[1] += mm3(gs, n1)

    def own_pair(n, y):
        def one(c, _):
            own_tokens(2 * y + c)
            return 0

        spread.core.wait_recv(n)
        lax.fori_loop(0, 2, one, 0)

    own_pair(0, pc.y)
    pan.pass_x()
    spread.ry.forward()
    pan.start_z()
    loss.start_z()
    pan.start_gather()
    loss.start_s()
    spread.near()
    own_pair(1, spread.ry.left)
    own_pair(2, spread.ry.right)
    pan.wait_z()
    steps = list(zip(lane_a.steps(), lane_b.steps()))
    for n, pair in enumerate(steps):
        for step_of in pair:
            step_of()
        if n == 0:
            spread.far()
            own_pair(3, spread.ry.opp)
            grad_ref[0, :, :half] = acc[0]
            grad_ref[0, :, half:] = acc[1]
    total_ref[...] = loss.total()
    lane_a.wait_core()
    lane_b.wait_core()
    for q in (ev, out, neg, pan, spread, lane_a, lane_b, loss):
        q.wait_sends()


def scatter_kernel(n_item, scale, panel_all, neg_ref, owner_ref, total_ref, table_ref, loss_ref, buf, sem):
    item = lax.axis_index("item")
    rows = table_ref.shape[0]
    panel = neg_ref.shape[1]
    half = buf.shape[3]
    def fetch(p):
        return pltpu.make_async_copy(
            panel_all.at[:, pl.ds(p * panel, panel), :], buf.at[p], sem.at[p]
        )

    for p in range(neg_ref.shape[0]):
        pl.when(owner_ref[p] == item)(fetch(p).start)
    table_ref[...] = jnp.zeros_like(table_ref)
    loss_ref[0, 0] = jnp.max(total_ref[...]) * scale
    for p in range(neg_ref.shape[0]):

        @pl.when(owner_ref[p] == item)
        def _():
            spot = lax.broadcasted_iota(jnp.int32, (rows, panel), 0)
            pick = jnp.where(spot == neg_ref[pl.ds(p, 1), :], 1.0, 0.0).astype(bf16)
            fetch(p).wait()
            for k in (0, 1):
                hi, lo = split(buf[p, k])
                table_ref[:, k * half:(k + 1) * half] += mm(pick, hi) + mm(pick, lo)


def params(cid=None):
    if cid is None:
        return pltpu.CompilerParams(vmem_limit_bytes=VMEM_LIMIT)
    return pltpu.CompilerParams(
        vmem_limit_bytes=VMEM_LIMIT, collective_id=cid, has_side_effects=True
    )


def per_device(
    n_seq, n_item, events, w_uvqk, out_gain, w_out, item_table,
    user_lengths, neg_ids, panel_owner, block_mask, targets,
):
    _, tok, D = events.shape
    X, Z, Y = X_RING, n_item // X_RING, n_seq // 2
    n_neg = neg_ids.shape[0] * neg_ids.shape[1]
    share = n_neg // n_seq
    R = share // n_item
    half = D // 2
    shape = jax.ShapeDtypeStruct

    aug = tok + 16
    step = 2 * tok
    full = (2, Y, 2, X, Z * R, half)
    one = pltpu.SemaphoreType.DMA
    event_grad, panel_all, total = pl.pallas_call(
        functools.partial(main_kernel, n_seq, n_item),
        out_shape=(shape(events.shape, f32), shape(full, f32), shape((8, 128), f32)),
        in_specs=[ANY, ANY, VM, ANY, ANY, VM, VM, VM, VM, VM], out_specs=(VM, ANY, VM),
        scratch_shapes=[
            pltpu.VMEM((n_seq, tok, D), f32), pltpu.VMEM(full, f32),
            pltpu.VMEM((n_seq, aug, D), f32), pltpu.VMEM(item_table.shape, f32),
            pltpu.VMEM(w_uvqk.shape, f32), pltpu.VMEM(w_out.shape, f32),
            pltpu.VMEM((8, D, half), bf16), pltpu.VMEM((8, D, half), bf16),
            pltpu.VMEM((4, step, half), bf16), pltpu.VMEM((4, step, half), bf16),
            pltpu.VMEM((2, tok, half), f32), pltpu.VMEM((2, tok, half), f32),
            pltpu.VMEM((2, tok, half), f32),
            pltpu.VMEM((X, Z, R, D), f32), pltpu.VMEM((X, Z, R, D), f32),
            pltpu.VMEM((2, tok, half), f32), pltpu.VMEM((share, step), f32),
            one, one, one, one,
        ] + SEQ_SEMS * 2 + reduce_scratch(X, Z, R, D) * 2 + SPREAD_XY_SEMS + LANE_SEMS * 2 + loss_scratch(X, Z, n_seq),
        compiler_params=params(1), name="main",
    )(events, w_uvqk, out_gain.reshape(1, D), w_out, item_table, user_lengths, neg_ids,
      panel_owner.reshape(1, -1), block_mask, targets)

    scale = 1.0 / (tok * n_seq * n_item)
    table_grad, mean_loss = pl.pallas_call(
        functools.partial(scatter_kernel, n_item, scale),
        out_shape=(shape(item_table.shape, f32), shape((1, 1), f32)),
        in_specs=[ANY, VM, SM, VM], out_specs=(VM, SM),
        scratch_shapes=[pltpu.VMEM((neg_ids.shape[0], 2, neg_ids.shape[1], half), f32), dma(neg_ids.shape[0])],
        compiler_params=params(), name="scatter",
    )(panel_all.reshape(2, n_neg, half), neg_ids, panel_owner, total)
    return (mean_loss.reshape(()), event_grad, table_grad)


def solution(mesh):
    placed = (
        P("item", "seq", None), P(), P(), P(), P("item", None), P("item", None),
        P(), P(), P("item", "seq"), P("item", "seq"),
    )
    body = functools.partial(per_device, mesh.shape["seq"], mesh.shape["item"])
    return jax.shard_map(
        body, mesh=mesh, in_specs=placed,
        out_specs=(P(), P("item", "seq", None), P("item", None)), check_vma=False,
    )
```

```python
import functools

import jax
import jax.numpy as jnp
from jax import lax
from jax.experimental import pallas as pl
from jax.experimental.pallas import tpu as pltpu
from jax.sharding import PartitionSpec as P

H = 16
X_RING = 4
beta_weight = 0.75
epsilon = 1e-05
f32, bf16 = jnp.float32, jnp.bfloat16
MESH = pl.DeviceIdType.MESH
VMEM_LIMIT = 60 * 1024 * 1024

VM = pl.BlockSpec(memory_space=pltpu.VMEM)
SM = pl.BlockSpec(memory_space=pltpu.SMEM)
ANY = pl.BlockSpec(memory_space=pl.ANY)
NN = (((1,), (0,)), ((), ()))
NT = (((1,), (1,)), ((), ()))
TN = (((0,), (0,)), ((), ()))


def split(x):
    hi = x.astype(bf16)
    return hi, (x - hi.astype(f32)).astype(bf16)


def mm(a, b, dims=NN):
    return lax.dot_general(a, b, dims, preferred_element_type=f32)


def mm3(a, b, dims=NN):
    (ah, al), (bh, bl) = a, b
    return mm(ah, bh, dims) + (mm(al, bh, dims) + mm(ah, bl, dims))


def sigmoid(x):
    return 0.5 + 0.5 * jnp.tanh(0.5 * x)


class Place:
    def __init__(self, n_seq, n_item):
        self.S, self.I = n_seq, n_item
        self.X = X_RING
        self.Z = n_item // self.X
        self.Y = n_seq // 2
        self.s = lax.axis_index("seq")
        self.i = lax.axis_index("item")
        self.y, self.c = self.s // 2, self.s % 2
        self.z, self.x = self.i // self.X, self.i % self.X

    def at_x(self, x):
        return (self.s, self.z * self.X + x)

    def at_z(self, z):
        return (self.s, z * self.X + self.x)

    def at_y(self, y):
        return (2 * y + self.c, self.i)

    def at_s(self, s):
        return (s, self.i)

    def partner(self):
        return (2 * self.y + 1 - self.c, self.i)


def rdma(src, dst, send, recv, dev):
    return pltpu.make_async_remote_copy(
        src_ref=src, dst_ref=dst, send_sem=send, recv_sem=recv, device_id=dev, device_id_type=MESH
    )


class Ring4:
    def __init__(self, me, dev, part, send, recv, causal=False):
        self.me, self.dev, self.part, self.causal = me, dev, part, causal
        self.send, self.recv = send, recv
        self.right, self.left = (me + 1) % 4, (me + 3) % 4
        self.opp = (me + 2) % 4

    def _c(self, slot, src, k, h, to):
        return rdma(src, self.part(k, h), self.send.at[slot], self.recv.at[slot], self.dev(to))

    def start(self):
        me = self.me
        self.r = [self._c(h, self.part(me, h), me, h, self.right) for h in (0, 1)]
        self.l1 = self._c(3, self.part(me, 1), me, 1, self.left)
        self.r[0].start()
        self.l1.start()
        self.r[1].start()
        self.l = [self.l1]
        if not self.causal:
            self.l.append(self._c(2, self.part(me, 0), me, 0, self.left))
            self.l[1].start()

    def forward_right(self):
        self.r[0].wait_recv()
        self.fr = self._c(4, self.part(self.left, 0), self.left, 0, self.right)
        self.fr.start()

    def forward_left(self):
        self.l1.wait_recv()
        self.fl = self._c(5, self.part(self.right, 1), self.right, 1, self.left)
        self.fl.start()

    def forward(self):
        self.forward_right()
        self.forward_left()

    def wait_left(self):
        self.r[1].wait_recv()

    def wait_right(self):
        self.l[1].wait_recv()

    def wait_opp(self):
        self.fr.wait_recv()
        self.fl.wait_recv()

    def wait_sends(self):
        for c in (*self.r, *self.l, self.fr, self.fl):
            c.wait_send()


class CoreSends:
    def __init__(self, dev, send, recv):
        self.dev, self.send, self.recv, self.copies = dev, send, recv, []

    def push(self, src, dst):
        n = len(self.copies)
        c = rdma(src, dst, self.send.at[n], self.recv.at[n], self.dev)
        c.start()
        self.copies.append(c)

    def wait_recv(self, n):
        self.copies[n].wait_recv()

    def wait_sends(self):
        for c in self.copies:
            c.wait_send()


def enter(devs):
    barrier = pltpu.get_barrier_semaphore()
    for d in devs:
        pl.semaphore_signal(barrier, inc=1, device_id=d, device_id_type=MESH)
    return lambda: pl.semaphore_wait(barrier, len(devs))


def seq_peers(pc):
    return [pc.at_s((pc.s + d) % pc.S) for d in range(1, pc.S)]


def plane_peers(pc):
    xs = [pc.at_x((pc.x + d) % pc.X) for d in range(1, pc.X)]
    zs = [pc.at_z((pc.z + d) % pc.Z) for d in range(1, pc.Z)]
    return xs + zs


class SeqGather:
    def __init__(self, pc, full, sems, causal=False):
        send, recv, csend, crecv = sems
        half = full.shape[1] // 2
        self.pc, self.full, self.causal = pc, full, causal
        part = lambda y, h: full.at[2 * y + pc.c, pl.ds(h * half, half)]
        self.ring = Ring4(pc.y, pc.at_y, part, send, recv, causal)
        self.core = CoreSends(pc.partner(), csend, crecv)

    def push(self, y):
        blk = self.full.at[2 * y + self.pc.c]
        self.core.push(blk, blk)

    def start(self):
        self.ring.start()
        self.push(self.pc.y)

    def forward(self):
        self.ring.forward()

    def near(self):
        r = self.ring
        r.wait_left()
        self.push(r.left)
        if not self.causal:
            r.wait_right()
            self.push(r.right)

    def far(self):
        self.ring.wait_opp()
        self.push(self.ring.opp)

    def pair(self, n):
        self.core.wait_recv(n)

    def wait_sends(self):
        self.ring.wait_sends()
        self.core.wait_sends()


def dma(n):
    return pltpu.SemaphoreType.DMA((n,))


SEQ_SEMS = [dma(6), dma(6), dma(4), dma(4)]


class Reduce:
    def __init__(self, pc, part, full, refs):
        self.pc, self.part, self.full = pc, part, full
        (self.rx, self.mid, self.sx, self.rz, self.own, self.xs, self.xr,
         self.zs, self.zr, self.gs, self.gr, self.lsem) = refs
        self.hz = part.shape[1] // 2
        self.right, self.left = (pc.x + 1) % 4, (pc.x + 3) % 4
        self.opp = (pc.x + 2) % 4

    def _half(self, k, h):
        return self.part.at[k, pl.ds(h * self.hz, self.hz)]

    def _x(self, slot, src, to):
        c = rdma(src, self.rx.at[slot], self.xs.at[slot], self.xr.at[slot], self.pc.at_x(to))
        c.start()
        self.cx.append(c)

    def start_x(self):
        self.cx = []
        self._x(0, self._half(self.opp, 0), self.right)
        self._x(1, self._half(self.opp, 1), self.left)
        self._x(2, self._half(self.right, 1), self.right)
        self._x(3, self._half(self.left, 0), self.left)

    def pass_x(self):
        h = self.hz
        self.cx[0].wait_recv()
        self.mid[0] = self.part[self.right, :h] + self.rx[0]
        self._x(4, self.mid.at[0], self.right)
        self.cx[1].wait_recv()
        self.mid[1] = self.part[self.left, h:] + self.rx[1]
        self._x(5, self.mid.at[1], self.left)

    def start_z(self):
        pc, h = self.pc, self.hz
        for c in self.cx[2:]:
            c.wait_recv()
        self.sx[:h] = self.part[pc.x, :h] + (self.rx[4] + self.rx[3])
        self.sx[h:] = self.part[pc.x, h:] + (self.rx[2] + self.rx[5])
        self.cz = []
        for d in range(1, pc.Z):
            to = (pc.z + d) % pc.Z
            c = rdma(self.sx.at[to], self.rz.at[d - 1], self.zs.at[d - 1], self.zr.at[d - 1], pc.at_z(to))
            c.start()
            self.cz.append(c)

    def start_gather(self):
        pc = self.pc
        total = self.sx[pc.z]
        for c in self.cz:
            c.wait_recv()
        for d in range(pc.Z - 1):
            total = total + self.rz[d]
        half = total.shape[1] // 2
        rows = total.shape[0]
        self.own[0] = total[:, :half]
        self.own[1] = total[:, half:]
        mine = self.full.at[:, pc.y, pc.c, pc.x, pl.ds(pl.multiple_of(pc.z * rows, rows), rows), :]
        self.local = pltpu.make_async_copy(self.own, mine, self.lsem)
        self.local.start()
        self.cg = []
        for d in range(1, pc.Z):
            to = (pc.z + d) % pc.Z
            c = rdma(self.own, mine, self.gs.at[d - 1], self.gr.at[d - 1], pc.at_z(to))
            c.start()
            self.cg.append(c)

    def wait_z(self):
        for c in self.cg:
            c.wait_recv()
        self.local.wait()

    def wait_sends(self):
        for c in (*self.cx, *self.cz, *self.cg):
            c.wait_send()


def reduce_scratch(X, Z, R, D):
    nz = max(Z - 1, 1)
    return [
        pltpu.VMEM((6, Z // 2, R, D), f32),
        pltpu.VMEM((2, Z // 2, R, D), f32),
        pltpu.VMEM((Z, R, D), f32),
        pltpu.VMEM((nz, R, D), f32),
        pltpu.VMEM((2, R, D // 2), f32),
        dma(6), dma(6), dma(nz), dma(nz), dma(nz), dma(nz), pltpu.SemaphoreType.DMA,
    ]


N_REDUCE = 12


class SpreadXY:
    def __init__(self, pc, full, sems):
        xs, xr, ys, yr, cs, cr = sems
        self.pc, self.full = pc, full
        self.rx = Ring4(pc.x, pc.at_x, lambda k, h: full.at[h, pc.y, pc.c, k], xs, xr)
        self.ry = Ring4(pc.y, pc.at_y, lambda k, h: full.at[h, k, pc.c], ys, yr)
        self.core = CoreSends(pc.partner(), cs, cr)

    def push(self, k):
        blk = self.full.at[:, k, self.pc.c]
        self.core.push(blk, blk)

    def x_wait(self):
        self.rx.wait_left()
        self.rx.wait_right()
        self.rx.wait_opp()

    def y_start(self):
        self.ry.start()

    def near(self):
        self.ry.wait_left()
        self.push(self.ry.left)
        self.ry.wait_right()
        self.push(self.ry.right)

    def far(self):
        self.ry.wait_opp()
        self.push(self.ry.opp)

    def wait_sends(self):
        for q in (self.rx, self.ry, self.core):
            q.wait_sends()


SPREAD_XY_SEMS = [dma(6), dma(6), dma(6), dma(6), dma(4), dma(4)]


class Lane:
    def __init__(self, pc, first, second, blk, sems):
        (f, fdev), (g, gdev) = first, second
        self.f, self.g, self.blk = f, g, blk
        rows = blk(0, 0).shape[0] // 2
        part = lambda ref, h: ref.at[pl.ds(h * rows, rows), :]
        self.one = Ring4(f, fdev, lambda k, h: part(blk(k, g), h), sems[0], sems[1])
        self.two = []
        for n, k in enumerate((f, (f + 3) % 4, (f + 1) % 4, (f + 2) % 4)):
            ring = Ring4(
                g, gdev, lambda j, h, k=k: part(blk(k, j), h), sems[2 + 2 * n], sems[3 + 2 * n]
            )
            ring.piece = k
            self.two.append(ring)
        self.core = CoreSends(pc.partner(), sems[10], sems[11])

    def push(self, k, j):
        self.core.push(self.blk(k, j), self.blk(k, j))

    def begin(self, n):
        ring = self.two[n]
        ring.start()
        self.push(ring.piece, self.g)

    def near(self, n):
        ring = self.two[n]
        ring.wait_left()
        self.push(ring.piece, ring.left)
        ring.wait_right()
        self.push(ring.piece, ring.right)

    def far(self, n):
        ring = self.two[n]
        ring.wait_opp()
        self.push(ring.piece, ring.opp)

    def steps(self):
        one, two = self.one, self.two
        return [
            lambda: (one.start(), self.begin(0)),
            lambda: one.forward(),
            lambda: (one.wait_left(), self.begin(1)),
            lambda: (one.wait_right(), self.begin(2)),
            lambda: two[0].forward(),
            lambda: (one.wait_opp(), self.begin(3)),
            lambda: two[1].forward(),
            lambda: two[2].forward(),
            lambda: self.near(0),
            lambda: two[3].forward(),
            lambda: self.near(1),
            lambda: self.near(2),
            lambda: self.far(0),
            lambda: self.near(3),
            lambda: self.far(1),
            lambda: self.far(2),
            lambda: self.far(3),
        ]

    def wait_core(self):
        for n in range(16):
            self.core.wait_recv(n)

    def wait_sends(self):
        for q in (self.one, *self.two, self.core):
            q.wait_sends()


LANE_SEMS = [dma(6)] * 10 + [dma(16)] * 2


class LossSum:
    def __init__(self, pc, refs):
        self.pc = pc
        (self.t0, self.lx, self.tx, self.lz, self.tz, self.ls,
         self.xs, self.xr, self.zs, self.zr, self.ss, self.sr) = refs
        self.all = []

    def _send(self, src, dst, send, recv, devs):
        out = []
        for d, dev in enumerate(devs):
            c = rdma(src, dst.at[d], send.at[d], recv.at[d], dev)
            c.start()
            out.append(c)
        self.all += out
        return out

    def start_x(self):
        pc = self.pc
        devs = [pc.at_x((pc.x + d) % pc.X) for d in range(1, pc.X)]
        self.c = self._send(self.t0, self.lx, self.xs, self.xr, devs)

    def _sum(self, own, got, n):
        for c in self.c:
            c.wait_recv()
        total = own[...]
        for d in range(n):
            total = total + got[d]
        return total

    def start_z(self):
        pc = self.pc
        self.tx[...] = self._sum(self.t0, self.lx, pc.X - 1)
        devs = [pc.at_z((pc.z + d) % pc.Z) for d in range(1, pc.Z)]
        self.c = self._send(self.tx, self.lz, self.zs, self.zr, devs)

    def start_s(self):
        pc = self.pc
        self.tz[...] = self._sum(self.tx, self.lz, pc.Z - 1)
        self.c = self._send(self.tz, self.ls, self.ss, self.sr, seq_peers(pc))

    def total(self):
        return self._sum(self.tz, self.ls, self.pc.S - 1)

    def wait_sends(self):
        for c in self.all:
            c.wait_send()


def loss_scratch(X, Z, S):
    nz = max(Z - 1, 1)
    tile = lambda *n: pltpu.VMEM((*n, 8, 128), f32)
    return [
        tile(), tile(X - 1), tile(), tile(nz), tile(), tile(S - 1),
        dma(X - 1), dma(X - 1), dma(nz), dma(nz), dma(S - 1), dma(S - 1),
    ]


N_LOSS = 12


def loss_core(logits, target, live):
    m = jnp.where(target, -logits, logits)
    w = jnp.where(target, -beta_weight, live)
    e = jnp.exp(-jnp.abs(m))
    sig = jnp.where(m >= 0.0, 1.0, e) / (1.0 + e)
    return w * sig, jnp.abs(w), jnp.maximum(m, 0.0) + jnp.log1p(e)


def main_kernel(
    n_seq, n_item, ev_ref, w_ref, gain_ref, wo_ref, table_ref, lens_ref, neg_ref, owner_ref,
    msk_ref, tgt_ref, grad_ref, panel_all, total_ref, *scratch,
):
    pc = Place(n_seq, n_item)
    (ev_all, neg_all, out_all, table, w, wo, wh, wl, kvh, kvl, qs, gates, att, part, panel,
     acc, loss_acc, s_ev, s_table, s_w, s_wo) = scratch[:21]
    rest = scratch[21:]
    ev = SeqGather(pc, ev_all, rest[:4], causal=True)
    out = SeqGather(pc, out_all, rest[4:8])
    rest = rest[8:]
    neg = Reduce(pc, part, neg_all, rest[:N_REDUCE])
    pan = Reduce(pc, panel, panel_all, rest[N_REDUCE:2 * N_REDUCE])
    rest = rest[2 * N_REDUCE:]
    spread = SpreadXY(pc, neg_all, rest[:6])
    along_x, along_y = (pc.x, pc.at_x), (pc.y, pc.at_y)
    lane_a = Lane(pc, along_x, along_y, lambda k, j: panel_all.at[0, j, pc.c, k], rest[6:18])
    lane_b = Lane(pc, along_y, along_x, lambda k, j: panel_all.at[1, k, pc.c, j], rest[18:30])
    loss = LossSum(pc, rest[30:])

    tok, D = grad_ref.shape[1], grad_ref.shape[2]
    half = D // 2
    step = 2 * tok
    rows = table.shape[0]
    X, Z, R = part.shape[0], part.shape[1], part.shape[2]
    share = X * Z * R
    hd = D // H
    hpg = 128 // hd

    ready = enter(plane_peers(pc) + seq_peers(pc))
    c_ev = pltpu.make_async_copy(ev_ref.at[0], ev_all.at[pc.s], s_ev)
    c_table = pltpu.make_async_copy(table_ref, table, s_table)
    c_w = pltpu.make_async_copy(w_ref, w, s_w)
    c_wo = pltpu.make_async_copy(wo_ref, wo, s_wo)
    for c in (c_ev, c_table, c_w, c_wo):
        c.start()

    per_panel = neg_ref.shape[1] // share
    p = pc.s // per_panel
    first = pl.multiple_of((pc.s % per_panel) * share, share)
    slot = lax.broadcasted_iota(jnp.int32, owner_ref.shape, 1)
    owner = jnp.sum(jnp.where(slot == p, owner_ref[...], 0), axis=1, keepdims=True)
    ids = neg_ref[pl.ds(p, 1), pl.ds(first, share)] + rows * jnp.broadcast_to(owner, (1, share))
    spot = pc.i * rows + lax.broadcasted_iota(jnp.int32, (rows, share), 0)
    pick = jnp.where(spot == jnp.broadcast_to(ids, spot.shape), 1.0, 0.0).astype(bf16)
    c_table.wait()
    hi, lo = split(table[...])
    part[...] = (mm(pick, hi, TN) + mm(pick, lo, TN)).reshape(part.shape)
    c_ev.wait()
    ready()
    ev.start()
    neg.start_x()

    c_w.wait()

    def split_w(n, _):
        wh[n], wl[n] = split(w[:, pl.ds(pl.multiple_of(n * half, half), half)])
        return 0

    lax.fori_loop(0, 8, split_w, 0)
    x_own = ev_all[pc.s]
    xo = split(x_own)

    def project(xs, n):
        r = mm3(xs, (wh[n], wl[n]))
        return r * sigmoid(r)

    for n in range(2):
        qs[n] = project(xo, 4 + n)
        gates[n] = project(xo, n)
    neg.pass_x()

    lane_head = lax.broadcasted_iota(jnp.int32, (tok, 128), 1) // hd
    sub = lax.broadcasted_iota(jnp.int32, (tok, tok), 0)
    lane = lax.broadcasted_iota(jnp.int32, (tok, tok), 1)
    row = pc.s * tok + sub
    begin = jnp.zeros((tok, tok), jnp.int32)
    end = jnp.zeros((1, 1), jnp.int32)
    for u in range(lens_ref.shape[1]):
        end = end + lens_ref[0:1, u:u + 1]
        wide = jnp.broadcast_to(end, row.shape)
        begin = jnp.where(row >= wide, wide, begin)

    def stacked(m, lanes):
        q = qs[m][:, lanes]
        parts = [jnp.where(lane_head == h, q, 0.0) for h in range(hpg)]
        return split(jnp.concatenate(parts, axis=0))

    def collect(m, lanes, o, base):
        got = base
        for h in range(hpg):
            got = got + jnp.where(lane_head == h, o[h * tok:(h + 1) * tok], 0.0)
        att[m, :, lanes] = got

    def weigh(sc, allow):
        pr = (sc * sigmoid(sc)).reshape(hpg, tok, sc.shape[1]) * allow[None]
        return split(pr.reshape(sc.shape))

    def keys_values(xs, n_rows):
        def kv_step(n, _):
            hi, lo = split(project(xs, jnp.where(n < 2, 2 + n, 4 + n)))
            kvh[n, :n_rows], kvl[n, :n_rows] = hi, lo
            return 0

        lax.fori_loop(0, 4, kv_step, 0)

    def attend_own():
        keys_values(xo, tok)
        ev.forward()
        allow = jnp.where((lane <= sub) & (pc.s * tok + lane >= begin), 1.0, 0.0)

        def heads(m, _):
            for g in range(half // 128):
                lanes = slice(g * 128, (g + 1) * 128)
                kh, kl = kvh[2 + m, :tok, lanes], kvl[2 + m, :tok, lanes]
                vh, vl = kvh[m, :tok, lanes], kvl[m, :tok, lanes]
                both = jnp.concatenate(stacked(m, lanes), axis=1)
                kk = jnp.concatenate([kh, kh], axis=1)
                k0 = jnp.concatenate([kl, jnp.zeros_like(kl)], axis=1)
                sc = mm(both, jnp.concatenate([kk, k0], axis=0), NT)
                pp = jnp.concatenate(weigh(sc[:, :tok] + sc[:, tok:], allow), axis=1)
                vv = jnp.concatenate([vh, vl], axis=1)
                o = mm(pp, jnp.concatenate([vv, vv], axis=0))
                collect(m, lanes, o[:, :128] + o[:, 128:], jnp.zeros((tok, 128), f32))
            return 0

        lax.fori_loop(0, 2, heads, 0)

    def attend(back, between):
        blocks = [(pc.s + pc.S - back - d) % pc.S for d in (0, 1)]
        keys_values(split(jnp.concatenate([ev_all[b] for b in blocks], axis=0)), step)
        between()
        cols = [b * tok + lane for b in blocks]
        allow = [jnp.where((c >= begin) & (c <= row), 1.0, 0.0) for c in cols]
        allow = jnp.concatenate(allow, axis=1)

        def heads(m, _):
            for g in range(half // 128):
                lanes = slice(g * 128, (g + 1) * 128)
                kh, kl = kvh[2 + m][:, lanes], kvl[2 + m][:, lanes]
                vh, vl = kvh[m][:, lanes], kvl[m][:, lanes]
                qh, ql = stacked(m, lanes)
                two = jnp.concatenate([qh, ql], axis=1)
                sc = mm(two, jnp.concatenate([kh, kh], axis=1), NT) + mm(qh, kl, NT)
                ph, plo = weigh(sc, allow)
                o = mm(ph, jnp.concatenate([vh, vl], axis=1))
                o = (o[:, :128] + o[:, 128:]) + mm(plo, vh)
                collect(m, lanes, o, att[m, :, lanes])
            return 0

        lax.fori_loop(0, 2, heads, 0)

    attend_own()
    neg.start_z()
    ev.near()
    ev.pair(0)
    ev.pair(1)
    attend(1, neg.start_gather)
    ev.far()
    ev.pair(2)
    attend(3, lambda: None)
    neg.wait_z()
    spread.rx.start()

    a = jnp.concatenate([att[0], att[1]], axis=1)
    centered = a - jnp.mean(a, axis=1, keepdims=True)
    var = jnp.mean(centered * centered, axis=1, keepdims=True)
    normed = centered * lax.rsqrt(var + epsilon) * gain_ref[...]
    gated = normed * jnp.concatenate([gates[0], gates[1]], axis=1)
    c_wo.wait()
    o_own = x_own + mm3(split(gated), split(wo[...]))
    pad = out_all.shape[1] - tok
    out_all[pc.s, :tok, :] = o_own
    out_all[pc.s, tok:, :] = jnp.zeros((pad, D), f32)
    out_all[pc.s, tok:tok + 1, :tok] = tgt_ref[...].astype(f32)
    out_all[pc.s, tok:tok + 1, tok:step] = jnp.broadcast_to(msk_ref[...], (1, tok)).astype(f32)
    out.start()
    spread.rx.forward()
    out.forward()
    spread.x_wait()
    spread.push(pc.y)

    m0 = split(neg_all[0, pc.y, pc.c].reshape(share, half))
    m1 = split(neg_all[1, pc.y, pc.c].reshape(share, half))
    column = pc.s * share + lax.broadcasted_iota(jnp.int32, (share, step), 0)
    panel[...] = jnp.zeros_like(panel)
    loss_acc[...] = jnp.zeros_like(loss_acc)

    def own_columns(y):
        pair = [out_all[2 * y], out_all[2 * y + 1]]
        ob = jnp.concatenate([q[:tok] for q in pair], axis=0)
        tg = jnp.concatenate([q[tok:tok + 1, :tok] for q in pair], axis=1).astype(jnp.int32)
        mk = jnp.concatenate([q[tok:tok + 1, tok:step] for q in pair], axis=1).astype(jnp.int32)
        obh, obl = split(ob)
        logits = mm3(m0, (obh[:, :half], obl[:, :half]), NT)
        logits = logits + mm3(m1, (obh[:, half:], obl[:, half:]), NT)
        bits = jnp.right_shift(jnp.broadcast_to(mk, column.shape), column // 128) & 1
        g, wt, sp = loss_core(logits, column == jnp.broadcast_to(tg, column.shape), bits.astype(f32))
        loss_acc[...] += wt * sp
        panel[...] += mm3(split(g), (obh, obl)).reshape(panel.shape)

    out.pair(0)
    own_columns(pc.y)
    out.near()
    out.pair(1)
    own_columns(out.ring.left)
    out.far()
    spread.y_start()
    out.pair(2)
    own_columns(out.ring.right)
    out.pair(3)
    own_columns(out.ring.opp)
    pan.start_x()
    loss.t0[...] = jnp.broadcast_to(jnp.sum(loss_acc[...]), loss.t0.shape)
    loss.start_x()

    mine = out_all[pc.s]
    oh = [split(mine[:tok, k * half:(k + 1) * half]) for k in (0, 1)]
    tcol = jnp.transpose(jnp.broadcast_to(mine[tok:tok + 1, :tok], (tok, tok)))
    tcol = jnp.concatenate([tcol, tcol], axis=1).astype(jnp.int32)
    mcol = jnp.broadcast_to(mine[tok:tok + 1, tok:tok + 1], (tok, step)).astype(jnp.int32)
    acc[...] = jnp.zeros_like(acc)

    lane2 = lax.broadcasted_iota(jnp.int32, (tok, step), 1)

    def own_tokens(j):
        n0 = split(neg_all[0, j // 2, j % 2].reshape(share, half))
        n1 = split(neg_all[1, j // 2, j % 2].reshape(share, half))
        logits = mm3(oh[0], n0, NT) + mm3(oh[1], n1, NT)
        live = (jnp.right_shift(mcol, 2 * j + lane2 // 128) & 1).astype(f32)
        g, _, _ = loss_core(logits, lane2 + j * share == tcol, live)
        gs = split(g)
        acc[0] += mm3(gs, n0)
        acc[1] += mm3(gs, n1)

    def own_pair(n, y):
        def one(c, _):
            own_tokens(2 * y + c)
            return 0

        spread.core.wait_recv(n)
        lax.fori_loop(0, 2, one, 0)

    own_pair(0, pc.y)
    pan.pass_x()
    spread.ry.forward()
    pan.start_z()
    loss.start_z()
    pan.start_gather()
    loss.start_s()
    spread.near()
    own_pair(1, spread.ry.left)
    own_pair(2, spread.ry.right)
    pan.wait_z()
    steps = list(zip(lane_a.steps(), lane_b.steps()))
    for n, pair in enumerate(steps):
        for step_of in pair:
            step_of()
        if n == 0:
            spread.far()
            own_pair(3, spread.ry.opp)
            grad_ref[0, :, :half] = acc[0]
            grad_ref[0, :, half:] = acc[1]
    total_ref[...] = loss.total()
    lane_a.wait_core()
    lane_b.wait_core()
    for q in (ev, out, neg, pan, spread, lane_a, lane_b, loss):
        q.wait_sends()


def scatter_kernel(n_item, scale, panel_all, neg_ref, owner_ref, total_ref, table_ref, loss_ref, buf, sem):
    item = lax.axis_index("item")
    rows = table_ref.shape[0]
    panel = neg_ref.shape[1]
    half = buf.shape[3]
    def fetch(p):
        return pltpu.make_async_copy(
            panel_all.at[:, pl.ds(p * panel, panel), :], buf.at[p], sem.at[p]
        )

    for p in range(neg_ref.shape[0]):
        pl.when(owner_ref[p] == item)(fetch(p).start)
    table_ref[...] = jnp.zeros_like(table_ref)
    loss_ref[0, 0] = jnp.max(total_ref[...]) * scale
    for p in range(neg_ref.shape[0]):

        @pl.when(owner_ref[p] == item)
        def _():
            spot = lax.broadcasted_iota(jnp.int32, (rows, panel), 0)
            pick = jnp.where(spot == neg_ref[pl.ds(p, 1), :], 1.0, 0.0).astype(bf16)
            fetch(p).wait()
            for k in (0, 1):
                hi, lo = split(buf[p, k])
                table_ref[:, k * half:(k + 1) * half] += mm(pick, hi) + mm(pick, lo)


def params(cid=None):
    if cid is None:
        return pltpu.CompilerParams(vmem_limit_bytes=VMEM_LIMIT)
    return pltpu.CompilerParams(
        vmem_limit_bytes=VMEM_LIMIT, collective_id=cid, has_side_effects=True
    )


def per_device(
    n_seq, n_item, events, w_uvqk, out_gain, w_out, item_table,
    user_lengths, neg_ids, panel_owner, block_mask, targets,
):
    _, tok, D = events.shape
    X, Z, Y = X_RING, n_item // X_RING, n_seq // 2
    n_neg = neg_ids.shape[0] * neg_ids.shape[1]
    share = n_neg // n_seq
    R = share // n_item
    half = D // 2
    shape = jax.ShapeDtypeStruct

    aug = tok + 16
    step = 2 * tok
    full = (2, Y, 2, X, Z * R, half)
    one = pltpu.SemaphoreType.DMA
    event_grad, panel_all, total = pl.pallas_call(
        functools.partial(main_kernel, n_seq, n_item),
        out_shape=(shape(events.shape, f32), shape(full, f32), shape((8, 128), f32)),
        in_specs=[ANY, ANY, VM, ANY, ANY, VM, VM, VM, VM, VM], out_specs=(VM, ANY, VM),
        scratch_shapes=[
            pltpu.VMEM((n_seq, tok, D), f32), pltpu.VMEM(full, f32),
            pltpu.VMEM((n_seq, aug, D), f32), pltpu.VMEM(item_table.shape, f32),
            pltpu.VMEM(w_uvqk.shape, f32), pltpu.VMEM(w_out.shape, f32),
            pltpu.VMEM((8, D, half), bf16), pltpu.VMEM((8, D, half), bf16),
            pltpu.VMEM((4, step, half), bf16), pltpu.VMEM((4, step, half), bf16),
            pltpu.VMEM((2, tok, half), f32), pltpu.VMEM((2, tok, half), f32),
            pltpu.VMEM((2, tok, half), f32),
            pltpu.VMEM((X, Z, R, D), f32), pltpu.VMEM((X, Z, R, D), f32),
            pltpu.VMEM((2, tok, half), f32), pltpu.VMEM((share, step), f32),
            one, one, one, one,
        ] + SEQ_SEMS * 2 + reduce_scratch(X, Z, R, D) * 2 + SPREAD_XY_SEMS + LANE_SEMS * 2 + loss_scratch(X, Z, n_seq),
        compiler_params=params(1), name="main",
    )(events, w_uvqk, out_gain.reshape(1, D), w_out, item_table, user_lengths, neg_ids,
      panel_owner.reshape(1, -1), block_mask, targets)

    scale = 1.0 / (tok * n_seq * n_item)
    table_grad, mean_loss = pl.pallas_call(
        functools.partial(scatter_kernel, n_item, scale),
        out_shape=(shape(item_table.shape, f32), shape((1, 1), f32)),
        in_specs=[ANY, VM, SM, VM], out_specs=(VM, SM),
        scratch_shapes=[pltpu.VMEM((neg_ids.shape[0], 2, neg_ids.shape[1], half), f32), dma(neg_ids.shape[0])],
        compiler_params=params(), name="scatter",
    )(panel_all.reshape(2, n_neg, half), neg_ids, panel_owner, total)
    return (mean_loss.reshape(()), event_grad, table_grad)


def solution(mesh):
    placed = (
        P("item", "seq", None), P(), P(), P(), P("item", None), P("item", None),
        P(), P(), P("item", "seq"), P("item", "seq"),
    )
    body = functools.partial(per_device, mesh.shape["seq"], mesh.shape["item"])
    return jax.shard_map(
        body, mesh=mesh, in_specs=placed,
        out_specs=(P(), P("item", "seq", None), P("item", None)), check_vma=False,
    )
```
